128 devices in a mesh: dev: 128 (over y, z, x, core).
Axes of the slice: x: 4, y: 4, z: 4, core: 2. Of those that a mesh axis runs over, the one named last changes fastest.
Arguments:
- gaussians: float32 [59, 1048576], P(None, 'dev'), may hold values from -6 to 3
- view_angles: float32 [3], replicated, may hold values from -4 to 4
- tile_order: int32 [2048], P('dev'), may hold values from 0 to 2047, as said below
- tile_owners: int32 [2048, 512], P('dev'), may hold values from 0 to 127, as said below
- tile_locals: int32 [2048, 512], P('dev'), may hold values from 0 to 8191
- list_counts: int32 [2048], P('dev'), may hold values from 1 to 512, as said below
- image_cotangent: float32 [3, 524288], P(None, 'dev'), may hold values from -6 to 6
Outputs:
- rendered: float32 [3, 524288], P(None, 'dev')
- gradients: float32 [59, 1048576], P(None, 'dev')
The draws below stay inside these ranges and needn't reach their ends.
Inputs may be any that keep to these rules, and one draw needn't show every extreme that they name: `tile_order`: each image tile once. `tile_owners`: the 16 x 512 slots of the tiles of one device name every owner exactly 64 times. Slots from list_counts[i] on are padding.
All inputs are finite; a program needn't handle non-finite values.
Results may differ from the reference program's by a relative error of at most 0.0003.
Values sent between devices are 32-bit elements; how exact they have to be, the bound alone decides.
A program may use at most 64 MiB of HBM per device.

```python
import jax
import jax.numpy as jnp
from jax import lax

PROJ = 9
PIX = 256
TX = 32
SLOTS = 512
G_DEV = 8192
TILE_DEV = 16
GAUSS = 1048576
TILES = 2048


def layout(key):
    keys = [jax.random.fold_in(key, 101 + index) for index in range(8)]
    angles = jax.random.uniform(keys[0], (3,), jnp.float32, -3.14159, 3.14159)
    cos_a = jnp.cos(angles[0])
    sin_a = jnp.sin(angles[0])
    cos_b = jnp.cos(angles[1])
    sin_b = jnp.sin(angles[1])
    cos_c = jnp.cos(angles[2])
    sin_c = jnp.sin(angles[2])
    row_zero = [cos_c * cos_b, cos_c * sin_b * sin_a - sin_c * cos_a, cos_c * sin_b * cos_a + sin_c * sin_a]
    row_one = [sin_c * cos_b, sin_c * sin_b * sin_a + cos_c * cos_a, sin_c * sin_b * cos_a - cos_c * sin_a]
    row_two = [-sin_b, cos_b * sin_a, cos_b * cos_a]
    order = jax.random.permutation(keys[1], jnp.arange(TILES, dtype=jnp.int32)).astype(jnp.int32)
    devices = TILES // TILE_DEV
    per_device = TILE_DEV * SLOTS
    base = jnp.arange(per_device, dtype=jnp.int32) % devices
    owner_keys = jax.random.split(keys[2], devices)
    owners = jax.vmap(lambda one_key: jax.random.permutation(one_key, base))(owner_keys).reshape(TILES, SLOTS).astype(jnp.int32)
    target = order[:, None]
    moved = jax.random.randint(keys[3], (TILES, SLOTS), -2, 3, dtype=jnp.int32)
    column = jnp.clip(target % TX + moved, 0, TX - 1)
    near = target // TX * TX + column
    anchor_rank = (near - owners * TILE_DEV) % TILES
    spread = max(G_DEV // TILES, 1)
    locals_drawn = anchor_rank * G_DEV // TILES + jax.random.randint(keys[4], (TILES, SLOTS), 0, spread, dtype=jnp.int32)
    locals_drawn = locals_drawn.at[0, 0].set(G_DEV - 1).at[0, 1].set(0).astype(jnp.int32)
    levels = jax.random.randint(keys[5], (GAUSS,), 0, 4096, dtype=jnp.int32)
    slot_levels = jnp.take(levels, owners * G_DEV + locals_drawn)
    ranks = jnp.argsort(slot_levels, axis=1, stable=True)
    owners = jnp.take_along_axis(owners, ranks, axis=1).astype(jnp.int32)
    locals_drawn = jnp.take_along_axis(locals_drawn, ranks, axis=1).astype(jnp.int32)
    index = jnp.arange(GAUSS, dtype=jnp.int32)
    anchor = (index % G_DEV * TILES // G_DEV + index // G_DEV * TILE_DEV) % TILES
    tiles_y = TILES // TX
    jitter = jax.random.uniform(keys[6], (2, GAUSS), jnp.float32, -16.0, 16.0)
    screen_x = jnp.clip(16.0 * (anchor % TX).astype(jnp.float32) + 8.0 + jitter[0], 0.0, 16.0 * TX)
    screen_y = jnp.clip(16.0 * (anchor // TX).astype(jnp.float32) + 8.0 + jitter[1], 0.0, 16.0 * tiles_y)
    view_x = (screen_x - 8.0 * TX) / (4.0 * TX)
    view_y = (screen_y - 8.0 * tiles_y) / (4.0 * tiles_y)
    depth = (levels.astype(jnp.float32) + 0.5) / 2048.0 - 1.0
    positions = jnp.stack([row_zero[j] * view_x + row_one[j] * view_y + row_two[j] * depth for j in range(3)])
    return (angles, order, owners, locals_drawn, positions)


def draw_view_angles(key, part):
    return layout(key)[0].astype(jnp.float32)


def draw_tile_order(key, part):
    return layout(key)[1]


def draw_tile_owners(key, part):
    return layout(key)[2]


def draw_tile_locals(key, part):
    return layout(key)[3]


def draw_gaussians(key, part):
    positions = layout(key)[4]
    keys = jax.random.split(jax.random.fold_in(key, 7), 5)
    harmonic_scale = jnp.where(jnp.arange(16) == 0, 0.5, 0.15).astype(jnp.float32)[None, :, None]
    log_scales = jax.random.uniform(keys[1], (3, GAUSS), jnp.float32, -2.3, -0.5)
    quats = jax.random.normal(keys[2], (4, GAUSS), jnp.float32) * 0.6
    opacity_logits = jax.random.uniform(keys[3], (1, GAUSS), jnp.float32, -5.5, -4.0)
    harmonic = jax.random.normal(keys[4], (3, 16, GAUSS), jnp.float32) * harmonic_scale
    stacked = jnp.concatenate([positions, log_scales, quats, opacity_logits, harmonic.reshape(48, GAUSS)], axis=0)
    return jnp.clip(stacked, -6.0, 3.0).astype(jnp.float32)


def draw_list_counts(key, part):
    keys = jax.random.split(jax.random.fold_in(key, 23), 2)
    counts = jax.random.randint(keys[0], (TILES,), SLOTS * 3 // 8, SLOTS + 1, dtype=jnp.int32)
    chosen = jax.random.randint(keys[1], (), 0, TILES, dtype=jnp.int32)
    return counts.at[chosen].set(SLOTS).at[(chosen + 1) % TILES].set(1).astype(jnp.int32)


def steps_of(key, extent, cuts, low, high):
    def one(position, shards_of):
        draws = jax.random.uniform(jax.random.fold_in(jax.random.fold_in(key, 6), position), (shards_of,), jnp.float32, low / len(cuts), high / len(cuts))
        return jnp.repeat(jnp.exp(draws), extent[position] // shards_of).reshape((-1,) + (1,) * (len(extent) - position - 1))

    gain = one(*cuts[0])
    for cut in cuts[1:]:
        gain = gain * one(*cut)
    return gain


def scatter_about(key, extent, scale, most, cuts=(), kind=jnp.bfloat16):
    gain = steps_of(key, extent, cuts, -0.22, 0.18) if cuts else 1.0
    values = jax.random.normal(key, extent, jnp.float32) * scale * gain
    return jnp.minimum(jnp.maximum(values, -most), most).astype(kind)


def setup_inputs(seed: int = 0) -> dict:
    key_of = jax.random.split(jax.random.key(seed), 8)
    return {
        "gaussians": draw_gaussians(jax.random.fold_in(key_of[7], 71), 0),
        "view_angles": draw_view_angles(jax.random.fold_in(key_of[7], 71), 0),
        "tile_order": draw_tile_order(jax.random.fold_in(key_of[7], 71), 0),
        "tile_owners": draw_tile_owners(jax.random.fold_in(key_of[7], 71), 0),
        "tile_locals": draw_tile_locals(jax.random.fold_in(key_of[7], 71), 0),
        "list_counts": draw_list_counts(jax.random.fold_in(key_of[7], 71), 0),
        "image_cotangent": scatter_about(key_of[6], (3, TILES * PIX), 1.0, 6.0, ((1, 128),), jnp.float32),
    }


highest = lax.Precision.HIGHEST

def rotation_of(view_angles):
    cos_a = jnp.cos(view_angles[0])
    sin_a = jnp.sin(view_angles[0])
    cos_b = jnp.cos(view_angles[1])
    sin_b = jnp.sin(view_angles[1])
    cos_c = jnp.cos(view_angles[2])
    sin_c = jnp.sin(view_angles[2])
    zero_val = jnp.zeros((), jnp.float32)
    one_val = jnp.ones((), jnp.float32)
    turn_x = jnp.stack([jnp.stack([one_val, zero_val, zero_val]), jnp.stack([zero_val, cos_a, -sin_a]), jnp.stack([zero_val, sin_a, cos_a])])
    turn_y = jnp.stack([jnp.stack([cos_b, zero_val, sin_b]), jnp.stack([zero_val, one_val, zero_val]), jnp.stack([-sin_b, zero_val, cos_b])])
    turn_z = jnp.stack([jnp.stack([cos_c, -sin_c, zero_val]), jnp.stack([sin_c, cos_c, zero_val]), jnp.stack([zero_val, zero_val, one_val])])
    return jnp.dot(turn_z, jnp.dot(turn_y, turn_x, precision=highest), precision=highest)

def harmonics(along_x, along_y, along_z):
    sq_x = along_x * along_x
    sq_y = along_y * along_y
    sq_z = along_z * along_z
    return jnp.stack([0.28209479177387814 + 0.0 * along_x, -0.4886025119029199 * along_y, 0.4886025119029199 * along_z, -0.4886025119029199 * along_x, 1.0925484305920792 * along_x * along_y, -1.0925484305920792 * along_y * along_z, 0.31539156525252005 * (2.0 * sq_z - sq_x - sq_y), -1.0925484305920792 * along_x * along_z, 0.5462742152960396 * (sq_x - sq_y), -0.5900435899266435 * along_y * (3.0 * sq_x - sq_y), 2.890611442640554 * along_x * along_y * along_z, -0.4570457994644658 * along_y * (4.0 * sq_z - sq_x - sq_y), 0.3731763325901154 * along_z * (2.0 * sq_z - 3.0 * sq_x - 3.0 * sq_y), -0.4570457994644658 * along_x * (4.0 * sq_z - sq_x - sq_y), 1.445305721320277 * along_z * (sq_x - sq_y), -0.5900435899266435 * along_x * (sq_x - 3.0 * sq_y)])

def project(columns, view_angles, camera_frame):
    focal_x, focal_y, centre_x, centre_y = camera_frame
    rotation = rotation_of(view_angles)
    positions = columns[0:3]
    cam_first = rotation[0, 0] * positions[0] + rotation[0, 1] * positions[1] + rotation[0, 2] * positions[2]
    cam_second = rotation[1, 0] * positions[0] + rotation[1, 1] * positions[1] + rotation[1, 2] * positions[2]
    mean_x = centre_x + focal_x * cam_first
    mean_y = centre_y + focal_y * cam_second
    scales = jnp.exp(columns[3:6])
    quat_w = columns[6]
    quat_x = columns[7]
    quat_y = columns[8]
    quat_z = columns[9]
    norm_sq = jnp.maximum(quat_w * quat_w + quat_x * quat_x + quat_y * quat_y + quat_z * quat_z, 1.0)
    turned = [[1.0 - 2.0 * (quat_y * quat_y + quat_z * quat_z) / norm_sq, 2.0 * (quat_x * quat_y - quat_w * quat_z) / norm_sq, 2.0 * (quat_x * quat_z + quat_w * quat_y) / norm_sq], [2.0 * (quat_x * quat_y + quat_w * quat_z) / norm_sq, 1.0 - 2.0 * (quat_x * quat_x + quat_z * quat_z) / norm_sq, 2.0 * (quat_y * quat_z - quat_w * quat_x) / norm_sq], [2.0 * (quat_x * quat_z - quat_w * quat_y) / norm_sq, 2.0 * (quat_y * quat_z + quat_w * quat_x) / norm_sq, 1.0 - 2.0 * (quat_x * quat_x + quat_y * quat_y) / norm_sq]]
    first_row = []
    second_row = []
    for column_index in range(3):
        first_row.append(focal_x * (rotation[0, 0] * turned[0][column_index] + rotation[0, 1] * turned[1][column_index] + rotation[0, 2] * turned[2][column_index]) * scales[column_index])
        second_row.append(focal_y * (rotation[1, 0] * turned[0][column_index] + rotation[1, 1] * turned[1][column_index] + rotation[1, 2] * turned[2][column_index]) * scales[column_index])
    cov_a = first_row[0] * first_row[0] + first_row[1] * first_row[1] + first_row[2] * first_row[2] + 0.3
    cov_b = first_row[0] * second_row[0] + first_row[1] * second_row[1] + first_row[2] * second_row[2]
    cov_c = second_row[0] * second_row[0] + second_row[1] * second_row[1] + second_row[2] * second_row[2] + 0.3
    determinant = cov_a * cov_c - cov_b * cov_b
    opacity = 1.0 / (1.0 + jnp.exp(-columns[10]))
    basis = harmonics(rotation[2, 0], rotation[2, 1], rotation[2, 2])
    coeffs = columns[11:59].reshape(3, 16, columns.shape[1])
    colours = 0.5 + jnp.einsum('k,ckn->cn', basis, coeffs, precision=highest)
    return jnp.stack([mean_x, mean_y, cov_c / determinant, -cov_b / determinant, cov_a / determinant, opacity, colours[0], colours[1], colours[2]])

def render_tile(tile_rows, live_count, tile_id):
    pixels = jnp.arange(PIX, dtype=jnp.int32)
    pixel_x = (tile_id % TX * 16 + pixels % 16).astype(jnp.float32) + 0.5
    pixel_y = (tile_id // TX * 16 + pixels // 16).astype(jnp.float32) + 0.5
    offset_x = pixel_x[:, None] - tile_rows[0][None, :]
    offset_y = pixel_y[:, None] - tile_rows[1][None, :]
    powers = -0.5 * (tile_rows[2][None, :] * offset_x * offset_x + tile_rows[4][None, :] * offset_y * offset_y) - tile_rows[3][None, :] * offset_x * offset_y
    slot_live = jnp.arange(SLOTS, dtype=jnp.int32) < live_count
    alphas = jnp.where(slot_live[None, :], tile_rows[5][None, :] * jnp.exp(powers), 0.0)
    logs = jnp.log1p(-alphas)
    trans = jnp.exp(jnp.cumsum(logs, axis=1) - logs)
    return jnp.einsum('ck,pk->cp', tile_rows[6:9], trans * alphas, precision=highest)

def reference(gaussians, view_angles, tile_order, tile_owners, tile_locals, list_counts, image_cotangent):
    tiles_y = TILES // TX
    camera_frame = (4.0 * TX, 4.0 * tiles_y, 8.0 * TX, 8.0 * tiles_y)
    indices = (tile_owners * G_DEV + tile_locals).reshape(-1).astype(jnp.int32)

    def shaded(table):
        return project(jnp.take(table, indices, axis=1), view_angles, camera_frame)
    projected, pullback = jax.vjp(shaded, gaussians)
    tile_rows = projected.reshape(PROJ, TILES, SLOTS).transpose(1, 0, 2)
    cotangents = image_cotangent.reshape(3, TILES, PIX).transpose(1, 0, 2)

    def one_tile(tile_item):
        columns, live_count, tile_id, tile_cot = tile_item
        tile_image, tile_back = jax.vjp(lambda values: render_tile(values, live_count, tile_id), columns)
        return (tile_image, tile_back(tile_cot)[0])
    images, slot_grads = lax.map(one_tile, (tile_rows, list_counts, tile_order, cotangents))
    rendered = images.transpose(1, 0, 2).reshape(3, TILES * PIX)
    gradients = pullback(slot_grads.transpose(1, 0, 2).reshape(PROJ, TILES * SLOTS))[0]
    return (rendered, gradients)
```

```python
from functools import partial

import jax
import jax.numpy as jnp
from jax import lax
from jax.experimental import pallas as pl
from jax.experimental.pallas import tpu as pltpu
from jax.sharding import PartitionSpec as P

DEVS = 128
CHIPS = 64
TILES = 16
SLOTS = 512
ROWS = 64
LANES = 128
PROJ = 9
PIX = 256
TX = 32
FOCAL_X = 128.0
FOCAL_Y = 256.0
CENTRE_X = 256.0
CENTRE_Y = 512.0
LOG2E = 1.4426950408889634
MESH = pl.DeviceIdType.MESH
f32 = jnp.float32
bf16 = jnp.bfloat16
i32 = jnp.int32


def iota(shape, dim):
    return lax.broadcasted_iota(i32, shape, dim)


def split2(x):
    hi = x.astype(bf16)
    return hi, (x - hi.astype(f32)).astype(bf16)


def split3(x):
    hi = x.astype(bf16)
    rest = x - hi.astype(f32)
    mid = rest.astype(bf16)
    return hi, mid, (rest - mid.astype(f32)).astype(bf16)


def lane_pick(table, index):
    return jnp.take_along_axis(table, index, axis=1)


def view_of(angle_ref):
    def turn(i):
        angle = jnp.full((8, LANES), angle_ref[i], f32)
        return jnp.cos(angle)[0:1], jnp.sin(angle)[0:1]

    (ca, sa), (cb, sb), (cc, sc) = turn(0), turn(1), turn(2)
    first = (cc * cb, cc * sb * sa - sc * ca, cc * sb * ca + sc * sa)
    second = (sc * cb, sc * sb * sa + cc * ca, sc * sb * ca - cc * sa)
    third = (-sb, cb * sa, cb * ca)
    return first, second, third


def harmonics(x, y, z):
    xx, yy, zz = x * x, y * y, z * z
    return [
        0.28209479177387814 + 0.0 * x,
        -0.4886025119029199 * y,
        0.4886025119029199 * z,
        -0.4886025119029199 * x,
        1.0925484305920792 * x * y,
        -1.0925484305920792 * y * z,
        0.31539156525252005 * (2.0 * zz - xx - yy),
        -1.0925484305920792 * x * z,
        0.5462742152960396 * (xx - yy),
        -0.5900435899266435 * y * (3.0 * xx - yy),
        2.890611442640554 * x * y * z,
        -0.4570457994644658 * y * (4.0 * zz - xx - yy),
        0.3731763325901154 * z * (2.0 * zz - 3.0 * xx - 3.0 * yy),
        -0.4570457994644658 * x * (4.0 * zz - xx - yy),
        1.445305721320277 * z * (xx - yy),
        -0.5900435899266435 * x * (xx - 3.0 * yy),
    ]


COLOUR_ROWS = ((8, 32), (24, 48), (40, 59))


def colour_weights(basis):
    out = []
    for c, (low, high) in enumerate(COLOUR_ROWS):
        row = iota((high - low, LANES), 0) + low - (11 + 16 * c)
        held = jnp.zeros((high - low, LANES), f32)
        for k in range(16):
            held = jnp.where(row == k, basis[k], held)
        out.append(held)
    return out


def project(params, first, second):
    px, py, pz, s0, s1, s2, qw, qx, qy, qz, logit = params
    mean_x = CENTRE_X + FOCAL_X * (first[0] * px + first[1] * py + first[2] * pz)
    mean_y = CENTRE_Y + FOCAL_Y * (second[0] * px + second[1] * py + second[2] * pz)
    scales = (jnp.exp(s0), jnp.exp(s1), jnp.exp(s2))
    two_n = 2.0 / jnp.maximum(qw * qw + qx * qx + qy * qy + qz * qz, 1.0)
    turned = (
        (1.0 - two_n * (qy * qy + qz * qz), two_n * (qx * qy - qw * qz), two_n * (qx * qz + qw * qy)),
        (two_n * (qx * qy + qw * qz), 1.0 - two_n * (qx * qx + qz * qz), two_n * (qy * qz - qw * qx)),
        (two_n * (qx * qz - qw * qy), two_n * (qy * qz + qw * qx), 1.0 - two_n * (qx * qx + qy * qy)),
    )
    va = []
    vb = []
    for j in range(3):
        va.append(FOCAL_X * (first[0] * turned[0][j] + first[1] * turned[1][j] + first[2] * turned[2][j]) * scales[j])
        vb.append(FOCAL_Y * (second[0] * turned[0][j] + second[1] * turned[1][j] + second[2] * turned[2][j]) * scales[j])
    cov_a = va[0] * va[0] + va[1] * va[1] + va[2] * va[2] + 0.3
    cov_b = va[0] * vb[0] + va[1] * vb[1] + va[2] * vb[2]
    cov_c = vb[0] * vb[0] + vb[1] * vb[1] + vb[2] * vb[2] + 0.3
    inv = 1.0 / (cov_a * cov_c - cov_b * cov_b)
    log_opacity = -jnp.log(1.0 + jnp.exp(-logit))
    return mean_x, mean_y, cov_c * inv, -cov_b * inv, cov_a * inv, log_opacity


def regroup(table_ref, rows_of, index, store):
    part_rows = 32
    for part in range(ROWS // part_rows):
        flat = index[part * part_rows : (part + 1) * part_rows]
        high = lax.shift_right_logical(flat, 7)
        low = jnp.bitwise_and(flat, 127)

        def step(i, held):
            here = high == i
            out = []
            for r in range(PROJ):
                row = jnp.broadcast_to(table_ref[r, pl.ds(i, 1), :], (part_rows, LANES))
                out.append(jnp.where(here, lane_pick(row, low), held[r]))
            return tuple(out)

        start = tuple(jnp.zeros((part_rows, LANES), f32) for _ in range(PROJ))
        taken = lax.fori_loop(0, ROWS, step, start, unroll=2)
        for r in range(PROJ):
            store(r, part * part_rows, taken[r])


def chain_length(count):
    return lax.shift_left(lax.shift_right_logical(count + 31, 5), 2)


def route_kernel(count_ref, owner_ref, local_ref, want_ref, pos_ref, group_ref, own_s, loc_s, carry_s, sum_s):
    tile = iota((TILES, LANES), 0)
    length = jnp.zeros((TILES, LANES), i32)
    for t in range(TILES):
        length = jnp.where(tile == t, chain_length(count_ref[t]), length)
    for d in range(SLOTS // LANES):
        row = iota((TILES, LANES), 1) + d * LANES
        slot = jnp.where(row < 8 * length, jnp.bitwise_and(row, 7) * length + lax.shift_right_logical(row, 3), row)
        high = lax.shift_right_logical(slot, 7)
        low = jnp.bitwise_and(slot, 127)
        for src, dst in ((owner_ref, own_s), (local_ref, loc_s)):
            held = jnp.zeros((TILES, LANES), i32)
            for c in range(SLOTS // LANES):
                held = jnp.where(high == c, lane_pick(src[:, c * LANES : (c + 1) * LANES], low), held)
            dst[:, d * LANES : (d + 1) * LANES] = held
    half = 256
    before = jnp.where(iota((half, half), 0) < iota((half, half), 1), 1.0, 0.0).astype(bf16)
    ones = jnp.ones((half, half), bf16)
    both = jnp.concatenate([before, ones], axis=1)
    carry_s[...] = jnp.zeros_like(carry_s)
    sum_s[...] = jnp.zeros_like(sum_s)
    owner_id = iota((DEVS, half), 0)
    pair_id = iota((ROWS, half), 0)
    lane_id = iota((LANES, half), 0)

    def step(t, _):
        for h in range(2):
            owner = own_s[pl.ds(t, 1), h * half : (h + 1) * half]
            local = loc_s[pl.ds(t, 1), h * half : (h + 1) * half]
            hit = owner_id == owner
            hit_f = jnp.where(hit, 1.0, 0.0)
            counts = jnp.dot(hit_f.astype(bf16), both, preferred_element_type=f32)
            seen = carry_s[...]
            rank = jnp.sum(hit_f * (counts[:, :half] + seen), axis=0, keepdims=True).astype(i32)
            carry_s[...] = seen + counts[:, half:]
            place = owner * ROWS + rank
            pos_ref[pl.ds(4 * t + 2 * h, 1), :] = place[:, :LANES]
            pos_ref[pl.ds(4 * t + 2 * h + 1, 1), :] = place[:, LANES:]
            pair = pair_id == lax.shift_right_logical(place, 7)
            lane = jnp.where(lane_id == jnp.bitwise_and(place, 127), 1.0, 0.0).astype(bf16)
            slot = t * SLOTS + h * half + iota((1, half), 1)
            parts = []
            for number in (local, slot):
                for part in (lax.shift_right_logical(number, 7), jnp.bitwise_and(number, 127)):
                    parts.append(jnp.where(pair, part.astype(f32), 0.0).astype(bf16))
            sum_s[...] += lax.dot_general(
                jnp.concatenate(parts, axis=0), lane, (((1,), (1,)), ((), ())), preferred_element_type=f32
            )
        return 0

    lax.fori_loop(0, TILES, step, 0)
    total = sum_s[...].astype(i32)
    want_ref[:, 0, :] = total[0:64] * 128 + total[64:128]
    group_ref[...] = total[128:192] * 128 + total[192:256]


def exchange_kernel(x_ref, y_ref, near, far, send_sem, recv_sem, pair_sem):
    me = lax.axis_index("dev")
    chip = me // 2
    core = me % 2
    other = chip * 2 + (1 - core)
    barrier = pltpu.get_barrier_semaphore()

    def greet(i, _):
        peer = ((chip + i) % CHIPS) * 2 + core
        pl.semaphore_signal(barrier, inc=1, device_id=(peer,), device_id_type=MESH)
        return 0

    lax.fori_loop(1, CHIPS, greet, 0)
    pl.semaphore_signal(barrier, inc=1, device_id=(other,), device_id_type=MESH)
    pl.semaphore_wait(barrier, CHIPS)

    def outgoing(i):
        to = (chip + i) % CHIPS
        return pltpu.make_async_remote_copy(
            src_ref=x_ref.at[to],
            dst_ref=near.at[chip],
            send_sem=send_sem.at[i],
            recv_sem=recv_sem.at[i],
            device_id=(to * 2 + core,),
            device_id_type=MESH,
        )

    def incoming(i):
        source = (chip + CHIPS - i) % CHIPS
        return pltpu.make_async_remote_copy(
            src_ref=x_ref.at[source],
            dst_ref=near.at[source],
            send_sem=send_sem.at[i],
            recv_sem=recv_sem.at[i],
            device_id=(source * 2 + core,),
            device_id_type=MESH,
        )

    def send(i, _):
        outgoing(i).start()
        return 0

    lax.fori_loop(1, CHIPS, send, 0)
    near[chip] = x_ref[chip]

    def receive(i, _):
        incoming(i).wait_recv()
        return 0

    lax.fori_loop(1, CHIPS, receive, 0)
    swap = pltpu.make_async_remote_copy(
        src_ref=near,
        dst_ref=far,
        send_sem=pair_sem.at[0],
        recv_sem=pair_sem.at[1],
        device_id=(other,),
        device_id_type=MESH,
    )
    swap.start()

    def sent(i, _):
        outgoing(i).wait_send()
        return 0

    lax.fori_loop(1, CHIPS, sent, 0)
    swap.wait()
    shape = (CHIPS, LANES)
    mine = lax.shift_right_logical(iota(shape, 1), 6) == core
    for r in range(x_ref.shape[1]):
        y_ref[:, r, :] = jnp.where(mine, near[:, r, :], pltpu.roll(far[:, r, :], 64, 1))


def exchange(x, number):
    vmem = pl.BlockSpec(memory_space=pltpu.VMEM)
    return pl.pallas_call(
        exchange_kernel,
        out_shape=jax.ShapeDtypeStruct(x.shape, x.dtype),
        in_specs=[vmem],
        out_specs=vmem,
        scratch_shapes=[
            pltpu.VMEM(x.shape, x.dtype),
            pltpu.VMEM(x.shape, x.dtype),
            pltpu.SemaphoreType.DMA((CHIPS,)),
            pltpu.SemaphoreType.DMA((CHIPS,)),
            pltpu.SemaphoreType.DMA((2,)),
        ],
        compiler_params=pltpu.CompilerParams(collective_id=number, has_side_effects=True),
        name="exchange_" + str(number),
    )(x)


def spread(gauss_ref, held, row_of):
    for i in range(ROWS):
        at = row_of(i) * 16
        held[at : at + 16, :] = gauss_ref[0:16, i * LANES : (i + 1) * LANES]
    return [held[pl.ds(r, ROWS, stride=16), :] for r in range(11)]


def answer_kernel(angle_ref, gauss_ref, asked_ref, out_ref, held, table):
    first, second, third = view_of(angle_ref)
    weights = colour_weights(harmonics(*third))
    params = spread(gauss_ref, held, lambda i: i)
    for r, value in enumerate(project(params, first, second)):
        table[r] = value
    for i in range(ROWS):
        lanes = slice(i * LANES, (i + 1) * LANES)
        for c, (low, high) in enumerate(COLOUR_ROWS):
            table[6 + c, i : i + 1, :] = 0.5 + jnp.sum(
                gauss_ref[low:high, lanes] * weights[c], axis=0, keepdims=True
            )

    def store(r, at, value):
        out_ref[at : at + value.shape[0], r, :] = value

    regroup(table, ROWS, asked_ref[:, 0, :], store)


def render_kernel(
    count_ref, order_ref, got_ref, pos_ref, group_ref, cot_ref, image_ref, grad_ref,
    table, where_s, coef, sums, alpha_s, w_s, v_s, gh_s, gl_s, wh_s, wl_s,
):
    shape = (ROWS, LANES)
    tile = lax.shift_right_logical(iota(shape, 0), 2)
    row = jnp.bitwise_and(iota(shape, 0), 3) * LANES + iota(shape, 1)
    length = jnp.zeros(shape, i32)
    count = jnp.zeros(shape, i32)
    shown = jnp.zeros(shape, i32)
    for t in range(TILES):
        here = tile == t
        length = jnp.where(here, chain_length(count_ref[t]), length)
        count = jnp.where(here, count_ref[t], count)
        shown = jnp.where(here, order_ref[t], shown)
    slot = jnp.where(row < 8 * length, jnp.bitwise_and(row, 7) * length + lax.shift_right_logical(row, 3), row)
    live = slot < count
    mid_x = (jnp.bitwise_and(shown, TX - 1) * 16 + 8).astype(f32)
    mid_y = (lax.shift_right_logical(shown, 5) * 16 + 8).astype(f32)

    for r in range(PROJ):
        table[r] = got_ref[:, r, :]

    def keep(r, at, value):
        where_s[r, at : at + value.shape[0], :] = value

    regroup(table, ROWS, pos_ref[...], keep)
    mx = where_s[0] - mid_x
    my = where_s[1] - mid_y
    ca, cb, cc = where_s[2], where_s[3], where_s[4]
    where_s[0] = mx
    where_s[1] = my
    numbers = (
        LOG2E * (-0.5 * (ca * mx * mx + cc * my * my) - cb * mx * my + where_s[5]),
        LOG2E * (ca * mx + cb * my),
        LOG2E * (cc * my + cb * mx),
        (-0.5 * LOG2E) * ca,
        -LOG2E * cb,
        (-0.5 * LOG2E) * cc,
        where_s[6],
        where_s[7],
        where_s[8],
    )
    coef[...] = jnp.zeros_like(coef)
    for q, number in enumerate(numbers):
        coef[pl.ds(q, ROWS, stride=16), :] = jnp.where(live, number, -1e9 if q == 0 else 0.0)
    wh_s[...] = jnp.zeros_like(wh_s)
    wl_s[...] = jnp.zeros_like(wl_s)
    gh_s[...] = jnp.zeros_like(gh_s)
    gl_s[...] = jnp.zeros_like(gl_s)

    flat = (16, PIX)
    line = iota(flat, 0)
    ox = jnp.bitwise_and(iota(flat, 1), 15).astype(f32) - 7.5
    oy = lax.shift_right_logical(iota(flat, 1), 4).astype(f32) - 7.5
    terms = (jnp.ones(flat, f32), ox, oy, ox * ox, ox * oy, oy * oy)
    basis = jnp.zeros(flat, f32)
    for q, term in enumerate(terms):
        basis = jnp.where(line == q, term, basis)
    basis = basis.astype(bf16)
    none = jnp.zeros(flat, bf16)
    powers_rhs = jnp.concatenate([basis, basis, basis, none, none, none], axis=0)
    sub = iota((8, PIX), 0)
    contract_first = (((0,), (0,)), ((), ()))
    contract_last = (((1,), (1,)), ((), ()))

    def one_tile(t, _):
        parts = []
        for c in range(4):
            at = pl.multiple_of((4 * t + c) * 16, 16)
            parts.append(coef[pl.ds(at, 16), :])
        hi, mid, lo = split3(jnp.concatenate(parts, axis=1))
        at = pl.multiple_of(t * PIX, PIX)
        cot = jnp.zeros(flat, f32)
        for c in range(3):
            cot = jnp.where(line == 6 + c, cot_ref[c : c + 1, pl.ds(at, PIX)], cot)
        t_hi, t_mid, t_lo = split3(cot)
        lhs = jnp.concatenate([hi, mid, lo, hi, mid, hi], axis=0)
        cot_rhs = jnp.concatenate([t_hi, t_hi, t_hi, t_mid, t_mid, t_lo], axis=0)
        alpha_s[...] = jnp.exp2(lax.dot_general(lhs, powers_rhs, contract_first, preferred_element_type=f32))
        w_s[...] = lax.dot_general(lhs, cot_rhs, contract_first, preferred_element_type=f32)
        blocks = lax.shift_right_logical(chain_length(count_ref[t]), 2)

        def forward(b, state):
            left, total = state
            base = pl.multiple_of(b * 32, 32)
            for j in range(4):
                rows = pl.ds(base + 8 * j, 8)
                v = left * alpha_s[rows, :]
                v_s[rows, :] = v
                left = left - v
                total = total + v * w_s[rows, :]
            return left, total

        left, total = lax.fori_loop(
            0, blocks, forward, (jnp.ones((8, PIX), f32), jnp.zeros((8, PIX), f32))
        )
        enter = jnp.ones((8, PIX), f32)
        run = left[0:1]
        for s in range(1, 8):
            enter = jnp.where(sub == s, run, enter)
            run = run * left[s : s + 1]
        behind = jnp.zeros((8, PIX), f32)
        run = total[7:8]
        for s in range(6, -1, -1):
            behind = jnp.where(sub == s, run, behind)
            run = total[s : s + 1] + left[s : s + 1] * run

        def backward(i, behind):
            base = pl.multiple_of((blocks - 1 - i) * 32, 32)
            weights = [None] * 4
            grads = [None] * 4
            for j in range(3, -1, -1):
                rows = pl.ds(base + 8 * j, 8)
                gap = w_s[rows, :] - behind
                weights[j] = enter * v_s[rows, :]
                grads[j] = weights[j] * gap
                behind = behind + alpha_s[rows, :] * gap
            rows = pl.ds(base, 32)
            wh_s[rows, :], wl_s[rows, :] = split2(jnp.concatenate(weights, axis=0))
            gh_s[rows, :], gl_s[rows, :] = split2(jnp.concatenate(grads, axis=0))
            return behind

        lax.fori_loop(0, blocks, backward, behind)
        wh, wl = wh_s[...], wl_s[...]

        def pixel_sum(a, b):
            return lax.dot_general(a, b, contract_last, preferred_element_type=f32)

        got = (
            pixel_sum(basis, gh_s[...])
            + pixel_sum(basis, gl_s[...])
            + pixel_sum(t_hi, wh)
            + pixel_sum(t_mid, wh)
            + pixel_sum(t_hi, wl)
        )
        for c in range(4):
            at_c = pl.multiple_of((4 * t + c) * 16, 16)
            sums[pl.ds(at_c, 16), :] = got[:, c * LANES : (c + 1) * LANES]
        image = (
            jnp.dot(hi, wh, preferred_element_type=f32)
            + jnp.dot(mid, wh, preferred_element_type=f32)
            + jnp.dot(hi, wl, preferred_element_type=f32)
        )
        image_ref[:, pl.ds(at, PIX)] = image[6:9]
        return 0

    lax.fori_loop(0, TILES, one_tile, 0)

    s = [sums[pl.ds(q, ROWS, stride=16), :] for q in range(PROJ)]
    mx, my, ca, cb, cc = (where_s[r] for r in range(5))
    sx = s[1] - mx * s[0]
    sy = s[2] - my * s[0]
    grads = (
        ca * sx + cb * sy,
        cc * sy + cb * sx,
        -0.5 * (s[3] - mx * (s[1] + sx)),
        -(s[4] - mx * s[2] - my * sx),
        -0.5 * (s[5] - my * (s[2] + sy)),
        s[0],
        s[6],
        s[7],
        s[8],
    )
    for r in range(PROJ):
        table[r] = jnp.where(live, grads[r], 0.0)

    def hand(r, at, value):
        grad_ref[at : at + value.shape[0], r, :] = value

    regroup(table, ROWS, group_ref[...], hand)


def pull_kernel(angle_ref, gauss_ref, asked_ref, got_ref, out_ref, held, acc, back):
    first, second, third = view_of(angle_ref)
    weights = colour_weights(harmonics(*third))
    acc[...] = jnp.zeros_like(acc)
    high_id = iota((32, PIX), 0)
    low_id = iota((PIX, PIX), 0)

    def add(i, _):
        index = jnp.concatenate([asked_ref[2 * i], asked_ref[2 * i + 1]], axis=1)
        here = high_id == lax.shift_right_logical(index, 8)
        low = jnp.where(low_id == jnp.bitwise_and(index, 255), 1.0, 0.0).astype(bf16)
        value = jnp.concatenate([got_ref[2 * i], got_ref[2 * i + 1]], axis=1)
        hi = value.astype(bf16).astype(f32)
        lo = value - hi
        rows = []
        for r in range(PROJ):
            for part in (hi, lo):
                rows.append(jnp.where(here, part[r : r + 1], 0.0).astype(bf16))
        acc[...] += lax.dot_general(
            jnp.concatenate(rows, axis=0), low, (((1,), (1,)), ((), ())), preferred_element_type=f32
        )
        return 0

    lax.fori_loop(0, ROWS // 2, add, 0)
    slot_sum = []
    for r in range(PROJ):
        both = acc[64 * r : 64 * r + 32, :] + acc[64 * r + 32 : 64 * r + 64, :]
        slot_sum.append(jnp.concatenate([both[:, :LANES], both[:, LANES:]], axis=0))

    def row_of(i):
        return (i % 2) * 32 + i // 2

    params = spread(gauss_ref, held, row_of)
    _, pullback = jax.vjp(lambda *p: project(p, first, second), *params)
    grads = pullback(tuple(slot_sum[:6]))
    held[...] = jnp.zeros_like(held)
    for r in range(11):
        held[pl.ds(r, ROWS, stride=16), :] = grads[r]
    for c in range(3):
        back[c] = slot_sum[6 + c]
    for i in range(ROWS):
        at = row_of(i)
        lanes = slice(i * LANES, (i + 1) * LANES)
        tint = [back[c, at : at + 1, :] for c in range(3)]
        w0, w1, w2 = weights
        out_ref[0:8, lanes] = held[at * 16 : at * 16 + 8, :]
        out_ref[8:16, lanes] = held[at * 16 + 8 : at * 16 + 16, :] + w0[0:8] * tint[0]
        out_ref[16:24, lanes] = w0[8:16] * tint[0]
        out_ref[24:32, lanes] = w0[16:24] * tint[0] + w1[0:8] * tint[1]
        out_ref[32:40, lanes] = w1[8:16] * tint[1]
        out_ref[40:48, lanes] = w1[16:24] * tint[1] + w2[0:8] * tint[2]
        out_ref[48:56, lanes] = w2[8:16] * tint[2]
        out_ref[56:59, lanes] = w2[16:19] * tint[2]


VMEM = pl.BlockSpec(memory_space=pltpu.VMEM)
SMEM = pl.BlockSpec(memory_space=pltpu.SMEM)


def sds(shape, dtype=f32):
    return jax.ShapeDtypeStruct(shape, dtype)


def route(counts, owners, locals_):
    return pl.pallas_call(
        route_kernel,
        out_shape=(sds((ROWS, 1, LANES), i32), sds((ROWS, LANES), i32), sds((ROWS, LANES), i32)),
        in_specs=[SMEM, VMEM, VMEM],
        out_specs=(VMEM, VMEM, VMEM),
        scratch_shapes=[
            pltpu.VMEM((TILES, SLOTS), i32),
            pltpu.VMEM((TILES, SLOTS), i32),
            pltpu.VMEM((DEVS, 256), f32),
            pltpu.VMEM((256, LANES), f32),
        ],
        name="route",
    )(counts, owners, locals_)


def answer(angles, gaussians, asked):
    return pl.pallas_call(
        answer_kernel,
        out_shape=sds((ROWS, PROJ, LANES)),
        in_specs=[SMEM, VMEM, VMEM],
        out_specs=VMEM,
        scratch_shapes=[pltpu.VMEM((ROWS * 16, LANES), f32), pltpu.VMEM((PROJ, ROWS, LANES), f32)],
        name="answer",
    )(angles, gaussians, asked)


def render(counts, order, got, pos, group, cot):
    return pl.pallas_call(
        render_kernel,
        out_shape=(sds((3, TILES * PIX)), sds((ROWS, PROJ, LANES))),
        in_specs=[SMEM, SMEM, VMEM, VMEM, VMEM, VMEM],
        out_specs=(VMEM, VMEM),
        scratch_shapes=[
            pltpu.VMEM((PROJ, ROWS, LANES), f32),
            pltpu.VMEM((PROJ, ROWS, LANES), f32),
            pltpu.VMEM((ROWS * 16, LANES), f32),
            pltpu.VMEM((ROWS * 16, LANES), f32),
            pltpu.VMEM((SLOTS, PIX), f32),
            pltpu.VMEM((SLOTS, PIX), f32),
            pltpu.VMEM((SLOTS, PIX), f32),
            pltpu.VMEM((SLOTS, PIX), bf16),
            pltpu.VMEM((SLOTS, PIX), bf16),
            pltpu.VMEM((SLOTS, PIX), bf16),
            pltpu.VMEM((SLOTS, PIX), bf16),
        ],
        name="render",
    )(counts, order, got, pos, group, cot)


def pull(angles, gaussians, asked, got):
    return pl.pallas_call(
        pull_kernel,
        out_shape=sds(gaussians.shape),
        in_specs=[SMEM, VMEM, VMEM, VMEM],
        out_specs=VMEM,
        scratch_shapes=[
            pltpu.VMEM((ROWS * 16, LANES), f32),
            pltpu.VMEM((64 * PROJ, PIX), f32),
            pltpu.VMEM((3, ROWS, LANES), f32),
        ],
        name="pull",
    )(angles, gaussians, asked, got)


def shards(gaussians, view_angles, tile_order, tile_owners, tile_locals, list_counts, image_cotangent):
    wanted, pos, group = route(list_counts, tile_owners, tile_locals)
    asked = exchange(wanted, 0)
    picked = answer(view_angles, gaussians, asked)
    arrived = exchange(picked, 1)
    rendered, slot_grads = render(list_counts, tile_order, arrived, pos, group, image_cotangent)
    returned = exchange(slot_grads, 2)
    gradients = pull(view_angles, gaussians, asked, returned)
    return rendered, gradients


def solution(mesh):
    return jax.shard_map(
        shards,
        mesh=mesh,
        in_specs=(
            P(None, "dev"),
            P(),
            P("dev"),
            P("dev", None),
            P("dev", None),
            P("dev"),
            P(None, "dev"),
        ),
        out_specs=(P(None, "dev"), P(None, "dev")),
        check_vma=False,
    )
```

```python
from functools import partial

import jax
import jax.numpy as jnp
from jax import lax
from jax.experimental import pallas as pl
from jax.experimental.pallas import tpu as pltpu
from jax.sharding import PartitionSpec as P

DEVS = 128
CHIPS = 64
TILES = 16
SLOTS = 512
ROWS = 64
LANES = 128
PROJ = 9
PIX = 256
TX = 32
FOCAL_X = 128.0
FOCAL_Y = 256.0
CENTRE_X = 256.0
CENTRE_Y = 512.0
LOG2E = 1.4426950408889634
MESH = pl.DeviceIdType.MESH
f32 = jnp.float32
bf16 = jnp.bfloat16
i32 = jnp.int32


def iota(shape, dim):
    return lax.broadcasted_iota(i32, shape, dim)


def split2(x):
    hi = x.astype(bf16)
    return hi, (x - hi.astype(f32)).astype(bf16)


def split3(x):
    hi = x.astype(bf16)
    rest = x - hi.astype(f32)
    mid = rest.astype(bf16)
    return hi, mid, (rest - mid.astype(f32)).astype(bf16)


def lane_pick(table, index):
    return jnp.take_along_axis(table, index, axis=1)


def view_of(angle_ref):
    def turn(i):
        angle = jnp.full((8, LANES), angle_ref[i], f32)
        return jnp.cos(angle)[0:1], jnp.sin(angle)[0:1]

    (ca, sa), (cb, sb), (cc, sc) = turn(0), turn(1), turn(2)
    first = (cc * cb, cc * sb * sa - sc * ca, cc * sb * ca + sc * sa)
    second = (sc * cb, sc * sb * sa + cc * ca, sc * sb * ca - cc * sa)
    third = (-sb, cb * sa, cb * ca)
    return first, second, third


def harmonics(x, y, z):
    xx, yy, zz = x * x, y * y, z * z
    return [
        0.28209479177387814 + 0.0 * x,
        -0.4886025119029199 * y,
        0.4886025119029199 * z,
        -0.4886025119029199 * x,
        1.0925484305920792 * x * y,
        -1.0925484305920792 * y * z,
        0.31539156525252005 * (2.0 * zz - xx - yy),
        -1.0925484305920792 * x * z,
        0.5462742152960396 * (xx - yy),
        -0.5900435899266435 * y * (3.0 * xx - yy),
        2.890611442640554 * x * y * z,
        -0.4570457994644658 * y * (4.0 * zz - xx - yy),
        0.3731763325901154 * z * (2.0 * zz - 3.0 * xx - 3.0 * yy),
        -0.4570457994644658 * x * (4.0 * zz - xx - yy),
        1.445305721320277 * z * (xx - yy),
        -0.5900435899266435 * x * (xx - 3.0 * yy),
    ]


COLOUR_ROWS = ((8, 32), (24, 48), (40, 59))


def colour_weights(basis):
    out = []
    for c, (low, high) in enumerate(COLOUR_ROWS):
        row = iota((high - low, LANES), 0) + low - (11 + 16 * c)
        held = jnp.zeros((high - low, LANES), f32)
        for k in range(16):
            held = jnp.where(row == k, basis[k], held)
        out.append(held)
    return out


def project(params, first, second):
    px, py, pz, s0, s1, s2, qw, qx, qy, qz, logit = params
    mean_x = CENTRE_X + FOCAL_X * (first[0] * px + first[1] * py + first[2] * pz)
    mean_y = CENTRE_Y + FOCAL_Y * (second[0] * px + second[1] * py + second[2] * pz)
    scales = (jnp.exp(s0), jnp.exp(s1), jnp.exp(s2))
    two_n = 2.0 / jnp.maximum(qw * qw + qx * qx + qy * qy + qz * qz, 1.0)
    turned = (
        (1.0 - two_n * (qy * qy + qz * qz), two_n * (qx * qy - qw * qz), two_n * (qx * qz + qw * qy)),
        (two_n * (qx * qy + qw * qz), 1.0 - two_n * (qx * qx + qz * qz), two_n * (qy * qz - qw * qx)),
        (two_n * (qx * qz - qw * qy), two_n * (qy * qz + qw * qx), 1.0 - two_n * (qx * qx + qy * qy)),
    )
    va = []
    vb = []
    for j in range(3):
        va.append(FOCAL_X * (first[0] * turned[0][j] + first[1] * turned[1][j] + first[2] * turned[2][j]) * scales[j])
        vb.append(FOCAL_Y * (second[0] * turned[0][j] + second[1] * turned[1][j] + second[2] * turned[2][j]) * scales[j])
    cov_a = va[0] * va[0] + va[1] * va[1] + va[2] * va[2] + 0.3
    cov_b = va[0] * vb[0] + va[1] * vb[1] + va[2] * vb[2]
    cov_c = vb[0] * vb[0] + vb[1] * vb[1] + vb[2] * vb[2] + 0.3
    inv = 1.0 / (cov_a * cov_c - cov_b * cov_b)
    log_opacity = -jnp.log(1.0 + jnp.exp(-logit))
    return mean_x, mean_y, cov_c * inv, -cov_b * inv, cov_a * inv, log_opacity


def regroup(table_ref, rows_of, index, store):
    part_rows = 16
    for part in range(ROWS // part_rows):
        flat = index[part * part_rows : (part + 1) * part_rows]
        high = lax.shift_right_logical(flat, 7)
        low = jnp.bitwise_and(flat, 127)

        def step(i, held):
            here = high == i
            out = []
            for r in range(PROJ):
                row = jnp.broadcast_to(table_ref[r, pl.ds(i, 1), :], (part_rows, LANES))
                out.append(jnp.where(here, lane_pick(row, low), held[r]))
            return tuple(out)

        start = tuple(jnp.zeros((part_rows, LANES), f32) for _ in range(PROJ))
        taken = lax.fori_loop(0, ROWS, step, start, unroll=16)
        for r in range(PROJ):
            store(r, part * part_rows, taken[r])


def chain_length(count):
    return lax.shift_left(lax.shift_right_logical(count + 31, 5), 2)


def route(count_ref, owner_ref, local_ref, want_ref, pos_ref, group_ref, own_s, loc_s, carry_s, sum_s):
    tile = iota((TILES, LANES), 0)
    length = jnp.zeros((TILES, LANES), i32)
    for t in range(TILES):
        length = jnp.where(tile == t, chain_length(count_ref[t]), length)
    for d in range(SLOTS // LANES):
        row = iota((TILES, LANES), 1) + d * LANES
        slot = jnp.where(row < 8 * length, jnp.bitwise_and(row, 7) * length + lax.shift_right_logical(row, 3), row)
        high = lax.shift_right_logical(slot, 7)
        low = jnp.bitwise_and(slot, 127)
        for src, dst in ((owner_ref, own_s), (local_ref, loc_s)):
            held = jnp.zeros((TILES, LANES), i32)
            for c in range(SLOTS // LANES):
                held = jnp.where(high == c, lane_pick(src[:, c * LANES : (c + 1) * LANES], low), held)
            dst[:, d * LANES : (d + 1) * LANES] = held
    half = 256
    before = jnp.where(iota((half, half), 0) < iota((half, half), 1), 1.0, 0.0).astype(bf16)
    ones = jnp.ones((half, half), bf16)
    both = jnp.concatenate([before, ones], axis=1)
    carry_s[...] = jnp.zeros_like(carry_s)
    sum_s[...] = jnp.zeros_like(sum_s)
    owner_id = iota((DEVS, half), 0)
    pair_id = iota((ROWS, half), 0)
    lane_id = iota((LANES, half), 0)

    def step(t, _):
        for h in range(2):
            owner = own_s[pl.ds(t, 1), h * half : (h + 1) * half]
            local = loc_s[pl.ds(t, 1), h * half : (h + 1) * half]
            hit = owner_id == owner
            hit_f = jnp.where(hit, 1.0, 0.0)
            counts = jnp.dot(hit_f.astype(bf16), both, preferred_element_type=f32)
            seen = carry_s[...]
            rank = jnp.sum(hit_f * (counts[:, :half] + seen), axis=0, keepdims=True).astype(i32)
            carry_s[...] = seen + counts[:, half:]
            place = owner * ROWS + rank
            pos_ref[pl.ds(4 * t + 2 * h, 1), :] = place[:, :LANES]
            pos_ref[pl.ds(4 * t + 2 * h + 1, 1), :] = place[:, LANES:]
            pair = pair_id == lax.shift_right_logical(place, 7)
            lane = jnp.where(lane_id == jnp.bitwise_and(place, 127), 1.0, 0.0).astype(bf16)
            slot = t * SLOTS + h * half + iota((1, half), 1)
            parts = []
            for number in (local, slot):
                for part in (lax.shift_right_logical(number, 7), jnp.bitwise_and(number, 127)):
                    parts.append(jnp.where(pair, part.astype(f32), 0.0).astype(bf16))
            sum_s[...] += lax.dot_general(
                jnp.concatenate(parts, axis=0), lane, (((1,), (1,)), ((), ())), preferred_element_type=f32
            )
        return 0

    lax.fori_loop(0, TILES, step, 0)
    total = sum_s[...].astype(i32)
    want_ref[:, 0, :] = total[0:64] * 128 + total[64:128]
    group_ref[...] = total[128:192] * 128 + total[192:256]


class Exchange:
    def __init__(self, x_ref, near, far, send_sem, recv_sem, pair_sem):
        self.refs = (x_ref, near, far)
        self.sems = (send_sem, recv_sem, pair_sem)
        me = lax.axis_index("dev")
        self.chip = me // 2
        self.core = me % 2
        self.other = self.chip * 2 + (1 - self.core)

    def copy(self, i):
        x_ref, near, _ = self.refs
        to = (self.chip + i) % CHIPS
        return pltpu.make_async_remote_copy(
            src_ref=x_ref.at[to],
            dst_ref=near.at[self.chip],
            send_sem=self.sems[0].at[i],
            recv_sem=self.sems[1].at[i],
            device_id=(to * 2 + self.core,),
            device_id_type=MESH,
        )

    def incoming(self, i):
        x_ref, near, _ = self.refs
        source = (self.chip + CHIPS - i) % CHIPS
        return pltpu.make_async_remote_copy(
            src_ref=x_ref.at[source],
            dst_ref=near.at[source],
            send_sem=self.sems[0].at[i],
            recv_sem=self.sems[1].at[i],
            device_id=(source * 2 + self.core,),
            device_id_type=MESH,
        )

    def send(self):
        def one(i, _):
            self.copy(i).start()
            return 0

        lax.fori_loop(1, CHIPS, one, 0)
        self.refs[1][self.chip] = self.refs[0][self.chip]

    def receive(self):
        _, near, far = self.refs

        def arrived(i, _):
            self.incoming(i).wait_recv()
            return 0

        lax.fori_loop(1, CHIPS, arrived, 0)
        swap = pltpu.make_async_remote_copy(
            src_ref=near,
            dst_ref=far,
            send_sem=self.sems[2].at[0],
            recv_sem=self.sems[2].at[1],
            device_id=(self.other,),
            device_id_type=MESH,
        )
        swap.start()

        def sent(i, _):
            self.copy(i).wait_send()
            return 0

        lax.fori_loop(1, CHIPS, sent, 0)
        swap.wait()

    def row(self, r):
        _, near, far = self.refs
        mine = lax.shift_right_logical(iota((CHIPS, LANES), 1), 6) == self.core
        return jnp.where(mine, near[:, r, :], pltpu.roll(far[:, r, :], 64, 1))


def greet():
    me = lax.axis_index("dev")
    chip = me // 2
    core = me % 2
    barrier = pltpu.get_barrier_semaphore()

    def one(i, _):
        peer = ((chip + i) % CHIPS) * 2 + core
        pl.semaphore_signal(barrier, inc=1, device_id=(peer,), device_id_type=MESH)
        return 0

    lax.fori_loop(1, CHIPS, one, 0)
    pl.semaphore_signal(barrier, inc=1, device_id=(chip * 2 + (1 - core),), device_id_type=MESH)


def met():
    pl.semaphore_wait(pltpu.get_barrier_semaphore(), CHIPS)


def exchange_scratch(rows, dtype):
    box = pltpu.VMEM((CHIPS, rows, LANES), dtype)
    sem = pltpu.SemaphoreType.DMA((CHIPS,))
    return [box, box, box, sem, sem, pltpu.SemaphoreType.DMA((2,))]


def spread(gauss_ref, held, row_of):
    for i in range(ROWS):
        at = row_of(i) * 16
        held[at : at + 16, :] = gauss_ref[0:16, i * LANES : (i + 1) * LANES]
    return [held[pl.ds(r, ROWS, stride=16), :] for r in range(11)]


def fetch_kernel(
    count_ref, angle_ref, owner_ref, local_ref, gauss_hbm, got_ref, asked_ref, pos_ref, group_ref, *scratch
):
    own_s, loc_s, carry_s, sum_s, gauss_ref, held, table, load_sem = scratch[:8]
    load = pltpu.make_async_copy(gauss_hbm, gauss_ref, load_sem)
    load.start()
    greet()
    ask = Exchange(*scratch[8:14])
    reply = Exchange(*scratch[14:20])
    route(count_ref, owner_ref, local_ref, scratch[8], pos_ref, group_ref, own_s, loc_s, carry_s, sum_s)
    met()
    ask.send()
    first, second, third = view_of(angle_ref)
    weights = colour_weights(harmonics(*third))
    load.wait()
    params = spread(gauss_ref, held, lambda i: i)
    for r, value in enumerate(project(params, first, second)):
        table[r] = value
    for i in range(ROWS):
        lanes = slice(i * LANES, (i + 1) * LANES)
        for c, (low, high) in enumerate(COLOUR_ROWS):
            table[6 + c, i : i + 1, :] = 0.5 + jnp.sum(
                gauss_ref[low:high, lanes] * weights[c], axis=0, keepdims=True
            )
    ask.receive()
    asked = ask.row(0)
    asked_ref[...] = asked
    picked = scratch[14]

    def store(r, at, value):
        picked[at : at + value.shape[0], r, :] = value

    regroup(table, ROWS, asked, store)
    reply.send()
    reply.receive()
    for r in range(PROJ):
        got_ref[r] = reply.row(r)


def render_kernel(
    count_ref, order_ref, got_ref, pos_ref, group_ref, cot_ref, image_ref, grad_ref,
    table, where_s, coef, sums, alpha_s, w_s, v_s, gh_s, gl_s, wh_s, wl_s,
):
    shape = (ROWS, LANES)
    tile = lax.shift_right_logical(iota(shape, 0), 2)
    row = jnp.bitwise_and(iota(shape, 0), 3) * LANES + iota(shape, 1)
    length = jnp.zeros(shape, i32)
    count = jnp.zeros(shape, i32)
    shown = jnp.zeros(shape, i32)
    for t in range(TILES):
        here = tile == t
        length = jnp.where(here, chain_length(count_ref[t]), length)
        count = jnp.where(here, count_ref[t], count)
        shown = jnp.where(here, order_ref[t], shown)
    slot = jnp.where(row < 8 * length, jnp.bitwise_and(row, 7) * length + lax.shift_right_logical(row, 3), row)
    live = slot < count
    mid_x = (jnp.bitwise_and(shown, TX - 1) * 16 + 8).astype(f32)
    mid_y = (lax.shift_right_logical(shown, 5) * 16 + 8).astype(f32)

    def keep(r, at, value):
        where_s[r, at : at + value.shape[0], :] = value

    regroup(got_ref, ROWS, pos_ref[...], keep)
    mx = where_s[0] - mid_x
    my = where_s[1] - mid_y
    ca, cb, cc = where_s[2], where_s[3], where_s[4]
    where_s[0] = mx
    where_s[1] = my
    numbers = (
        LOG2E * (-0.5 * (ca * mx * mx + cc * my * my) - cb * mx * my + where_s[5]),
        LOG2E * (ca * mx + cb * my),
        LOG2E * (cc * my + cb * mx),
        (-0.5 * LOG2E) * ca,
        -LOG2E * cb,
        (-0.5 * LOG2E) * cc,
        where_s[6],
        where_s[7],
        where_s[8],
    )
    coef[...] = jnp.zeros_like(coef)
    for q, number in enumerate(numbers):
        coef[pl.ds(q, ROWS, stride=16), :] = jnp.where(live, number, -1e9 if q == 0 else 0.0)
    wh_s[...] = jnp.zeros_like(wh_s)
    wl_s[...] = jnp.zeros_like(wl_s)
    gh_s[...] = jnp.zeros_like(gh_s)
    gl_s[...] = jnp.zeros_like(gl_s)

    flat = (16, PIX)
    line = iota(flat, 0)
    ox = jnp.bitwise_and(iota(flat, 1), 15).astype(f32) - 7.5
    oy = lax.shift_right_logical(iota(flat, 1), 4).astype(f32) - 7.5
    terms = (jnp.ones(flat, f32), ox, oy, ox * ox, ox * oy, oy * oy)
    basis = jnp.zeros(flat, f32)
    for q, term in enumerate(terms):
        basis = jnp.where(line == q, term, basis)
    basis = basis.astype(bf16)
    none = jnp.zeros(flat, bf16)
    powers_rhs = jnp.concatenate([basis, basis, basis, none, none, none], axis=0)
    sub = iota((8, PIX), 0)
    contract_first = (((0,), (0,)), ((), ()))
    contract_last = (((1,), (1,)), ((), ()))

    def one_tile(t, _):
        parts = []
        for c in range(4):
            at = pl.multiple_of((4 * t + c) * 16, 16)
            parts.append(coef[pl.ds(at, 16), :])
        hi, mid, lo = split3(jnp.concatenate(parts, axis=1))
        at = pl.multiple_of(t * PIX, PIX)
        cot = jnp.zeros(flat, f32)
        for c in range(3):
            cot = jnp.where(line == 6 + c, cot_ref[c : c + 1, pl.ds(at, PIX)], cot)
        t_hi, t_mid, t_lo = split3(cot)
        lhs = jnp.concatenate([hi, mid, lo, hi, mid, hi], axis=0)
        cot_rhs = jnp.concatenate([t_hi, t_hi, t_hi, t_mid, t_mid, t_lo], axis=0)
        alpha_s[...] = jnp.exp2(lax.dot_general(lhs, powers_rhs, contract_first, preferred_element_type=f32))
        w_s[...] = lax.dot_general(lhs, cot_rhs, contract_first, preferred_element_type=f32)
        blocks = lax.shift_right_logical(chain_length(count_ref[t]), 2)

        def forward(b, state):
            left, total = state
            base = pl.multiple_of(b * 32, 32)
            for j in range(4):
                rows = pl.ds(base + 8 * j, 8)
                v = left * alpha_s[rows, :]
                v_s[rows, :] = v
                left = left - v
                total = total + v * w_s[rows, :]
            return left, total

        left, total = lax.fori_loop(
            0, blocks, forward, (jnp.ones((8, PIX), f32), jnp.zeros((8, PIX), f32))
        )
        enter = jnp.ones((8, PIX), f32)
        run = left[0:1]
        for s in range(1, 8):
            enter = jnp.where(sub == s, run, enter)
            run = run * left[s : s + 1]
        behind = jnp.zeros((8, PIX), f32)
        run = total[7:8]
        for s in range(6, -1, -1):
            behind = jnp.where(sub == s, run, behind)
            run = total[s : s + 1] + left[s : s + 1] * run

        def backward(i, behind):
            base = pl.multiple_of((blocks - 1 - i) * 32, 32)
            weights = [None] * 4
            grads = [None] * 4
            for j in range(3, -1, -1):
                rows = pl.ds(base + 8 * j, 8)
                gap = w_s[rows, :] - behind
                weights[j] = enter * v_s[rows, :]
                grads[j] = weights[j] * gap
                behind = behind + alpha_s[rows, :] * gap
            rows = pl.ds(base, 32)
            wh_s[rows, :], wl_s[rows, :] = split2(jnp.concatenate(weights, axis=0))
            gh_s[rows, :], gl_s[rows, :] = split2(jnp.concatenate(grads, axis=0))
            return behind

        lax.fori_loop(0, blocks, backward, behind)
        wh, wl = wh_s[...], wl_s[...]

        def pixel_sum(a, b):
            return lax.dot_general(a, b, contract_last, preferred_element_type=f32)

        got = (
            pixel_sum(basis, gh_s[...])
            + pixel_sum(basis, gl_s[...])
            + pixel_sum(t_hi, wh)
            + pixel_sum(t_mid, wh)
            + pixel_sum(t_hi, wl)
        )
        for c in range(4):
            at_c = pl.multiple_of((4 * t + c) * 16, 16)
            sums[pl.ds(at_c, 16), :] = got[:, c * LANES : (c + 1) * LANES]
        image = (
            jnp.dot(hi, wh, preferred_element_type=f32)
            + jnp.dot(mid, wh, preferred_element_type=f32)
            + jnp.dot(hi, wl, preferred_element_type=f32)
        )
        image_ref[:, pl.ds(at, PIX)] = image[6:9]
        return 0

    lax.fori_loop(0, TILES, one_tile, 0)

    s = [sums[pl.ds(q, ROWS, stride=16), :] for q in range(PROJ)]
    mx, my, ca, cb, cc = (where_s[r] for r in range(5))
    sx = s[1] - mx * s[0]
    sy = s[2] - my * s[0]
    grads = (
        ca * sx + cb * sy,
        cc * sy + cb * sx,
        -0.5 * (s[3] - mx * (s[1] + sx)),
        -(s[4] - mx * s[2] - my * sx),
        -0.5 * (s[5] - my * (s[2] + sy)),
        s[0],
        s[6],
        s[7],
        s[8],
    )
    for r in range(PROJ):
        table[r] = jnp.where(live, grads[r], 0.0)

    def hand(r, at, value):
        grad_ref[at : at + value.shape[0], r, :] = value

    regroup(table, ROWS, group_ref[...], hand)


def add_kernel(asked_ref, grad_ref, sum_ref, acc, low_s, *scratch):
    greet()
    back = Exchange(grad_ref, *scratch)
    near, far = scratch[:2]
    low_id = iota((PIX, PIX), 0)
    high_id = iota((32, PIX), 0)

    def find(i, _):
        index = jnp.concatenate([asked_ref[pl.ds(2 * i, 1), :], asked_ref[pl.ds(2 * i + 1, 1), :]], axis=1)
        at = pl.multiple_of(i * PIX, PIX)
        low_s[pl.ds(at, PIX), :] = jnp.where(low_id == jnp.bitwise_and(index, 255), 1.0, 0.0).astype(bf16)
        return 0

    met()
    back.send()
    lax.fori_loop(0, ROWS // 2, find, 0)
    acc[...] = jnp.zeros_like(acc)
    back.receive()
    mine = lax.shift_right_logical(iota((PROJ, LANES), 1), 6) == back.core

    def add(i, _):
        index = jnp.concatenate([asked_ref[pl.ds(2 * i, 1), :], asked_ref[pl.ds(2 * i + 1, 1), :]], axis=1)
        here = high_id == lax.shift_right_logical(index, 8)
        halves = []
        for j in range(2):
            halves.append(jnp.where(mine, near[2 * i + j], pltpu.roll(far[2 * i + j], 64, 1)))
        value = jnp.concatenate(halves, axis=1)
        hi = value.astype(bf16).astype(f32)
        lo = value - hi
        rows = []
        for r in range(PROJ):
            for part in (hi, lo):
                rows.append(jnp.where(here, part[r : r + 1], 0.0).astype(bf16))
        at = pl.multiple_of(i * PIX, PIX)
        acc[...] += lax.dot_general(
            jnp.concatenate(rows, axis=0),
            low_s[pl.ds(at, PIX), :],
            (((1,), (1,)), ((), ())),
            preferred_element_type=f32,
        )
        return 0

    lax.fori_loop(0, ROWS // 2, add, 0)
    for r in range(PROJ):
        both = acc[64 * r : 64 * r + 32, :] + acc[64 * r + 32 : 64 * r + 64, :]
        sum_ref[r] = jnp.concatenate([both[:, :LANES], both[:, LANES:]], axis=0)


def pull_kernel(angle_ref, gauss_ref, sum_ref, out_ref, held):
    first, second, third = view_of(angle_ref)
    weights = colour_weights(harmonics(*third))

    def row_of(i):
        return (i % 2) * 32 + i // 2

    params = spread(gauss_ref, held, row_of)
    _, pullback = jax.vjp(lambda *p: project(p, first, second), *params)
    grads = pullback(tuple(sum_ref[r] for r in range(6)))
    held[...] = jnp.zeros_like(held)
    for r in range(11):
        held[pl.ds(r, ROWS, stride=16), :] = grads[r]
    w0, w1, w2 = weights
    for i in range(ROWS):
        at = row_of(i)
        lanes = slice(i * LANES, (i + 1) * LANES)
        tint = [sum_ref[6 + c, at : at + 1, :] for c in range(3)]
        out_ref[0:8, lanes] = held[at * 16 : at * 16 + 8, :]
        out_ref[8:16, lanes] = held[at * 16 + 8 : at * 16 + 16, :] + w0[0:8] * tint[0]
        out_ref[16:24, lanes] = w0[8:16] * tint[0]
        out_ref[24:32, lanes] = w0[16:24] * tint[0] + w1[0:8] * tint[1]
        out_ref[32:40, lanes] = w1[8:16] * tint[1]
        out_ref[40:48, lanes] = w1[16:24] * tint[1] + w2[0:8] * tint[2]
        out_ref[48:56, lanes] = w2[8:16] * tint[2]
        out_ref[56:59, lanes] = w2[16:19] * tint[2]


VMEM = pl.BlockSpec(memory_space=pltpu.VMEM)
SMEM = pl.BlockSpec(memory_space=pltpu.SMEM)
ANY = pl.BlockSpec(memory_space=pl.ANY)


def sds(shape, dtype=f32):
    return jax.ShapeDtypeStruct(shape, dtype)


def fetch(counts, angles, owners, locals_, gaussians):
    box = sds((ROWS, LANES), i32)
    return pl.pallas_call(
        fetch_kernel,
        out_shape=(sds((PROJ, ROWS, LANES)), box, box, box),
        in_specs=[SMEM, SMEM, VMEM, VMEM, ANY],
        out_specs=(VMEM, VMEM, VMEM, VMEM),
        scratch_shapes=[
            pltpu.VMEM((TILES, SLOTS), i32),
            pltpu.VMEM((TILES, SLOTS), i32),
            pltpu.VMEM((DEVS, 256), f32),
            pltpu.VMEM((256, LANES), f32),
            pltpu.VMEM(gaussians.shape, f32),
            pltpu.VMEM((ROWS * 16, LANES), f32),
            pltpu.VMEM((PROJ, ROWS, LANES), f32),
            pltpu.SemaphoreType.DMA,
        ]
        + exchange_scratch(1, i32)
        + exchange_scratch(PROJ, f32),
        compiler_params=pltpu.CompilerParams(collective_id=0, has_side_effects=True),
        name="fetch",
    )(counts, angles, owners, locals_, gaussians)


def render(counts, order, got, pos, group, cot):
    return pl.pallas_call(
        render_kernel,
        out_shape=(sds((3, TILES * PIX)), sds((ROWS, PROJ, LANES))),
        in_specs=[SMEM, SMEM, VMEM, VMEM, VMEM, VMEM],
        out_specs=(VMEM, VMEM),
        scratch_shapes=[
            pltpu.VMEM((PROJ, ROWS, LANES), f32),
            pltpu.VMEM((PROJ, ROWS, LANES), f32),
            pltpu.VMEM((ROWS * 16, LANES), f32),
            pltpu.VMEM((ROWS * 16, LANES), f32),
            pltpu.VMEM((SLOTS, PIX), f32),
            pltpu.VMEM((SLOTS, PIX), f32),
            pltpu.VMEM((SLOTS, PIX), f32),
            pltpu.VMEM((SLOTS, PIX), bf16),
            pltpu.VMEM((SLOTS, PIX), bf16),
            pltpu.VMEM((SLOTS, PIX), bf16),
            pltpu.VMEM((SLOTS, PIX), bf16),
        ],
        name="render",
    )(counts, order, got, pos, group, cot)


def add(asked, grads):
    return pl.pallas_call(
        add_kernel,
        out_shape=sds((PROJ, ROWS, LANES)),
        in_specs=[VMEM, VMEM],
        out_specs=VMEM,
        scratch_shapes=[pltpu.VMEM((64 * PROJ, PIX), f32), pltpu.VMEM((TILES * SLOTS, PIX), bf16)]
        + exchange_scratch(PROJ, f32)[1:],
        compiler_params=pltpu.CompilerParams(collective_id=1, has_side_effects=True),
        name="add",
    )(asked, grads)


def pull(angles, gaussians, sums):
    return pl.pallas_call(
        pull_kernel,
        out_shape=sds(gaussians.shape),
        in_specs=[SMEM, VMEM, VMEM],
        out_specs=VMEM,
        scratch_shapes=[pltpu.VMEM((ROWS * 16, LANES), f32)],
        name="pull",
    )(angles, gaussians, sums)


def shards(gaussians, view_angles, tile_order, tile_owners, tile_locals, list_counts, image_cotangent):
    got, asked, pos, group = fetch(list_counts, view_angles, tile_owners, tile_locals, gaussians)
    rendered, slot_grads = render(list_counts, tile_order, got, pos, group, image_cotangent)
    return rendered, pull(view_angles, gaussians, add(asked, slot_grads))


def solution(mesh):
    return jax.shard_map(
        shards,
        mesh=mesh,
        in_specs=(
            P(None, "dev"),
            P(),
            P("dev"),
            P("dev", None),
            P("dev", None),
            P("dev"),
            P(None, "dev"),
        ),
        out_specs=(P(None, "dev"), P(None, "dev")),
        check_vma=False,
    )
```

```python
from functools import partial

import jax
import jax.numpy as jnp
from jax import lax
from jax.experimental import pallas as pl
from jax.experimental.pallas import tpu as pltpu
from jax.sharding import PartitionSpec as P

DEVS = 128
CHIPS = 64
TILES = 16
SLOTS = 512
ROWS = 64
LANES = 128
PROJ = 9
PIX = 256
TX = 32
FOCAL_X = 128.0
FOCAL_Y = 256.0
CENTRE_X = 256.0
CENTRE_Y = 512.0
LOG2E = 1.4426950408889634
MESH = pl.DeviceIdType.MESH
f32 = jnp.float32
bf16 = jnp.bfloat16
i32 = jnp.int32


def iota(shape, dim):
    return lax.broadcasted_iota(i32, shape, dim)


def split2(x):
    hi = x.astype(bf16)
    return hi, (x - hi.astype(f32)).astype(bf16)


def split3(x):
    hi = x.astype(bf16)
    rest = x - hi.astype(f32)
    mid = rest.astype(bf16)
    return hi, mid, (rest - mid.astype(f32)).astype(bf16)


def lane_pick(table, index):
    return jnp.take_along_axis(table, index, axis=1)


def view_of(angle_ref):
    def turn(i):
        angle = jnp.full((8, LANES), angle_ref[i], f32)
        return jnp.cos(angle)[0:1], jnp.sin(angle)[0:1]

    (ca, sa), (cb, sb), (cc, sc) = turn(0), turn(1), turn(2)
    first = (cc * cb, cc * sb * sa - sc * ca, cc * sb * ca + sc * sa)
    second = (sc * cb, sc * sb * sa + cc * ca, sc * sb * ca - cc * sa)
    third = (-sb, cb * sa, cb * ca)
    return first, second, third


def harmonics(x, y, z):
    xx, yy, zz = x * x, y * y, z * z
    return [
        0.28209479177387814 + 0.0 * x,
        -0.4886025119029199 * y,
        0.4886025119029199 * z,
        -0.4886025119029199 * x,
        1.0925484305920792 * x * y,
        -1.0925484305920792 * y * z,
        0.31539156525252005 * (2.0 * zz - xx - yy),
        -1.0925484305920792 * x * z,
        0.5462742152960396 * (xx - yy),
        -0.5900435899266435 * y * (3.0 * xx - yy),
        2.890611442640554 * x * y * z,
        -0.4570457994644658 * y * (4.0 * zz - xx - yy),
        0.3731763325901154 * z * (2.0 * zz - 3.0 * xx - 3.0 * yy),
        -0.4570457994644658 * x * (4.0 * zz - xx - yy),
        1.445305721320277 * z * (xx - yy),
        -0.5900435899266435 * x * (xx - 3.0 * yy),
    ]


COLOUR_ROWS = ((8, 32), (24, 48), (40, 59))


def colour_weights(basis):
    out = []
    for c, (low, high) in enumerate(COLOUR_ROWS):
        row = iota((high - low, LANES), 0) + low - (11 + 16 * c)
        held = jnp.zeros((high - low, LANES), f32)
        for k in range(16):
            held = jnp.where(row == k, basis[k], held)
        out.append(held)
    return out


def project(params, first, second):
    px, py, pz, s0, s1, s2, qw, qx, qy, qz, logit = params
    mean_x = CENTRE_X + FOCAL_X * (first[0] * px + first[1] * py + first[2] * pz)
    mean_y = CENTRE_Y + FOCAL_Y * (second[0] * px + second[1] * py + second[2] * pz)
    scales = (jnp.exp(s0), jnp.exp(s1), jnp.exp(s2))
    two_n = 2.0 / jnp.maximum(qw * qw + qx * qx + qy * qy + qz * qz, 1.0)
    turned = (
        (1.0 - two_n * (qy * qy + qz * qz), two_n * (qx * qy - qw * qz), two_n * (qx * qz + qw * qy)),
        (two_n * (qx * qy + qw * qz), 1.0 - two_n * (qx * qx + qz * qz), two_n * (qy * qz - qw * qx)),
        (two_n * (qx * qz - qw * qy), two_n * (qy * qz + qw * qx), 1.0 - two_n * (qx * qx + qy * qy)),
    )
    va = []
    vb = []
    for j in range(3):
        va.append(FOCAL_X * (first[0] * turned[0][j] + first[1] * turned[1][j] + first[2] * turned[2][j]) * scales[j])
        vb.append(FOCAL_Y * (second[0] * turned[0][j] + second[1] * turned[1][j] + second[2] * turned[2][j]) * scales[j])
    cov_a = va[0] * va[0] + va[1] * va[1] + va[2] * va[2] + 0.3
    cov_b = va[0] * vb[0] + va[1] * vb[1] + va[2] * vb[2]
    cov_c = vb[0] * vb[0] + vb[1] * vb[1] + vb[2] * vb[2] + 0.3
    inv = 1.0 / (cov_a * cov_c - cov_b * cov_b)
    log_opacity = -jnp.log(1.0 + jnp.exp(-logit))
    return mean_x, mean_y, cov_c * inv, -cov_b * inv, cov_a * inv, log_opacity


def regroup(table_ref, rows_of, index, store):
    part_rows = 16
    for part in range(ROWS // part_rows):
        flat = index[part * part_rows : (part + 1) * part_rows]
        high = lax.shift_right_logical(flat, 7)
        low = jnp.bitwise_and(flat, 127)

        def step(i, held):
            here = high == i
            out = []
            for r in range(PROJ):
                row = jnp.broadcast_to(table_ref[r, pl.ds(i, 1), :], (part_rows, LANES))
                out.append(jnp.where(here, lane_pick(row, low), held[r]))
            return tuple(out)

        start = tuple(jnp.zeros((part_rows, LANES), f32) for _ in range(PROJ))
        taken = lax.fori_loop(0, ROWS, step, start, unroll=16)
        for r in range(PROJ):
            store(r, part * part_rows, taken[r])


def slot_of(row):
    return jnp.bitwise_and(row, 7) * (SLOTS // 8) + lax.shift_right_logical(row, 3)


def route(owner_ref, local_ref, want_ref, pos_ref, group_ref, own_s, loc_s, carry_s, sum_s):
    for d in range(SLOTS // LANES):
        row = iota((TILES, LANES), 1) + d * LANES
        slot = slot_of(row)
        high = lax.shift_right_logical(slot, 7)
        low = jnp.bitwise_and(slot, 127)
        for src, dst in ((owner_ref, own_s), (local_ref, loc_s)):
            held = jnp.zeros((TILES, LANES), i32)
            for c in range(SLOTS // LANES):
                held = jnp.where(high == c, lane_pick(src[:, c * LANES : (c + 1) * LANES], low), held)
            dst[:, d * LANES : (d + 1) * LANES] = held
    half = 256
    before = jnp.where(iota((half, half), 0) < iota((half, half), 1), 1.0, 0.0).astype(bf16)
    ones = jnp.ones((half, half), bf16)
    both = jnp.concatenate([before, ones], axis=1)
    carry_s[...] = jnp.zeros_like(carry_s)
    sum_s[...] = jnp.zeros_like(sum_s)
    owner_id = iota((DEVS, half), 0)
    pair_id = iota((ROWS, half), 0)
    lane_id = iota((LANES, half), 0)

    def step(t, _):
        for h in range(2):
            owner = own_s[pl.ds(t, 1), h * half : (h + 1) * half]
            local = loc_s[pl.ds(t, 1), h * half : (h + 1) * half]
            hit = owner_id == owner
            hit_f = jnp.where(hit, 1.0, 0.0)
            counts = jnp.dot(hit_f.astype(bf16), both, preferred_element_type=f32)
            seen = carry_s[...]
            rank = jnp.sum(hit_f * (counts[:, :half] + seen), axis=0, keepdims=True).astype(i32)
            carry_s[...] = seen + counts[:, half:]
            place = owner * ROWS + rank
            pos_ref[pl.ds(4 * t + 2 * h, 1), :] = place[:, :LANES]
            pos_ref[pl.ds(4 * t + 2 * h + 1, 1), :] = place[:, LANES:]
            pair = pair_id == lax.shift_right_logical(place, 7)
            lane = jnp.where(lane_id == jnp.bitwise_and(place, 127), 1.0, 0.0).astype(bf16)
            slot = t * SLOTS + h * half + iota((1, half), 1)
            parts = []
            for number in (local, slot):
                for part in (lax.shift_right_logical(number, 7), jnp.bitwise_and(number, 127)):
                    parts.append(jnp.where(pair, part.astype(f32), 0.0).astype(bf16))
            sum_s[...] += lax.dot_general(
                jnp.concatenate(parts, axis=0), lane, (((1,), (1,)), ((), ())), preferred_element_type=f32
            )
        return 0

    lax.fori_loop(0, TILES, step, 0)
    total = sum_s[...].astype(i32)
    want_ref[:, 0, :] = total[0:64] * 128 + total[64:128]
    group_ref[...] = total[128:192] * 128 + total[192:256]


class Exchange:
    def __init__(self, x_ref, near, far, send_sem, recv_sem, pair_sem):
        self.refs = (x_ref, near, far)
        self.sems = (send_sem, recv_sem, pair_sem)
        me = lax.axis_index("dev")
        self.chip = me // 2
        self.core = me % 2
        self.other = self.chip * 2 + (1 - self.core)

    def copy(self, i):
        x_ref, near, _ = self.refs
        to = (self.chip + i) % CHIPS
        return pltpu.make_async_remote_copy(
            src_ref=x_ref.at[to],
            dst_ref=near.at[self.chip],
            send_sem=self.sems[0].at[i],
            recv_sem=self.sems[1].at[i],
            device_id=(to * 2 + self.core,),
            device_id_type=MESH,
        )

    def incoming(self, i):
        x_ref, near, _ = self.refs
        source = (self.chip + CHIPS - i) % CHIPS
        return pltpu.make_async_remote_copy(
            src_ref=x_ref.at[source],
            dst_ref=near.at[source],
            send_sem=self.sems[0].at[i],
            recv_sem=self.sems[1].at[i],
            device_id=(source * 2 + self.core,),
            device_id_type=MESH,
        )

    def send(self):
        def one(i, _):
            self.copy(i).start()
            return 0

        lax.fori_loop(1, CHIPS, one, 0)
        self.refs[1][self.chip] = self.refs[0][self.chip]

    def receive(self):
        _, near, far = self.refs

        def arrived(i, _):
            self.incoming(i).wait_recv()
            return 0

        lax.fori_loop(1, CHIPS, arrived, 0)
        swap = pltpu.make_async_remote_copy(
            src_ref=near,
            dst_ref=far,
            send_sem=self.sems[2].at[0],
            recv_sem=self.sems[2].at[1],
            device_id=(self.other,),
            device_id_type=MESH,
        )
        swap.start()

        def sent(i, _):
            self.copy(i).wait_send()
            return 0

        lax.fori_loop(1, CHIPS, sent, 0)
        swap.wait()

    def row(self, r):
        _, near, far = self.refs
        mine = lax.shift_right_logical(iota((CHIPS, LANES), 1), 6) == self.core
        return jnp.where(mine, near[:, r, :], pltpu.roll(far[:, r, :], 64, 1))


def greet():
    me = lax.axis_index("dev")
    chip = me // 2
    core = me % 2
    barrier = pltpu.get_barrier_semaphore()

    def one(i, _):
        peer = ((chip + i) % CHIPS) * 2 + core
        pl.semaphore_signal(barrier, inc=1, device_id=(peer,), device_id_type=MESH)
        return 0

    lax.fori_loop(1, CHIPS, one, 0)
    pl.semaphore_signal(barrier, inc=1, device_id=(chip * 2 + (1 - core),), device_id_type=MESH)


def met():
    pl.semaphore_wait(pltpu.get_barrier_semaphore(), CHIPS)


def exchange_scratch(rows, dtype):
    box = pltpu.VMEM((CHIPS, rows, LANES), dtype)
    sem = pltpu.SemaphoreType.DMA((CHIPS,))
    return [box, box, box, sem, sem, pltpu.SemaphoreType.DMA((2,))]


def spread(gauss_ref, held, row_of):
    for i in range(ROWS):
        at = row_of(i) * 16
        held[at : at + 16, :] = gauss_ref[0:16, i * LANES : (i + 1) * LANES]
    return [held[pl.ds(r, ROWS, stride=16), :] for r in range(11)]


def splat_kernel(
    count_ref, order_ref, angle_ref, owner_ref, local_ref, cot_ref, gauss_hbm, image_ref, sum_ref,
    own_s, loc_s, carry_s, sum_s, gauss_ref, held, table, where_s, pos_s, group_s, asked_s, coef, sums,
    alpha_s, w_s, v_s, gh_s, gl_s, wh_s, wl_s, acc, low_s, load_sem, *boxes,
):
    load = pltpu.make_async_copy(gauss_hbm, gauss_ref, load_sem)
    load.start()
    greet()
    ask, reply, back = (Exchange(*boxes[6 * n : 6 * n + 6]) for n in range(3))
    wanted, picked, grad_box = boxes[0], boxes[6], boxes[12]
    near, far = boxes[13], boxes[14]

    route(owner_ref, local_ref, wanted, pos_s, group_s, own_s, loc_s, carry_s, sum_s)
    met()
    ask.send()

    first, second, third = view_of(angle_ref)
    weights = colour_weights(harmonics(*third))
    load.wait()
    params = spread(gauss_ref, held, lambda i: i)
    for r, value in enumerate(project(params, first, second)):
        table[r] = value
    for i in range(ROWS):
        lanes = slice(i * LANES, (i + 1) * LANES)
        for c, (low, high) in enumerate(COLOUR_ROWS):
            table[6 + c, i : i + 1, :] = 0.5 + jnp.sum(
                gauss_ref[low:high, lanes] * weights[c], axis=0, keepdims=True
            )

    ask.receive()
    asked_s[...] = ask.row(0)

    def answer(r, at, value):
        picked[at : at + value.shape[0], r, :] = value

    regroup(table, ROWS, asked_s[...], answer)
    reply.send()

    low_id = iota((PIX, PIX), 0)
    high_id = iota((32, PIX), 0)

    def find(i, _):
        index = jnp.concatenate([asked_s[pl.ds(2 * i, 1), :], asked_s[pl.ds(2 * i + 1, 1), :]], axis=1)
        at = pl.multiple_of(i * PIX, PIX)
        low_s[pl.ds(at, PIX), :] = jnp.where(low_id == jnp.bitwise_and(index, 255), 1.0, 0.0).astype(bf16)
        return 0

    lax.fori_loop(0, ROWS // 2, find, 0)
    acc[...] = jnp.zeros_like(acc)
    shape = (ROWS, LANES)
    tile = lax.shift_right_logical(iota(shape, 0), 2)
    slot = slot_of(jnp.bitwise_and(iota(shape, 0), 3) * LANES + iota(shape, 1))
    count = jnp.zeros(shape, i32)
    shown = jnp.zeros(shape, i32)
    for t in range(TILES):
        here = tile == t
        count = jnp.where(here, count_ref[t], count)
        shown = jnp.where(here, order_ref[t], shown)
    live = slot < count
    mid_x = (jnp.bitwise_and(shown, TX - 1) * 16 + 8).astype(f32)
    mid_y = (lax.shift_right_logical(shown, 5) * 16 + 8).astype(f32)
    reply.receive()
    for r in range(PROJ):
        table[r] = reply.row(r)

    def keep(r, at, value):
        where_s[r, at : at + value.shape[0], :] = value

    regroup(table, ROWS, pos_s[...], keep)
    mx = where_s[0] - mid_x
    my = where_s[1] - mid_y
    ca, cb, cc = where_s[2], where_s[3], where_s[4]
    where_s[0] = mx
    where_s[1] = my
    numbers = (
        LOG2E * (-0.5 * (ca * mx * mx + cc * my * my) - cb * mx * my + where_s[5]),
        LOG2E * (ca * mx + cb * my),
        LOG2E * (cc * my + cb * mx),
        (-0.5 * LOG2E) * ca,
        -LOG2E * cb,
        (-0.5 * LOG2E) * cc,
        where_s[6],
        where_s[7],
        where_s[8],
    )
    coef[...] = jnp.zeros_like(coef)
    for q, number in enumerate(numbers):
        coef[pl.ds(q, ROWS, stride=16), :] = jnp.where(live, number, -1e9 if q == 0 else 0.0)

    flat = (16, PIX)
    line = iota(flat, 0)
    ox = jnp.bitwise_and(iota(flat, 1), 15).astype(f32) - 7.5
    oy = lax.shift_right_logical(iota(flat, 1), 4).astype(f32) - 7.5
    terms = (jnp.ones(flat, f32), ox, oy, ox * ox, ox * oy, oy * oy)
    basis = jnp.zeros(flat, f32)
    for q, term in enumerate(terms):
        basis = jnp.where(line == q, term, basis)
    basis = basis.astype(bf16)
    none = jnp.zeros(flat, bf16)
    powers_rhs = jnp.concatenate([basis, basis, basis, none, none, none], axis=0)
    sub = iota((8, PIX), 0)
    contract_first = (((0,), (0,)), ((), ()))
    contract_last = (((1,), (1,)), ((), ()))

    def one_pair(p, _):
        at, hi, mid, t_hi, t_mid, lhs, cot_rhs = [], [], [], [], [], [], []
        for u in range(2):
            t = 2 * p + u
            parts = []
            for c in range(4):
                at_c = pl.multiple_of((4 * t + c) * 16, 16)
                parts.append(coef[pl.ds(at_c, 16), :])
            c_hi, c_mid, c_lo = split3(jnp.concatenate(parts, axis=1))
            at.append(pl.multiple_of(t * PIX, PIX))
            cot = jnp.zeros(flat, f32)
            for c in range(3):
                cot = jnp.where(line == 6 + c, cot_ref[c : c + 1, pl.ds(at[u], PIX)], cot)
            d_hi, d_mid, d_lo = split3(cot)
            hi.append(c_hi)
            mid.append(c_mid)
            t_hi.append(d_hi)
            t_mid.append(d_mid)
            lhs.append(jnp.concatenate([c_hi, c_mid, c_lo, c_hi, c_mid, c_hi], axis=0))
            cot_rhs.append(jnp.concatenate([d_hi, d_hi, d_hi, d_mid, d_mid, d_lo], axis=0))

        for u in range(2):
            for b in range(4):
                part = lhs[u][:, b * 128 : (b + 1) * 128]
                rows = slice(b * 128, (b + 1) * 128)
                alpha_s[u, rows] = jnp.exp2(
                    lax.dot_general(part, powers_rhs, contract_first, preferred_element_type=f32)
                )
                w_s[u, rows] = lax.dot_general(part, cot_rhs[u], contract_first, preferred_element_type=f32)

        left = [jnp.ones((8, PIX), f32)] * 2
        total = [jnp.zeros((8, PIX), f32)] * 2
        for j in range(SLOTS // 8):
            rows = slice(8 * j, 8 * j + 8)
            for u in range(2):
                v = left[u] * alpha_s[u, rows]
                v_s[u, rows] = v
                left[u] = left[u] - v
                total[u] = total[u] + v * w_s[u, rows]
        enter, behind = [], []
        for u in range(2):
            front = jnp.ones((8, PIX), f32)
            run = left[u][0:1]
            for s in range(1, 8):
                front = jnp.where(sub == s, run, front)
                run = run * left[u][s : s + 1]
            enter.append(front)
            back = jnp.zeros((8, PIX), f32)
            run = total[u][7:8]
            for s in range(6, -1, -1):
                back = jnp.where(sub == s, run, back)
                run = total[u][s : s + 1] + left[u][s : s + 1] * run
            behind.append(back)
        for i in range(SLOTS // 16 - 1, -1, -1):
            both = slice(16 * i, 16 * i + 16)
            for u in range(2):
                weights = [None] * 2
                grads = [None] * 2
                for j in (1, 0):
                    rows = slice(16 * i + 8 * j, 16 * i + 8 * j + 8)
                    gap = w_s[u, rows] - behind[u]
                    weights[j] = enter[u] * v_s[u, rows]
                    grads[j] = weights[j] * gap
                    behind[u] = behind[u] + alpha_s[u, rows] * gap
                wh_s[u, both], wl_s[u, both] = split2(jnp.concatenate(weights, axis=0))
                gh_s[u, both], gl_s[u, both] = split2(jnp.concatenate(grads, axis=0))

        def pixel_sum(a, b):
            return lax.dot_general(a, b, contract_last, preferred_element_type=f32)

        for u in range(2):
            two = pixel_sum(jnp.concatenate([t_hi[u], t_mid[u]], axis=0), wh_s[u])
            got = (
                pixel_sum(basis, gh_s[u])
                + pixel_sum(basis, gl_s[u])
                + two[:16]
                + two[16:]
                + pixel_sum(t_hi[u], wl_s[u])
            )
            for c in range(4):
                at_c = pl.multiple_of((8 * p + 4 * u + c) * 16, 16)
                sums[pl.ds(at_c, 16), :] = got[:, c * LANES : (c + 1) * LANES]
            two = jnp.dot(jnp.concatenate([hi[u], mid[u]], axis=0), wh_s[u], preferred_element_type=f32)
            image = two[:16] + two[16:] + jnp.dot(hi[u], wl_s[u], preferred_element_type=f32)
            image_ref[:, pl.ds(at[u], PIX)] = image[6:9]
        return 0

    lax.fori_loop(0, TILES // 2, one_pair, 0)

    s = [sums[pl.ds(q, ROWS, stride=16), :] for q in range(PROJ)]
    mx, my, ca, cb, cc = (where_s[r] for r in range(5))
    sx = s[1] - mx * s[0]
    sy = s[2] - my * s[0]
    grads = (
        ca * sx + cb * sy,
        cc * sy + cb * sx,
        -0.5 * (s[3] - mx * (s[1] + sx)),
        -(s[4] - mx * s[2] - my * sx),
        -0.5 * (s[5] - my * (s[2] + sy)),
        s[0],
        s[6],
        s[7],
        s[8],
    )
    for r in range(PROJ):
        table[r] = jnp.where(live, grads[r], 0.0)


    def hand(r, at, value):
        grad_box[at : at + value.shape[0], r, :] = value

    regroup(table, ROWS, group_s[...], hand)
    back.send()
    back.receive()

    mine = lax.shift_right_logical(iota((PROJ, LANES), 1), 6) == back.core

    def add(i, _):
        index = jnp.concatenate([asked_s[pl.ds(2 * i, 1), :], asked_s[pl.ds(2 * i + 1, 1), :]], axis=1)
        here = high_id == lax.shift_right_logical(index, 8)
        halves = []
        for j in range(2):
            halves.append(jnp.where(mine, near[2 * i + j], pltpu.roll(far[2 * i + j], 64, 1)))
        value = jnp.concatenate(halves, axis=1)
        hi = value.astype(bf16).astype(f32)
        lo = value - hi
        rows = []
        for r in range(PROJ):
            for part in (hi, lo):
                rows.append(jnp.where(here, part[r : r + 1], 0.0).astype(bf16))
        at = pl.multiple_of(i * PIX, PIX)
        acc[...] += lax.dot_general(
            jnp.concatenate(rows, axis=0),
            low_s[pl.ds(at, PIX), :],
            (((1,), (1,)), ((), ())),
            preferred_element_type=f32,
        )
        return 0

    lax.fori_loop(0, ROWS // 2, add, 0)
    for r in range(PROJ):
        both = acc[64 * r : 64 * r + 32, :] + acc[64 * r + 32 : 64 * r + 64, :]
        sum_ref[r] = jnp.concatenate([both[:, :LANES], both[:, LANES:]], axis=0)


def pull_kernel(angle_ref, gauss_ref, sum_ref, out_ref, held):
    first, second, third = view_of(angle_ref)
    weights = colour_weights(harmonics(*third))

    def row_of(i):
        return (i % 2) * 32 + i // 2

    params = spread(gauss_ref, held, row_of)
    _, pullback = jax.vjp(lambda *p: project(p, first, second), *params)
    grads = pullback(tuple(sum_ref[r] for r in range(6)))
    held[...] = jnp.zeros_like(held)
    for r in range(11):
        held[pl.ds(r, ROWS, stride=16), :] = grads[r]
    w0, w1, w2 = weights
    for i in range(ROWS):
        at = row_of(i)
        lanes = slice(i * LANES, (i + 1) * LANES)
        tint = [sum_ref[6 + c, at : at + 1, :] for c in range(3)]
        out_ref[0:8, lanes] = held[at * 16 : at * 16 + 8, :]
        out_ref[8:16, lanes] = held[at * 16 + 8 : at * 16 + 16, :] + w0[0:8] * tint[0]
        out_ref[16:24, lanes] = w0[8:16] * tint[0]
        out_ref[24:32, lanes] = w0[16:24] * tint[0] + w1[0:8] * tint[1]
        out_ref[32:40, lanes] = w1[8:16] * tint[1]
        out_ref[40:48, lanes] = w1[16:24] * tint[1] + w2[0:8] * tint[2]
        out_ref[48:56, lanes] = w2[8:16] * tint[2]
        out_ref[56:59, lanes] = w2[16:19] * tint[2]


VMEM = pl.BlockSpec(memory_space=pltpu.VMEM)
SMEM = pl.BlockSpec(memory_space=pltpu.SMEM)
ANY = pl.BlockSpec(memory_space=pl.ANY)


def sds(shape, dtype=f32):
    return jax.ShapeDtypeStruct(shape, dtype)


def splat(counts, order, angles, owners, locals_, cot, gaussians):
    square = pltpu.VMEM((ROWS, LANES), i32)
    pair = pltpu.VMEM((2, SLOTS, PIX), f32)
    pair_half = pltpu.VMEM((2, SLOTS, PIX), bf16)
    values = pltpu.VMEM((PROJ, ROWS, LANES), f32)
    lines = pltpu.VMEM((ROWS * 16, LANES), f32)
    return pl.pallas_call(
        splat_kernel,
        out_shape=(sds(cot.shape), sds((PROJ, ROWS, LANES))),
        in_specs=[SMEM, SMEM, SMEM, VMEM, VMEM, VMEM, ANY],
        out_specs=(VMEM, VMEM),
        scratch_shapes=[
            pltpu.VMEM((TILES, SLOTS), i32),
            pltpu.VMEM((TILES, SLOTS), i32),
            pltpu.VMEM((DEVS, 256), f32),
            pltpu.VMEM((256, LANES), f32),
            pltpu.VMEM(gaussians.shape, f32),
            lines,
            values,
            values,
            square,
            square,
            square,
            lines,
            lines,
            pair,
            pair,
            pair,
            pair_half,
            pair_half,
            pair_half,
            pair_half,
            pltpu.VMEM((64 * PROJ, PIX), f32),
            pltpu.VMEM((TILES * SLOTS, PIX), bf16),
            pltpu.SemaphoreType.DMA,
        ]
        + exchange_scratch(1, i32)
        + exchange_scratch(PROJ, f32)
        + exchange_scratch(PROJ, f32),
        compiler_params=pltpu.CompilerParams(
            collective_id=0, has_side_effects=True, vmem_limit_bytes=40 * 1024 * 1024
        ),
        name="splat",
    )(counts, order, angles, owners, locals_, cot, gaussians)


def pull(angles, gaussians, sums):
    return pl.pallas_call(
        pull_kernel,
        out_shape=sds(gaussians.shape),
        in_specs=[SMEM, VMEM, VMEM],
        out_specs=VMEM,
        scratch_shapes=[pltpu.VMEM((ROWS * 16, LANES), f32)],
        name="pull",
    )(angles, gaussians, sums)


def shards(gaussians, view_angles, tile_order, tile_owners, tile_locals, list_counts, image_cotangent):
    rendered, sums = splat(
        list_counts, tile_order, view_angles, tile_owners, tile_locals, image_cotangent, gaussians
    )
    return rendered, pull(view_angles, gaussians, sums)


def solution(mesh):
    return jax.shard_map(
        shards,
        mesh=mesh,
        in_specs=(
            P(None, "dev"),
            P(),
            P("dev"),
            P("dev", None),
            P("dev", None),
            P("dev"),
            P(None, "dev"),
        ),
        out_specs=(P(None, "dev"), P(None, "dev")),
        check_vma=False,
    )
```

```python
from functools import partial

import jax
import jax.numpy as jnp
from jax import lax
from jax.experimental import pallas as pl
from jax.experimental.pallas import tpu as pltpu
from jax.sharding import PartitionSpec as P

DEVS = 128
CHIPS = 64
TILES = 16
SLOTS = 512
ROWS = 64
LANES = 128
PROJ = 9
PIX = 256
TX = 32
FOCAL_X = 128.0
FOCAL_Y = 256.0
CENTRE_X = 256.0
CENTRE_Y = 512.0
LOG2E = 1.4426950408889634
MESH = pl.DeviceIdType.MESH
f32 = jnp.float32
bf16 = jnp.bfloat16
i32 = jnp.int32


def iota(shape, dim):
    return lax.broadcasted_iota(i32, shape, dim)


def split2(x):
    hi = x.astype(bf16)
    return hi, (x - hi.astype(f32)).astype(bf16)


def split3(x):
    hi = x.astype(bf16)
    rest = x - hi.astype(f32)
    mid = rest.astype(bf16)
    return hi, mid, (rest - mid.astype(f32)).astype(bf16)


def lane_pick(table, index):
    return jnp.take_along_axis(table, index, axis=1)


def view_of(angle_ref):
    def turn(i):
        angle = jnp.full((8, LANES), angle_ref[i], f32)
        return jnp.cos(angle)[0:1], jnp.sin(angle)[0:1]

    (ca, sa), (cb, sb), (cc, sc) = turn(0), turn(1), turn(2)
    first = (cc * cb, cc * sb * sa - sc * ca, cc * sb * ca + sc * sa)
    second = (sc * cb, sc * sb * sa + cc * ca, sc * sb * ca - cc * sa)
    third = (-sb, cb * sa, cb * ca)
    return first, second, third


def harmonics(x, y, z):
    xx, yy, zz = x * x, y * y, z * z
    return [
        0.28209479177387814 + 0.0 * x,
        -0.4886025119029199 * y,
        0.4886025119029199 * z,
        -0.4886025119029199 * x,
        1.0925484305920792 * x * y,
        -1.0925484305920792 * y * z,
        0.31539156525252005 * (2.0 * zz - xx - yy),
        -1.0925484305920792 * x * z,
        0.5462742152960396 * (xx - yy),
        -0.5900435899266435 * y * (3.0 * xx - yy),
        2.890611442640554 * x * y * z,
        -0.4570457994644658 * y * (4.0 * zz - xx - yy),
        0.3731763325901154 * z * (2.0 * zz - 3.0 * xx - 3.0 * yy),
        -0.4570457994644658 * x * (4.0 * zz - xx - yy),
        1.445305721320277 * z * (xx - yy),
        -0.5900435899266435 * x * (xx - 3.0 * yy),
    ]


COLOUR_ROWS = ((8, 32), (24, 48), (40, 59))
VIEW_ROWS = 80


def colour_weights(basis):
    out = []
    for c, (low, high) in enumerate(COLOUR_ROWS):
        row = iota((high - low, LANES), 0) + low - (11 + 16 * c)
        held = jnp.zeros((high - low, LANES), f32)
        for k in range(16):
            held = jnp.where(row == k, basis[k], held)
        out.append(held)
    return out


def project(params, first, second):
    px, py, pz, s0, s1, s2, qw, qx, qy, qz, logit = params
    mean_x = CENTRE_X + FOCAL_X * (first[0] * px + first[1] * py + first[2] * pz)
    mean_y = CENTRE_Y + FOCAL_Y * (second[0] * px + second[1] * py + second[2] * pz)
    scales = (jnp.exp(s0), jnp.exp(s1), jnp.exp(s2))
    two_n = 2.0 / jnp.maximum(qw * qw + qx * qx + qy * qy + qz * qz, 1.0)
    turned = (
        (1.0 - two_n * (qy * qy + qz * qz), two_n * (qx * qy - qw * qz), two_n * (qx * qz + qw * qy)),
        (two_n * (qx * qy + qw * qz), 1.0 - two_n * (qx * qx + qz * qz), two_n * (qy * qz - qw * qx)),
        (two_n * (qx * qz - qw * qy), two_n * (qy * qz + qw * qx), 1.0 - two_n * (qx * qx + qy * qy)),
    )
    va = []
    vb = []
    for j in range(3):
        va.append(FOCAL_X * (first[0] * turned[0][j] + first[1] * turned[1][j] + first[2] * turned[2][j]) * scales[j])
        vb.append(FOCAL_Y * (second[0] * turned[0][j] + second[1] * turned[1][j] + second[2] * turned[2][j]) * scales[j])
    cov_a = va[0] * va[0] + va[1] * va[1] + va[2] * va[2] + 0.3
    cov_b = va[0] * vb[0] + va[1] * vb[1] + va[2] * vb[2]
    cov_c = vb[0] * vb[0] + vb[1] * vb[1] + vb[2] * vb[2] + 0.3
    inv = 1.0 / (cov_a * cov_c - cov_b * cov_b)
    log_opacity = -jnp.log(1.0 + jnp.exp(-logit))
    return mean_x, mean_y, cov_c * inv, -cov_b * inv, cov_a * inv, log_opacity


def regroup(table_ref, parts_s, index_ref, store, done=None, start=0):
    for r in range(PROJ):
        even = table_ref[r, pl.ds(0, 32, stride=2), :]
        odd = table_ref[r, pl.ds(1, 32, stride=2), :]
        for n, part in enumerate(split3(jnp.concatenate([even, odd], axis=1))):
            parts_s[r * 32 : (r + 1) * 32, n * PIX : (n + 1) * PIX] = part
    high_id = iota((32, PIX), 0)
    low_id = iota((PIX, PIX), 0)

    def step(n, _):
        g = (n + start) % 4
        at = pl.multiple_of(8 * g, 8)
        flat = index_ref[pl.ds(at, 8), :]
        high = lax.shift_right_logical(flat, 7)
        low = jnp.bitwise_and(flat, 127)
        held = [jnp.zeros((8, LANES), f32)] * PROJ
        for i in range(ROWS):
            here = high == i
            for r in range(PROJ):
                row = jnp.broadcast_to(table_ref[r, i : i + 1, :], (8, LANES))
                held[r] = jnp.where(here, lane_pick(row, low), held[r])
        for r in range(PROJ):
            store(r, at, held[r])
        for q in range(4):
            line = 32 + 8 * g + 2 * q
            index = jnp.concatenate([index_ref[pl.ds(line, 1), :], index_ref[pl.ds(line + 1, 1), :]], axis=1)
            column = jnp.where(low_id == jnp.bitwise_and(index, 255), 1.0, 0.0).astype(bf16)
            here = high_id == lax.shift_right_logical(index, 8)
            got = jnp.dot(
                parts_s[...], jnp.concatenate([column] * 3, axis=0), preferred_element_type=f32
            )
            for r in range(PROJ):
                value = jnp.sum(jnp.where(here, got[r * 32 : (r + 1) * 32], 0.0), axis=0, keepdims=True)
                store(r, line, value[:, :LANES])
                store(r, line + 1, value[:, LANES:])
        if done is not None:
            done(g)
        return 0

    lax.fori_loop(0, 4, step, 0)


def slot_of(row):
    return jnp.bitwise_and(row, 7) * (SLOTS // 8) + lax.shift_right_logical(row, 3)


def route(owner_ref, local_ref, want_ref, pos_ref, group_ref, own_s, loc_s, carry_s, sum_s):
    for d in range(SLOTS // LANES):
        row = iota((TILES, LANES), 1) + d * LANES
        slot = slot_of(row)
        high = lax.shift_right_logical(slot, 7)
        low = jnp.bitwise_and(slot, 127)
        for src, dst in ((owner_ref, own_s), (local_ref, loc_s)):
            held = jnp.zeros((TILES, LANES), i32)
            for c in range(SLOTS // LANES):
                held = jnp.where(high == c, lane_pick(src[:, c * LANES : (c + 1) * LANES], low), held)
            dst[:, d * LANES : (d + 1) * LANES] = held
    half = 256
    before = jnp.where(iota((half, half), 0) < iota((half, half), 1), 1.0, 0.0).astype(bf16)
    ones = jnp.ones((half, half), bf16)
    both = jnp.concatenate([before, ones], axis=1)
    carry_s[...] = jnp.zeros_like(carry_s)
    sum_s[...] = jnp.zeros_like(sum_s)
    owner_id = iota((DEVS, half), 0)
    pair_id = iota((ROWS, half), 0)
    lane_id = iota((LANES, half), 0)

    def step(t, _):
        for h in range(2):
            owner = own_s[pl.ds(t, 1), h * half : (h + 1) * half]
            local = loc_s[pl.ds(t, 1), h * half : (h + 1) * half]
            hit = owner_id == owner
            hit_f = jnp.where(hit, 1.0, 0.0)
            counts = jnp.dot(hit_f.astype(bf16), both, preferred_element_type=f32)
            seen = carry_s[...]
            rank = jnp.sum(hit_f * (counts[:, :half] + seen), axis=0, keepdims=True).astype(i32)
            carry_s[...] = seen + counts[:, half:]
            place = owner * ROWS + rank
            pos_ref[pl.ds(4 * t + 2 * h, 1), :] = place[:, :LANES]
            pos_ref[pl.ds(4 * t + 2 * h + 1, 1), :] = place[:, LANES:]
            pair = pair_id == lax.shift_right_logical(place, 7)
            lane = jnp.where(lane_id == jnp.bitwise_and(place, 127), 1.0, 0.0).astype(bf16)
            slot = t * SLOTS + h * half + iota((1, half), 1)
            parts = []
            for number in (local, slot):
                for part in (lax.shift_right_logical(number, 7), jnp.bitwise_and(number, 127)):
                    parts.append(jnp.where(pair, part.astype(f32), 0.0).astype(bf16))
            sum_s[...] += lax.dot_general(
                jnp.concatenate(parts, axis=0), lane, (((1,), (1,)), ((), ())), preferred_element_type=f32
            )
        return 0

    lax.fori_loop(0, TILES, step, 0, unroll=4)
    total = sum_s[...].astype(i32)
    want_ref[:, 0, :] = total[0:64] * 128 + total[64:128]
    group_ref[...] = total[128:192] * 128 + total[192:256]


class Exchange:
    def __init__(self, x_ref, near, far, send_sem, recv_sem, pair_sem):
        self.refs = (x_ref, near, far)
        self.sems = (send_sem, recv_sem, pair_sem)
        me = lax.axis_index("dev")
        self.chip = me // 2
        self.core = me % 2
        self.other = self.chip * 2 + (1 - self.core)

    def copy(self, i):
        x_ref, near, _ = self.refs
        to = (self.chip + i) % CHIPS
        return pltpu.make_async_remote_copy(
            src_ref=x_ref.at[to],
            dst_ref=near.at[self.chip],
            send_sem=self.sems[0].at[i],
            recv_sem=self.sems[1].at[i],
            device_id=(to * 2 + self.core,),
            device_id_type=MESH,
        )

    def incoming(self, i):
        x_ref, near, _ = self.refs
        source = (self.chip + CHIPS - i) % CHIPS
        return pltpu.make_async_remote_copy(
            src_ref=x_ref.at[source],
            dst_ref=near.at[source],
            send_sem=self.sems[0].at[i],
            recv_sem=self.sems[1].at[i],
            device_id=(source * 2 + self.core,),
            device_id_type=MESH,
        )

    def send(self):
        def one(i, _):
            self.copy(i).start()
            return 0

        lax.fori_loop(1, CHIPS, one, 0)
        self.refs[1][self.chip] = self.refs[0][self.chip]

    def send_group(self, g):
        def one(n, _):
            to = 8 * g + n % 8 + 32 * (n // 8)
            i = (to + CHIPS - self.chip) % CHIPS

            @pl.when(i > 0)
            def _():
                self.copy(i).start()

            return 0

        lax.fori_loop(0, 16, one, 0)

    def keep_own(self):
        self.refs[1][self.chip] = self.refs[0][self.chip]

    def receive(self):
        _, near, far = self.refs

        def arrived(i, _):
            self.incoming(i).wait_recv()
            return 0

        lax.fori_loop(1, CHIPS, arrived, 0)
        swap = pltpu.make_async_remote_copy(
            src_ref=near,
            dst_ref=far,
            send_sem=self.sems[2].at[0],
            recv_sem=self.sems[2].at[1],
            device_id=(self.other,),
            device_id_type=MESH,
        )
        swap.start()

        def sent(i, _):
            self.copy(i).wait_send()
            return 0

        lax.fori_loop(1, CHIPS, sent, 0)
        swap.wait()

    def row(self, r):
        _, near, far = self.refs
        mine = lax.shift_right_logical(iota((CHIPS, LANES), 1), 6) == self.core
        return jnp.where(mine, near[:, r, :], pltpu.roll(far[:, r, :], 64, 1))


def greet():
    me = lax.axis_index("dev")
    chip = me // 2
    core = me % 2
    barrier = pltpu.get_barrier_semaphore()

    def one(i, _):
        peer = ((chip + i) % CHIPS) * 2 + core
        pl.semaphore_signal(barrier, inc=1, device_id=(peer,), device_id_type=MESH)
        return 0

    lax.fori_loop(1, CHIPS, one, 0)
    pl.semaphore_signal(barrier, inc=1, device_id=(chip * 2 + (1 - core),), device_id_type=MESH)


def met():
    pl.semaphore_wait(pltpu.get_barrier_semaphore(), CHIPS)


def exchange_scratch(rows, dtype):
    box = pltpu.VMEM((CHIPS, rows, LANES), dtype)
    sem = pltpu.SemaphoreType.DMA((CHIPS,))
    return [box, box, box, sem, sem, pltpu.SemaphoreType.DMA((2,))]


def spread(gauss_ref, held, tiles):
    for i in range(tiles):
        held[i * 16 : i * 16 + 16, :] = gauss_ref[0:16, i * LANES : (i + 1) * LANES]
    return [held[pl.ds(r, tiles, stride=16), :] for r in range(11)]


def splat_kernel(
    count_ref, order_ref, angle_ref, owner_ref, local_ref, cot_ref, gauss_hbm, image_ref, sum_ref, view_ref,
    own_s, loc_s, carry_s, sum_s, gauss_ref, held, table, where_s, pos_s, group_s, asked_s, coef, sums,
    alpha_s, w_s, v_s, gh_s, gl_s, wh_s, wl_s, acc, low_s, parts_s, load_sem, *boxes,
):
    load = pltpu.make_async_copy(gauss_hbm, gauss_ref, load_sem)
    load.start()
    greet()
    ask, reply, back = (Exchange(*boxes[6 * n : 6 * n + 6]) for n in range(3))
    wanted, picked, grad_box = boxes[0], boxes[6], boxes[12]
    near, far = boxes[13], boxes[14]

    route(owner_ref, local_ref, wanted, pos_s, group_s, own_s, loc_s, carry_s, sum_s)
    met()
    ask.send()

    first, second, third = view_of(angle_ref)
    weights = colour_weights(harmonics(*third))
    for n, entry in enumerate(first + second):
        view_ref[n : n + 1, :] = entry
    for c, (low, high) in enumerate(COLOUR_ROWS):
        view_ref[8 + 24 * c : 8 + 24 * c + high - low, :] = weights[c]
    load.wait()
    params = spread(gauss_ref, held, ROWS)
    for r, value in enumerate(project(params, first, second)):
        table[r] = value
    for i in range(ROWS):
        lanes = slice(i * LANES, (i + 1) * LANES)
        for c, (low, high) in enumerate(COLOUR_ROWS):
            table[6 + c, i : i + 1, :] = 0.5 + jnp.sum(
                gauss_ref[low:high, lanes] * weights[c], axis=0, keepdims=True
            )

    ask.receive()
    asked_s[...] = ask.row(0)

    def answer(r, at, value):
        picked[pl.ds(at, value.shape[0]), r, :] = value

    turn = ask.chip // 8
    regroup(table, parts_s, asked_s, answer, reply.send_group, turn)
    reply.keep_own()

    low_id = iota((PIX, PIX), 0)
    high_id = iota((32, PIX), 0)

    def find(i, _):
        index = jnp.concatenate([asked_s[pl.ds(2 * i, 1), :], asked_s[pl.ds(2 * i + 1, 1), :]], axis=1)
        at = pl.multiple_of(i * PIX, PIX)
        low_s[pl.ds(at, PIX), :] = jnp.where(low_id == jnp.bitwise_and(index, 255), 1.0, 0.0).astype(bf16)
        return 0

    lax.fori_loop(0, ROWS // 2, find, 0)
    acc[...] = jnp.zeros_like(acc)
    shape = (ROWS, LANES)
    tile = lax.shift_right_logical(iota(shape, 0), 2)
    slot = slot_of(jnp.bitwise_and(iota(shape, 0), 3) * LANES + iota(shape, 1))
    count = jnp.zeros(shape, i32)
    shown = jnp.zeros(shape, i32)
    for t in range(TILES):
        here = tile == t
        count = jnp.where(here, count_ref[t], count)
        shown = jnp.where(here, order_ref[t], shown)
    live = slot < count
    mid_x = (jnp.bitwise_and(shown, TX - 1) * 16 + 8).astype(f32)
    mid_y = (lax.shift_right_logical(shown, 5) * 16 + 8).astype(f32)
    reply.receive()
    for r in range(PROJ):
        table[r] = reply.row(r)

    def keep(r, at, value):
        where_s[r, pl.ds(at, value.shape[0]), :] = value

    regroup(table, parts_s, pos_s, keep)
    mx = where_s[0] - mid_x
    my = where_s[1] - mid_y
    ca, cb, cc = where_s[2], where_s[3], where_s[4]
    where_s[0] = mx
    where_s[1] = my
    numbers = (
        LOG2E * (-0.5 * (ca * mx * mx + cc * my * my) - cb * mx * my + where_s[5]),
        LOG2E * (ca * mx + cb * my),
        LOG2E * (cc * my + cb * mx),
        (-0.5 * LOG2E) * ca,
        -LOG2E * cb,
        (-0.5 * LOG2E) * cc,
        where_s[6],
        where_s[7],
        where_s[8],
    )
    coef[...] = jnp.zeros_like(coef)
    for q, number in enumerate(numbers):
        coef[pl.ds(q, ROWS, stride=16), :] = jnp.where(live, number, -1e9 if q == 0 else 0.0)

    flat = (16, PIX)
    line = iota(flat, 0)
    ox = jnp.bitwise_and(iota(flat, 1), 15).astype(f32) - 7.5
    oy = lax.shift_right_logical(iota(flat, 1), 4).astype(f32) - 7.5
    terms = (jnp.ones(flat, f32), ox, oy, ox * ox, ox * oy, oy * oy)
    basis = jnp.zeros(flat, f32)
    for q, term in enumerate(terms):
        basis = jnp.where(line == q, term, basis)
    basis = basis.astype(bf16)
    none = jnp.zeros(flat, bf16)
    powers_rhs = jnp.concatenate([basis, basis, basis, none, none, none], axis=0)
    sub = iota((8, PIX), 0)
    contract_first = (((0,), (0,)), ((), ()))
    contract_last = (((1,), (1,)), ((), ()))

    def one_pair(p, _):
        at, hi, mid, t_hi, t_mid, lhs, cot_rhs = [], [], [], [], [], [], []
        for u in range(2):
            t = 2 * p + u
            parts = []
            for c in range(4):
                at_c = pl.multiple_of((4 * t + c) * 16, 16)
                parts.append(coef[pl.ds(at_c, 16), :])
            c_hi, c_mid, c_lo = split3(jnp.concatenate(parts, axis=1))
            at.append(pl.multiple_of(t * PIX, PIX))
            cot = jnp.zeros(flat, f32)
            for c in range(3):
                cot = jnp.where(line == 6 + c, cot_ref[c : c + 1, pl.ds(at[u], PIX)], cot)
            d_hi, d_mid, d_lo = split3(cot)
            hi.append(c_hi)
            mid.append(c_mid)
            t_hi.append(d_hi)
            t_mid.append(d_mid)
            lhs.append(jnp.concatenate([c_hi, c_mid, c_lo, c_hi, c_mid, c_hi], axis=0))
            cot_rhs.append(jnp.concatenate([d_hi, d_hi, d_hi, d_mid, d_mid, d_lo], axis=0))

        for u in range(2):
            for b in range(4):
                part = lhs[u][:, b * 128 : (b + 1) * 128]
                rows = slice(b * 128, (b + 1) * 128)
                alpha_s[u, rows] = jnp.exp2(
                    lax.dot_general(part, powers_rhs, contract_first, preferred_element_type=f32)
                )
                w_s[u, rows] = lax.dot_general(part, cot_rhs[u], contract_first, preferred_element_type=f32)

        left = [jnp.ones((8, PIX), f32)] * 2
        total = [jnp.zeros((8, PIX), f32)] * 2
        for j in range(SLOTS // 8):
            rows = slice(8 * j, 8 * j + 8)
            for u in range(2):
                v = left[u] * alpha_s[u, rows]
                v_s[u, rows] = v
                left[u] = left[u] - v
                total[u] = total[u] + v * w_s[u, rows]
        enter, behind = [], []
        for u in range(2):
            front = jnp.ones((8, PIX), f32)
            run = left[u][0:1]
            for s in range(1, 8):
                front = jnp.where(sub == s, run, front)
                run = run * left[u][s : s + 1]
            enter.append(front)
            back = jnp.zeros((8, PIX), f32)
            run = total[u][7:8]
            for s in range(6, -1, -1):
                back = jnp.where(sub == s, run, back)
                run = total[u][s : s + 1] + left[u][s : s + 1] * run
            behind.append(back)
        for i in range(SLOTS // 16 - 1, -1, -1):
            both = slice(16 * i, 16 * i + 16)
            for u in range(2):
                weights = [None] * 2
                grads = [None] * 2
                for j in (1, 0):
                    rows = slice(16 * i + 8 * j, 16 * i + 8 * j + 8)
                    gap = w_s[u, rows] - behind[u]
                    weights[j] = enter[u] * v_s[u, rows]
                    grads[j] = weights[j] * gap
                    behind[u] = behind[u] + alpha_s[u, rows] * gap
                wh_s[u, both], wl_s[u, both] = split2(jnp.concatenate(weights, axis=0))
                gh_s[u, both], gl_s[u, both] = split2(jnp.concatenate(grads, axis=0))

        def pixel_sum(a, b):
            return lax.dot_general(a, b, contract_last, preferred_element_type=f32)

        for u in range(2):
            two = pixel_sum(jnp.concatenate([t_hi[u], t_mid[u]], axis=0), wh_s[u])
            got = (
                pixel_sum(basis, gh_s[u])
                + pixel_sum(basis, gl_s[u])
                + two[:16]
                + two[16:]
                + pixel_sum(t_hi[u], wl_s[u])
            )
            for c in range(4):
                at_c = pl.multiple_of((8 * p + 4 * u + c) * 16, 16)
                sums[pl.ds(at_c, 16), :] = got[:, c * LANES : (c + 1) * LANES]
            two = jnp.dot(jnp.concatenate([hi[u], mid[u]], axis=0), wh_s[u], preferred_element_type=f32)
            image = two[:16] + two[16:] + jnp.dot(hi[u], wl_s[u], preferred_element_type=f32)
            image_ref[:, pl.ds(at[u], PIX)] = image[6:9]
        return 0

    lax.fori_loop(0, TILES // 2, one_pair, 0)

    s = [sums[pl.ds(q, ROWS, stride=16), :] for q in range(PROJ)]
    mx, my, ca, cb, cc = (where_s[r] for r in range(5))
    sx = s[1] - mx * s[0]
    sy = s[2] - my * s[0]
    grads = (
        ca * sx + cb * sy,
        cc * sy + cb * sx,
        -0.5 * (s[3] - mx * (s[1] + sx)),
        -(s[4] - mx * s[2] - my * sx),
        -0.5 * (s[5] - my * (s[2] + sy)),
        s[0],
        s[6],
        s[7],
        s[8],
    )
    for r in range(PROJ):
        table[r] = jnp.where(live, grads[r], 0.0)


    def hand(r, at, value):
        grad_box[pl.ds(at, value.shape[0]), r, :] = value

    regroup(table, parts_s, group_s, hand, back.send_group, turn)
    back.keep_own()
    back.receive()

    mine = lax.shift_right_logical(iota((PROJ, LANES), 1), 6) == back.core

    def add(i, _):
        index = jnp.concatenate([asked_s[pl.ds(2 * i, 1), :], asked_s[pl.ds(2 * i + 1, 1), :]], axis=1)
        here = high_id == lax.shift_right_logical(index, 8)
        halves = []
        for j in range(2):
            halves.append(jnp.where(mine, near[2 * i + j], pltpu.roll(far[2 * i + j], 64, 1)))
        value = jnp.concatenate(halves, axis=1)
        hi = value.astype(bf16).astype(f32)
        lo = value - hi
        rows = []
        for r in range(PROJ):
            for part in (hi, lo):
                rows.append(jnp.where(here, part[r : r + 1], 0.0).astype(bf16))
        at = pl.multiple_of(i * PIX, PIX)
        acc[...] += lax.dot_general(
            jnp.concatenate(rows, axis=0),
            low_s[pl.ds(at, PIX), :],
            (((1,), (1,)), ((), ())),
            preferred_element_type=f32,
        )
        return 0

    lax.fori_loop(0, ROWS // 2, add, 0, unroll=4)
    for r in range(PROJ):
        both = acc[64 * r : 64 * r + 32, :] + acc[64 * r + 32 : 64 * r + 64, :]
        sum_ref[r, pl.ds(0, 32, stride=2), :] = both[:, :LANES]
        sum_ref[r, pl.ds(1, 32, stride=2), :] = both[:, LANES:]


def pull_kernel(view_ref, gauss_ref, sum_ref, out_ref, held):
    tiles = sum_ref.shape[1]
    first = tuple(view_ref[n : n + 1, :] for n in range(3))
    second = tuple(view_ref[n : n + 1, :] for n in range(3, 6))
    w0, w1, w2 = (view_ref[8 + 24 * c : 8 + 24 * c + high - low, :] for c, (low, high) in enumerate(COLOUR_ROWS))
    params = spread(gauss_ref, held, tiles)
    _, pullback = jax.vjp(lambda *p: project(p, first, second), *params)
    grads = pullback(tuple(sum_ref[r] for r in range(6)))
    held[...] = jnp.zeros_like(held)
    for r in range(11):
        held[pl.ds(r, tiles, stride=16), :] = grads[r]
    for i in range(tiles):
        lanes = slice(i * LANES, (i + 1) * LANES)
        tint = [sum_ref[6 + c, i : i + 1, :] for c in range(3)]
        out_ref[0:8, lanes] = held[i * 16 : i * 16 + 8, :]
        out_ref[8:16, lanes] = held[i * 16 + 8 : i * 16 + 16, :] + w0[0:8] * tint[0]
        out_ref[16:24, lanes] = w0[8:16] * tint[0]
        out_ref[24:32, lanes] = w0[16:24] * tint[0] + w1[0:8] * tint[1]
        out_ref[32:40, lanes] = w1[8:16] * tint[1]
        out_ref[40:48, lanes] = w1[16:24] * tint[1] + w2[0:8] * tint[2]
        out_ref[48:56, lanes] = w2[8:16] * tint[2]
        out_ref[56:59, lanes] = w2[16:19] * tint[2]


VMEM = pl.BlockSpec(memory_space=pltpu.VMEM)
SMEM = pl.BlockSpec(memory_space=pltpu.SMEM)
ANY = pl.BlockSpec(memory_space=pl.ANY)


def sds(shape, dtype=f32):
    return jax.ShapeDtypeStruct(shape, dtype)


def splat(counts, order, angles, owners, locals_, cot, gaussians):
    square = pltpu.VMEM((ROWS, LANES), i32)
    pair = pltpu.VMEM((2, SLOTS, PIX), f32)
    pair_half = pltpu.VMEM((2, SLOTS, PIX), bf16)
    values = pltpu.VMEM((PROJ, ROWS, LANES), f32)
    lines = pltpu.VMEM((ROWS * 16, LANES), f32)
    return pl.pallas_call(
        splat_kernel,
        out_shape=(sds(cot.shape), sds((PROJ, ROWS, LANES)), sds((VIEW_ROWS, LANES))),
        in_specs=[SMEM, SMEM, SMEM, VMEM, VMEM, VMEM, ANY],
        out_specs=(VMEM, VMEM, VMEM),
        scratch_shapes=[
            pltpu.VMEM((TILES, SLOTS), i32),
            pltpu.VMEM((TILES, SLOTS), i32),
            pltpu.VMEM((DEVS, 256), f32),
            pltpu.VMEM((256, LANES), f32),
            pltpu.VMEM(gaussians.shape, f32),
            lines,
            values,
            values,
            square,
            square,
            square,
            lines,
            lines,
            pair,
            pair,
            pair,
            pair_half,
            pair_half,
            pair_half,
            pair_half,
            pltpu.VMEM((64 * PROJ, PIX), f32),
            pltpu.VMEM((TILES * SLOTS, PIX), bf16),
            pltpu.VMEM((32 * PROJ, 3 * PIX), bf16),
            pltpu.SemaphoreType.DMA,
        ]
        + exchange_scratch(1, i32)
        + exchange_scratch(PROJ, f32)
        + exchange_scratch(PROJ, f32),
        compiler_params=pltpu.CompilerParams(
            collective_id=0, has_side_effects=True, vmem_limit_bytes=60 * 1024 * 1024
        ),
        name="splat",
    )(counts, order, angles, owners, locals_, cot, gaussians)


def pull(view, gaussians, sums, steps=4):
    tiles = ROWS // steps
    slab = pl.BlockSpec((gaussians.shape[0], tiles * LANES), lambda i: (0, i))
    return pl.pallas_call(
        pull_kernel,
        grid=(steps,),
        out_shape=sds(gaussians.shape),
        in_specs=[
            pl.BlockSpec((VIEW_ROWS, LANES), lambda i: (0, 0)),
            slab,
            pl.BlockSpec((PROJ, tiles, LANES), lambda i: (0, i, 0)),
        ],
        out_specs=slab,
        scratch_shapes=[pltpu.VMEM((tiles * 16, LANES), f32)],
        name="pull",
    )(view, gaussians, sums)


def shards(gaussians, view_angles, tile_order, tile_owners, tile_locals, list_counts, image_cotangent):
    rendered, sums, view = splat(
        list_counts, tile_order, view_angles, tile_owners, tile_locals, image_cotangent, gaussians
    )
    return rendered, pull(view, gaussians, sums)


def solution(mesh):
    return jax.shard_map(
        shards,
        mesh=mesh,
        in_specs=(
            P(None, "dev"),
            P(),
            P("dev"),
            P("dev", None),
            P("dev", None),
            P("dev"),
            P(None, "dev"),
        ),
        out_specs=(P(None, "dev"), P(None, "dev")),
        check_vma=False,
    )
```

```python
from functools import partial

import jax
import jax.numpy as jnp
from jax import lax
from jax.experimental import pallas as pl
from jax.experimental.pallas import tpu as pltpu
from jax.sharding import PartitionSpec as P

DEVS = 128
CHIPS = 64
TILES = 16
SLOTS = 512
ROWS = 64
LANES = 128
PROJ = 9
PIX = 256
TX = 32
FOCAL_X = 128.0
FOCAL_Y = 256.0
CENTRE_X = 256.0
CENTRE_Y = 512.0
LOG2E = 1.4426950408889634
MESH = pl.DeviceIdType.MESH
f32 = jnp.float32
bf16 = jnp.bfloat16
i32 = jnp.int32


def iota(shape, dim):
    return lax.broadcasted_iota(i32, shape, dim)


def split2(x):
    hi = x.astype(bf16)
    return hi, (x - hi.astype(f32)).astype(bf16)


def split3(x):
    hi = x.astype(bf16)
    rest = x - hi.astype(f32)
    mid = rest.astype(bf16)
    return hi, mid, (rest - mid.astype(f32)).astype(bf16)


def lane_pick(table, index):
    return jnp.take_along_axis(table, index, axis=1)


def view_of(angle_ref):
    def turn(i):
        angle = jnp.full((8, LANES), angle_ref[i], f32)
        return jnp.cos(angle)[0:1], jnp.sin(angle)[0:1]

    (ca, sa), (cb, sb), (cc, sc) = turn(0), turn(1), turn(2)
    first = (cc * cb, cc * sb * sa - sc * ca, cc * sb * ca + sc * sa)
    second = (sc * cb, sc * sb * sa + cc * ca, sc * sb * ca - cc * sa)
    third = (-sb, cb * sa, cb * ca)
    return first, second, third


def harmonics(x, y, z):
    xx, yy, zz = x * x, y * y, z * z
    return [
        0.28209479177387814 + 0.0 * x,
        -0.4886025119029199 * y,
        0.4886025119029199 * z,
        -0.4886025119029199 * x,
        1.0925484305920792 * x * y,
        -1.0925484305920792 * y * z,
        0.31539156525252005 * (2.0 * zz - xx - yy),
        -1.0925484305920792 * x * z,
        0.5462742152960396 * (xx - yy),
        -0.5900435899266435 * y * (3.0 * xx - yy),
        2.890611442640554 * x * y * z,
        -0.4570457994644658 * y * (4.0 * zz - xx - yy),
        0.3731763325901154 * z * (2.0 * zz - 3.0 * xx - 3.0 * yy),
        -0.4570457994644658 * x * (4.0 * zz - xx - yy),
        1.445305721320277 * z * (xx - yy),
        -0.5900435899266435 * x * (xx - 3.0 * yy),
    ]


COLOUR_ROWS = ((8, 32), (24, 48), (40, 59))
VIEW_ROWS = 80


def colour_weights(basis):
    out = []
    for c, (low, high) in enumerate(COLOUR_ROWS):
        row = iota((high - low, LANES), 0) + low - (11 + 16 * c)
        held = jnp.zeros((high - low, LANES), f32)
        for k in range(16):
            held = jnp.where(row == k, basis[k], held)
        out.append(held)
    return out


def project(params, first, second):
    px, py, pz, s0, s1, s2, qw, qx, qy, qz, logit = params
    mean_x = CENTRE_X + FOCAL_X * (first[0] * px + first[1] * py + first[2] * pz)
    mean_y = CENTRE_Y + FOCAL_Y * (second[0] * px + second[1] * py + second[2] * pz)
    scales = (jnp.exp(s0), jnp.exp(s1), jnp.exp(s2))
    two_n = 2.0 / jnp.maximum(qw * qw + qx * qx + qy * qy + qz * qz, 1.0)
    turned = (
        (1.0 - two_n * (qy * qy + qz * qz), two_n * (qx * qy - qw * qz), two_n * (qx * qz + qw * qy)),
        (two_n * (qx * qy + qw * qz), 1.0 - two_n * (qx * qx + qz * qz), two_n * (qy * qz - qw * qx)),
        (two_n * (qx * qz - qw * qy), two_n * (qy * qz + qw * qx), 1.0 - two_n * (qx * qx + qy * qy)),
    )
    va = []
    vb = []
    for j in range(3):
        va.append(FOCAL_X * (first[0] * turned[0][j] + first[1] * turned[1][j] + first[2] * turned[2][j]) * scales[j])
        vb.append(FOCAL_Y * (second[0] * turned[0][j] + second[1] * turned[1][j] + second[2] * turned[2][j]) * scales[j])
    cov_a = va[0] * va[0] + va[1] * va[1] + va[2] * va[2] + 0.3
    cov_b = va[0] * vb[0] + va[1] * vb[1] + va[2] * vb[2]
    cov_c = vb[0] * vb[0] + vb[1] * vb[1] + vb[2] * vb[2] + 0.3
    inv = 1.0 / (cov_a * cov_c - cov_b * cov_b)
    log_opacity = -jnp.log(1.0 + jnp.exp(-logit))
    return mean_x, mean_y, cov_c * inv, -cov_b * inv, cov_a * inv, log_opacity


def plane(y, n):
    return (y + 2 + 3 * n + 3 * (n // 2) + 2 * (n // 3)) % 4


def regroup(table_ref, parts_s, index_ref, store, done=None, y=0):
    for r in range(PROJ):
        even = table_ref[r, pl.ds(0, 32, stride=2), :]
        odd = table_ref[r, pl.ds(1, 32, stride=2), :]
        for n, part in enumerate(split3(jnp.concatenate([even, odd], axis=1))):
            parts_s[r * 32 : (r + 1) * 32, n * PIX : (n + 1) * PIX] = part
    high_id = iota((32, PIX), 0)
    low_id = iota((PIX, PIX), 0)

    def step(n, _):
        g = plane(y, n)
        at = pl.multiple_of(16 * g, 8)
        flat = index_ref[pl.ds(at, 8), :]
        high = lax.shift_right_logical(flat, 7)
        low = jnp.bitwise_and(flat, 127)
        held = [jnp.zeros((8, LANES), f32)] * PROJ
        for i in range(ROWS):
            here = high == i
            for r in range(PROJ):
                row = jnp.broadcast_to(table_ref[r, i : i + 1, :], (8, LANES))
                held[r] = jnp.where(here, lane_pick(row, low), held[r])
        for r in range(PROJ):
            store(r, at, held[r])
        for q in range(4):
            line = 16 * g + 8 + 2 * q
            index = jnp.concatenate([index_ref[pl.ds(line, 1), :], index_ref[pl.ds(line + 1, 1), :]], axis=1)
            column = jnp.where(low_id == jnp.bitwise_and(index, 255), 1.0, 0.0).astype(bf16)
            here = high_id == lax.shift_right_logical(index, 8)
            got = jnp.dot(
                parts_s[...], jnp.concatenate([column] * 3, axis=0), preferred_element_type=f32
            )
            for r in range(PROJ):
                value = jnp.sum(jnp.where(here, got[r * 32 : (r + 1) * 32], 0.0), axis=0, keepdims=True)
                store(r, line, value[:, :LANES])
                store(r, line + 1, value[:, LANES:])
        if done is not None:
            done(g)
        return 0

    lax.fori_loop(0, 4, step, 0)


def slot_of(row):
    return jnp.bitwise_and(row, 7) * (SLOTS // 8) + lax.shift_right_logical(row, 3)


def route(owner_ref, local_ref, want_ref, pos_ref, group_ref, own_s, loc_s, carry_s, sum_s):
    for d in range(SLOTS // LANES):
        row = iota((TILES, LANES), 1) + d * LANES
        slot = slot_of(row)
        high = lax.shift_right_logical(slot, 7)
        low = jnp.bitwise_and(slot, 127)
        for src, dst in ((owner_ref, own_s), (local_ref, loc_s)):
            held = jnp.zeros((TILES, LANES), i32)
            for c in range(SLOTS // LANES):
                held = jnp.where(high == c, lane_pick(src[:, c * LANES : (c + 1) * LANES], low), held)
            dst[:, d * LANES : (d + 1) * LANES] = held
    half = 256
    before = jnp.where(iota((half, half), 0) < iota((half, half), 1), 1.0, 0.0).astype(bf16)
    ones = jnp.ones((half, half), bf16)
    both = jnp.concatenate([before, ones], axis=1)
    carry_s[...] = jnp.zeros_like(carry_s)
    sum_s[...] = jnp.zeros_like(sum_s)
    owner_id = iota((DEVS, half), 0)
    pair_id = iota((ROWS, half), 0)
    lane_id = iota((LANES, half), 0)

    def step(t, _):
        for h in range(2):
            owner = own_s[pl.ds(t, 1), h * half : (h + 1) * half]
            local = loc_s[pl.ds(t, 1), h * half : (h + 1) * half]
            hit = owner_id == owner
            hit_f = jnp.where(hit, 1.0, 0.0)
            counts = jnp.dot(hit_f.astype(bf16), both, preferred_element_type=f32)
            seen = carry_s[...]
            rank = jnp.sum(hit_f * (counts[:, :half] + seen), axis=0, keepdims=True).astype(i32)
            carry_s[...] = seen + counts[:, half:]
            place = owner * ROWS + rank
            pos_ref[pl.ds(4 * t + 2 * h, 1), :] = place[:, :LANES]
            pos_ref[pl.ds(4 * t + 2 * h + 1, 1), :] = place[:, LANES:]
            pair = pair_id == lax.shift_right_logical(place, 7)
            lane = jnp.where(lane_id == jnp.bitwise_and(place, 127), 1.0, 0.0).astype(bf16)
            slot = t * SLOTS + h * half + iota((1, half), 1)
            parts = []
            for number in (local, slot):
                for part in (lax.shift_right_logical(number, 7), jnp.bitwise_and(number, 127)):
                    parts.append(jnp.where(pair, part.astype(f32), 0.0).astype(bf16))
            sum_s[...] += lax.dot_general(
                jnp.concatenate(parts, axis=0), lane, (((1,), (1,)), ((), ())), preferred_element_type=f32
            )
        return 0

    lax.fori_loop(0, TILES, step, 0, unroll=4)
    total = sum_s[...].astype(i32)
    want_ref[:, 0, :] = total[0:64] * 128 + total[64:128]
    group_ref[...] = total[128:192] * 128 + total[192:256]


class Exchange:
    def __init__(self, x_ref, near, far, send_sem, recv_sem, pair_sem):
        self.refs = (x_ref, near, far)
        self.sems = (send_sem, recv_sem, pair_sem)
        me = lax.axis_index("dev")
        self.chip = me // 2
        self.core = me % 2
        self.y = self.chip // 16
        self.other = self.chip * 2 + (1 - self.core)

    def copy(self, to):
        x_ref, near, _ = self.refs
        return pltpu.make_async_remote_copy(
            src_ref=x_ref.at[to],
            dst_ref=near.at[self.chip],
            send_sem=self.sems[0].at[0],
            recv_sem=self.sems[1].at[self.y],
            device_id=(to * 2 + self.core,),
            device_id_type=MESH,
        )

    def many(self, row, count, g):
        x_ref, near, _ = self.refs
        return pltpu.make_async_remote_copy(
            src_ref=x_ref.at[pl.ds(row, count)],
            dst_ref=near.at[pl.ds(row, count)],
            send_sem=self.sems[0].at[0],
            recv_sem=self.sems[1].at[g],
            device_id=(self.other,),
            device_id_type=MESH,
        )

    def send_group(self, g):
        def one(n, _):
            to = 16 * g + (self.chip + n) % 16

            @pl.when(to != self.chip)
            def _():
                self.copy(to).start()

            return 0

        lax.fori_loop(0, 16, one, 0, unroll=4)

    def keep_own(self):
        self.refs[1][self.chip] = self.refs[0][self.chip]

    def send(self):
        for n in range(4):
            self.send_group(plane(self.y, n))
        self.keep_own()

    def wait_group(self, n):
        g = plane(self.y, n)
        self.many(16 * g, 16 if n < 3 else 15, g).wait_recv()

    def swap(self, n):
        _, near, far = self.refs
        rows = pl.ds(16 * plane(self.y, n), 16)
        return pltpu.make_async_remote_copy(
            src_ref=near.at[rows],
            dst_ref=far.at[rows],
            send_sem=self.sems[2].at[n],
            recv_sem=self.sems[2].at[4 + n],
            device_id=(self.other,),
            device_id_type=MESH,
        )

    def receive(self, work):
        for n in range(4):
            self.wait_group(n)
            self.swap(n).start()
            if n > 0:
                self.swap(n - 1).wait()
                work(plane(self.y, n - 1))

        self.many(0, CHIPS - 1, 0).wait_send()
        self.swap(3).wait()
        work(plane(self.y, 3))

    def rows(self, g, r):
        _, near, far = self.refs
        at = pl.ds(16 * g, 16)
        mine = lax.shift_right_logical(iota((16, LANES), 1), 6) == self.core
        return jnp.where(mine, near[at, r, :], pltpu.roll(far[at, r, :], 64, 1))


def greet():
    me = lax.axis_index("dev")
    chip = me // 2
    core = me % 2
    barrier = pltpu.get_barrier_semaphore()

    def one(i, _):
        peer = ((chip + i) % CHIPS) * 2 + core
        pl.semaphore_signal(barrier, inc=1, device_id=(peer,), device_id_type=MESH)
        return 0

    lax.fori_loop(1, CHIPS, one, 0)
    pl.semaphore_signal(barrier, inc=1, device_id=(chip * 2 + (1 - core),), device_id_type=MESH)


def met():
    pl.semaphore_wait(pltpu.get_barrier_semaphore(), CHIPS)


def exchange_scratch(rows, dtype):
    box = pltpu.VMEM((CHIPS, rows, LANES), dtype)
    sem = pltpu.SemaphoreType.DMA
    return [box, box, box, sem((1,)), sem((4,)), sem((8,))]


def spread(gauss_ref, held, tiles):
    for i in range(tiles):
        held[i * 16 : i * 16 + 16, :] = gauss_ref[0:16, i * LANES : (i + 1) * LANES]
    return [held[pl.ds(r, tiles, stride=16), :] for r in range(11)]


def splat_kernel(
    count_ref, order_ref, angle_ref, owner_ref, local_ref, cot_ref, gauss_hbm, image_ref, sum_ref, view_ref,
    own_s, loc_s, carry_s, sum_s, gauss_ref, held, table, where_s, pos_s, group_s, asked_s, coef, sums,
    alpha_s, w_s, v_s, gh_s, gl_s, wh_s, wl_s, acc, low_s, parts_s, load_sem, *boxes,
):
    load = pltpu.make_async_copy(gauss_hbm, gauss_ref, load_sem)
    load.start()
    greet()
    ask, reply, back = (Exchange(*boxes[6 * n : 6 * n + 6]) for n in range(3))
    wanted, picked, grad_box = boxes[0], boxes[6], boxes[12]
    near, far = boxes[13], boxes[14]

    route(owner_ref, local_ref, wanted, pos_s, group_s, own_s, loc_s, carry_s, sum_s)
    met()
    ask.send()

    first, second, third = view_of(angle_ref)
    weights = colour_weights(harmonics(*third))
    for n, entry in enumerate(first + second):
        view_ref[n : n + 1, :] = entry
    for c, (low, high) in enumerate(COLOUR_ROWS):
        view_ref[8 + 24 * c : 8 + 24 * c + high - low, :] = weights[c]
    load.wait()
    params = spread(gauss_ref, held, ROWS)
    for r, value in enumerate(project(params, first, second)):
        table[r] = value
    for i in range(ROWS):
        lanes = slice(i * LANES, (i + 1) * LANES)
        for c, (low, high) in enumerate(COLOUR_ROWS):
            table[6 + c, i : i + 1, :] = 0.5 + jnp.sum(
                gauss_ref[low:high, lanes] * weights[c], axis=0, keepdims=True
            )

    def note(g):
        asked_s[pl.ds(pl.multiple_of(16 * g, 16), 16), :] = ask.rows(g, 0)

    ask.receive(note)

    def answer(r, at, value):
        picked[pl.ds(at, value.shape[0]), r, :] = value

    regroup(table, parts_s, asked_s, answer, reply.send_group, reply.y)
    reply.keep_own()

    low_id = iota((PIX, PIX), 0)
    high_id = iota((32, PIX), 0)

    def find(i, _):
        index = jnp.concatenate([asked_s[pl.ds(2 * i, 1), :], asked_s[pl.ds(2 * i + 1, 1), :]], axis=1)
        at = pl.multiple_of(i * PIX, PIX)
        low_s[pl.ds(at, PIX), :] = jnp.where(low_id == jnp.bitwise_and(index, 255), 1.0, 0.0).astype(bf16)
        return 0

    lax.fori_loop(0, ROWS // 2, find, 0)
    acc[...] = jnp.zeros_like(acc)
    shape = (ROWS, LANES)
    tile = lax.shift_right_logical(iota(shape, 0), 2)
    slot = slot_of(jnp.bitwise_and(iota(shape, 0), 3) * LANES + iota(shape, 1))
    count = jnp.zeros(shape, i32)
    shown = jnp.zeros(shape, i32)
    for t in range(TILES):
        here = tile == t
        count = jnp.where(here, count_ref[t], count)
        shown = jnp.where(here, order_ref[t], shown)
    live = slot < count
    mid_x = (jnp.bitwise_and(shown, TX - 1) * 16 + 8).astype(f32)
    mid_y = (lax.shift_right_logical(shown, 5) * 16 + 8).astype(f32)

    def collect(g):
        for r in range(PROJ):
            table[r, pl.ds(pl.multiple_of(16 * g, 16), 16), :] = reply.rows(g, r)

    reply.receive(collect)

    def keep(r, at, value):
        where_s[r, pl.ds(at, value.shape[0]), :] = value

    regroup(table, parts_s, pos_s, keep)
    mx = where_s[0] - mid_x
    my = where_s[1] - mid_y
    ca, cb, cc = where_s[2], where_s[3], where_s[4]
    where_s[0] = mx
    where_s[1] = my
    numbers = (
        LOG2E * (-0.5 * (ca * mx * mx + cc * my * my) - cb * mx * my + where_s[5]),
        LOG2E * (ca * mx + cb * my),
        LOG2E * (cc * my + cb * mx),
        (-0.5 * LOG2E) * ca,
        -LOG2E * cb,
        (-0.5 * LOG2E) * cc,
        where_s[6],
        where_s[7],
        where_s[8],
    )
    coef[...] = jnp.zeros_like(coef)
    for q, number in enumerate(numbers):
        coef[pl.ds(q, ROWS, stride=16), :] = jnp.where(live, number, -1e9 if q == 0 else 0.0)

    flat = (16, PIX)
    line = iota(flat, 0)
    ox = jnp.bitwise_and(iota(flat, 1), 15).astype(f32) - 7.5
    oy = lax.shift_right_logical(iota(flat, 1), 4).astype(f32) - 7.5
    terms = (jnp.ones(flat, f32), ox, oy, ox * ox, ox * oy, oy * oy)
    basis = jnp.zeros(flat, f32)
    for q, term in enumerate(terms):
        basis = jnp.where(line == q, term, basis)
    basis = basis.astype(bf16)
    none = jnp.zeros(flat, bf16)
    powers_rhs = jnp.concatenate([basis, basis, basis, none, none, none], axis=0)
    sub = iota((8, PIX), 0)
    contract_first = (((0,), (0,)), ((), ()))
    contract_last = (((1,), (1,)), ((), ()))

    def one_pair(p, _):
        at, hi, mid, t_hi, t_mid, lhs, cot_rhs = [], [], [], [], [], [], []
        for u in range(2):
            t = 2 * p + u
            parts = []
            for c in range(4):
                at_c = pl.multiple_of((4 * t + c) * 16, 16)
                parts.append(coef[pl.ds(at_c, 16), :])
            c_hi, c_mid, c_lo = split3(jnp.concatenate(parts, axis=1))
            at.append(pl.multiple_of(t * PIX, PIX))
            cot = jnp.zeros(flat, f32)
            for c in range(3):
                cot = jnp.where(line == 6 + c, cot_ref[c : c + 1, pl.ds(at[u], PIX)], cot)
            d_hi, d_mid, d_lo = split3(cot)
            hi.append(c_hi)
            mid.append(c_mid)
            t_hi.append(d_hi)
            t_mid.append(d_mid)
            lhs.append(jnp.concatenate([c_hi, c_mid, c_lo, c_hi, c_mid, c_hi], axis=0))
            cot_rhs.append(jnp.concatenate([d_hi, d_hi, d_hi, d_mid, d_mid, d_lo], axis=0))

        for u in range(2):
            for b in range(4):
                part = lhs[u][:, b * 128 : (b + 1) * 128]
                rows = slice(b * 128, (b + 1) * 128)
                alpha_s[u, rows] = jnp.exp2(
                    lax.dot_general(part, powers_rhs, contract_first, preferred_element_type=f32)
                )
                w_s[u, rows] = lax.dot_general(part, cot_rhs[u], contract_first, preferred_element_type=f32)

        left = [jnp.ones((8, PIX), f32)] * 2
        total = [jnp.zeros((8, PIX), f32)] * 2
        for j in range(SLOTS // 8):
            rows = slice(8 * j, 8 * j + 8)
            for u in range(2):
                v = left[u] * alpha_s[u, rows]
                v_s[u, rows] = v
                left[u] = left[u] - v
                total[u] = total[u] + v * w_s[u, rows]
        enter, behind = [], []
        for u in range(2):
            front = jnp.ones((8, PIX), f32)
            run = left[u][0:1]
            for s in range(1, 8):
                front = jnp.where(sub == s, run, front)
                run = run * left[u][s : s + 1]
            enter.append(front)
            back = jnp.zeros((8, PIX), f32)
            run = total[u][7:8]
            for s in range(6, -1, -1):
                back = jnp.where(sub == s, run, back)
                run = total[u][s : s + 1] + left[u][s : s + 1] * run
            behind.append(back)
        for i in range(SLOTS // 16 - 1, -1, -1):
            both = slice(16 * i, 16 * i + 16)
            for u in range(2):
                weights = [None] * 2
                grads = [None] * 2
                for j in (1, 0):
                    rows = slice(16 * i + 8 * j, 16 * i + 8 * j + 8)
                    gap = w_s[u, rows] - behind[u]
                    weights[j] = enter[u] * v_s[u, rows]
                    grads[j] = weights[j] * gap
                    behind[u] = behind[u] + alpha_s[u, rows] * gap
                wh_s[u, both], wl_s[u, both] = split2(jnp.concatenate(weights, axis=0))
                gh_s[u, both], gl_s[u, both] = split2(jnp.concatenate(grads, axis=0))

        def pixel_sum(a, b):
            return lax.dot_general(a, b, contract_last, preferred_element_type=f32)

        for u in range(2):
            two = pixel_sum(jnp.concatenate([t_hi[u], t_mid[u]], axis=0), wh_s[u])
            got = (
                pixel_sum(basis, gh_s[u])
                + pixel_sum(basis, gl_s[u])
                + two[:16]
                + two[16:]
                + pixel_sum(t_hi[u], wl_s[u])
            )
            for c in range(4):
                at_c = pl.multiple_of((8 * p + 4 * u + c) * 16, 16)
                sums[pl.ds(at_c, 16), :] = got[:, c * LANES : (c + 1) * LANES]
            two = jnp.dot(jnp.concatenate([hi[u], mid[u]], axis=0), wh_s[u], preferred_element_type=f32)
            image = two[:16] + two[16:] + jnp.dot(hi[u], wl_s[u], preferred_element_type=f32)
            image_ref[:, pl.ds(at[u], PIX)] = image[6:9]
        return 0

    lax.fori_loop(0, TILES // 2, one_pair, 0)

    s = [sums[pl.ds(q, ROWS, stride=16), :] for q in range(PROJ)]
    mx, my, ca, cb, cc = (where_s[r] for r in range(5))
    sx = s[1] - mx * s[0]
    sy = s[2] - my * s[0]
    grads = (
        ca * sx + cb * sy,
        cc * sy + cb * sx,
        -0.5 * (s[3] - mx * (s[1] + sx)),
        -(s[4] - mx * s[2] - my * sx),
        -0.5 * (s[5] - my * (s[2] + sy)),
        s[0],
        s[6],
        s[7],
        s[8],
    )
    for r in range(PROJ):
        table[r] = jnp.where(live, grads[r], 0.0)


    def hand(r, at, value):
        grad_box[pl.ds(at, value.shape[0]), r, :] = value

    regroup(table, parts_s, group_s, hand, back.send_group, back.y)
    back.keep_own()

    mine = lax.shift_right_logical(iota((PROJ, LANES), 1), 6) == back.core

    def add(i, _):
        index = jnp.concatenate([asked_s[pl.ds(2 * i, 1), :], asked_s[pl.ds(2 * i + 1, 1), :]], axis=1)
        here = high_id == lax.shift_right_logical(index, 8)
        halves = []
        for j in range(2):
            halves.append(jnp.where(mine, near[2 * i + j], pltpu.roll(far[2 * i + j], 64, 1)))
        value = jnp.concatenate(halves, axis=1)
        hi = value.astype(bf16).astype(f32)
        lo = value - hi
        rows = []
        for r in range(PROJ):
            for part in (hi, lo):
                rows.append(jnp.where(here, part[r : r + 1], 0.0).astype(bf16))
        at = pl.multiple_of(i * PIX, PIX)
        acc[...] += lax.dot_general(
            jnp.concatenate(rows, axis=0),
            low_s[pl.ds(at, PIX), :],
            (((1,), (1,)), ((), ())),
            preferred_element_type=f32,
        )
        return 0

    def add_plane(g):
        lax.fori_loop(0, 8, lambda n, _: add(8 * g + n, 0), 0, unroll=4)

    back.receive(add_plane)
    for r in range(PROJ):
        both = acc[64 * r : 64 * r + 32, :] + acc[64 * r + 32 : 64 * r + 64, :]
        sum_ref[r, pl.ds(0, 32, stride=2), :] = both[:, :LANES]
        sum_ref[r, pl.ds(1, 32, stride=2), :] = both[:, LANES:]


def pull_kernel(view_ref, gauss_ref, sum_ref, out_ref, held):
    tiles = sum_ref.shape[1]
    first = tuple(view_ref[n : n + 1, :] for n in range(3))
    second = tuple(view_ref[n : n + 1, :] for n in range(3, 6))
    w0, w1, w2 = (view_ref[8 + 24 * c : 8 + 24 * c + high - low, :] for c, (low, high) in enumerate(COLOUR_ROWS))
    params = spread(gauss_ref, held, tiles)
    _, pullback = jax.vjp(lambda *p: project(p, first, second), *params)
    grads = pullback(tuple(sum_ref[r] for r in range(6)))
    held[...] = jnp.zeros_like(held)
    for r in range(11):
        held[pl.ds(r, tiles, stride=16), :] = grads[r]
    for i in range(tiles):
        lanes = slice(i * LANES, (i + 1) * LANES)
        tint = [sum_ref[6 + c, i : i + 1, :] for c in range(3)]
        out_ref[0:8, lanes] = held[i * 16 : i * 16 + 8, :]
        out_ref[8:16, lanes] = held[i * 16 + 8 : i * 16 + 16, :] + w0[0:8] * tint[0]
        out_ref[16:24, lanes] = w0[8:16] * tint[0]
        out_ref[24:32, lanes] = w0[16:24] * tint[0] + w1[0:8] * tint[1]
        out_ref[32:40, lanes] = w1[8:16] * tint[1]
        out_ref[40:48, lanes] = w1[16:24] * tint[1] + w2[0:8] * tint[2]
        out_ref[48:56, lanes] = w2[8:16] * tint[2]
        out_ref[56:59, lanes] = w2[16:19] * tint[2]


VMEM = pl.BlockSpec(memory_space=pltpu.VMEM)
SMEM = pl.BlockSpec(memory_space=pltpu.SMEM)
ANY = pl.BlockSpec(memory_space=pl.ANY)


def sds(shape, dtype=f32):
    return jax.ShapeDtypeStruct(shape, dtype)


def splat(counts, order, angles, owners, locals_, cot, gaussians):
    square = pltpu.VMEM((ROWS, LANES), i32)
    pair = pltpu.VMEM((2, SLOTS, PIX), f32)
    pair_half = pltpu.VMEM((2, SLOTS, PIX), bf16)
    values = pltpu.VMEM((PROJ, ROWS, LANES), f32)
    lines = pltpu.VMEM((ROWS * 16, LANES), f32)
    return pl.pallas_call(
        splat_kernel,
        out_shape=(sds(cot.shape), sds((PROJ, ROWS, LANES)), sds((VIEW_ROWS, LANES))),
        in_specs=[SMEM, SMEM, SMEM, VMEM, VMEM, VMEM, ANY],
        out_specs=(VMEM, VMEM, VMEM),
        scratch_shapes=[
            pltpu.VMEM((TILES, SLOTS), i32),
            pltpu.VMEM((TILES, SLOTS), i32),
            pltpu.VMEM((DEVS, 256), f32),
            pltpu.VMEM((256, LANES), f32),
            pltpu.VMEM(gaussians.shape, f32),
            lines,
            values,
            values,
            square,
            square,
            square,
            lines,
            lines,
            pair,
            pair,
            pair,
            pair_half,
            pair_half,
            pair_half,
            pair_half,
            pltpu.VMEM((64 * PROJ, PIX), f32),
            pltpu.VMEM((TILES * SLOTS, PIX), bf16),
            pltpu.VMEM((32 * PROJ, 3 * PIX), bf16),
            pltpu.SemaphoreType.DMA,
        ]
        + exchange_scratch(1, i32)
        + exchange_scratch(PROJ, f32)
        + exchange_scratch(PROJ, f32),
        compiler_params=pltpu.CompilerParams(
            collective_id=0, has_side_effects=True, vmem_limit_bytes=60 * 1024 * 1024
        ),
        name="splat",
    )(counts, order, angles, owners, locals_, cot, gaussians)


def pull(view, gaussians, sums, steps=2):
    tiles = ROWS // steps
    slab = pl.BlockSpec((gaussians.shape[0], tiles * LANES), lambda i: (0, i))
    return pl.pallas_call(
        pull_kernel,
        grid=(steps,),
        out_shape=sds(gaussians.shape),
        in_specs=[
            pl.BlockSpec((VIEW_ROWS, LANES), lambda i: (0, 0)),
            slab,
            pl.BlockSpec((PROJ, tiles, LANES), lambda i: (0, i, 0)),
        ],
        out_specs=slab,
        scratch_shapes=[pltpu.VMEM((tiles * 16, LANES), f32)],
        name="pull",
    )(view, gaussians, sums)


def shards(gaussians, view_angles, tile_order, tile_owners, tile_locals, list_counts, image_cotangent):
    rendered, sums, view = splat(
        list_counts, tile_order, view_angles, tile_owners, tile_locals, image_cotangent, gaussians
    )
    return rendered, pull(view, gaussians, sums)


def solution(mesh):
    return jax.shard_map(
        shards,
        mesh=mesh,
        in_specs=(
            P(None, "dev"),
            P(),
            P("dev"),
            P("dev", None),
            P("dev", None),
            P("dev"),
            P(None, "dev"),
        ),
        out_specs=(P(None, "dev"), P(None, "dev")),
        check_vma=False,
    )
```

```python
from functools import partial

import jax
import jax.numpy as jnp
from jax import lax
from jax.experimental import pallas as pl
from jax.experimental.pallas import tpu as pltpu
from jax.sharding import PartitionSpec as P

DEVS = 128
CHIPS = 64
TILES = 16
SLOTS = 512
ROWS = 64
LANES = 128
PROJ = 9
PIX = 256
TX = 32
FOCAL_X = 128.0
FOCAL_Y = 256.0
CENTRE_X = 256.0
CENTRE_Y = 512.0
LOG2E = 1.4426950408889634
MESH = pl.DeviceIdType.MESH
f32 = jnp.float32
bf16 = jnp.bfloat16
i32 = jnp.int32


def iota(shape, dim):
    return lax.broadcasted_iota(i32, shape, dim)


def split2(x):
    hi = x.astype(bf16)
    return hi, (x - hi.astype(f32)).astype(bf16)


def split3(x):
    hi = x.astype(bf16)
    rest = x - hi.astype(f32)
    mid = rest.astype(bf16)
    return hi, mid, (rest - mid.astype(f32)).astype(bf16)


def lane_pick(table, index):
    return jnp.take_along_axis(table, index, axis=1)


def view_of(angle_ref):
    def turn(i):
        angle = jnp.full((8, LANES), angle_ref[i], f32)
        return jnp.cos(angle)[0:1], jnp.sin(angle)[0:1]

    (ca, sa), (cb, sb), (cc, sc) = turn(0), turn(1), turn(2)
    first = (cc * cb, cc * sb * sa - sc * ca, cc * sb * ca + sc * sa)
    second = (sc * cb, sc * sb * sa + cc * ca, sc * sb * ca - cc * sa)
    third = (-sb, cb * sa, cb * ca)
    return first, second, third


def harmonics(x, y, z):
    xx, yy, zz = x * x, y * y, z * z
    return [
        0.28209479177387814 + 0.0 * x,
        -0.4886025119029199 * y,
        0.4886025119029199 * z,
        -0.4886025119029199 * x,
        1.0925484305920792 * x * y,
        -1.0925484305920792 * y * z,
        0.31539156525252005 * (2.0 * zz - xx - yy),
        -1.0925484305920792 * x * z,
        0.5462742152960396 * (xx - yy),
        -0.5900435899266435 * y * (3.0 * xx - yy),
        2.890611442640554 * x * y * z,
        -0.4570457994644658 * y * (4.0 * zz - xx - yy),
        0.3731763325901154 * z * (2.0 * zz - 3.0 * xx - 3.0 * yy),
        -0.4570457994644658 * x * (4.0 * zz - xx - yy),
        1.445305721320277 * z * (xx - yy),
        -0.5900435899266435 * x * (xx - 3.0 * yy),
    ]


COLOUR_ROWS = ((8, 32), (24, 48), (40, 59))
VIEW_ROWS = 80


def colour_weights(basis):
    out = []
    for c, (low, high) in enumerate(COLOUR_ROWS):
        row = iota((high - low, LANES), 0) + low - (11 + 16 * c)
        held = jnp.zeros((high - low, LANES), f32)
        for k in range(16):
            held = jnp.where(row == k, basis[k], held)
        out.append(held)
    return out


def project(params, first, second):
    px, py, pz, s0, s1, s2, qw, qx, qy, qz, logit = params
    mean_x = CENTRE_X + FOCAL_X * (first[0] * px + first[1] * py + first[2] * pz)
    mean_y = CENTRE_Y + FOCAL_Y * (second[0] * px + second[1] * py + second[2] * pz)
    scales = (jnp.exp(s0), jnp.exp(s1), jnp.exp(s2))
    two_n = 2.0 / jnp.maximum(qw * qw + qx * qx + qy * qy + qz * qz, 1.0)
    turned = (
        (1.0 - two_n * (qy * qy + qz * qz), two_n * (qx * qy - qw * qz), two_n * (qx * qz + qw * qy)),
        (two_n * (qx * qy + qw * qz), 1.0 - two_n * (qx * qx + qz * qz), two_n * (qy * qz - qw * qx)),
        (two_n * (qx * qz - qw * qy), two_n * (qy * qz + qw * qx), 1.0 - two_n * (qx * qx + qy * qy)),
    )
    va = []
    vb = []
    for j in range(3):
        va.append(FOCAL_X * (first[0] * turned[0][j] + first[1] * turned[1][j] + first[2] * turned[2][j]) * scales[j])
        vb.append(FOCAL_Y * (second[0] * turned[0][j] + second[1] * turned[1][j] + second[2] * turned[2][j]) * scales[j])
    cov_a = va[0] * va[0] + va[1] * va[1] + va[2] * va[2] + 0.3
    cov_b = va[0] * vb[0] + va[1] * vb[1] + va[2] * vb[2]
    cov_c = vb[0] * vb[0] + vb[1] * vb[1] + vb[2] * vb[2] + 0.3
    inv = 1.0 / (cov_a * cov_c - cov_b * cov_b)
    log_opacity = -jnp.log(1.0 + jnp.exp(-logit))
    return mean_x, mean_y, cov_c * inv, -cov_b * inv, cov_a * inv, log_opacity


def plane(y, n):
    return (y + 2 + 3 * n + 3 * (n // 2) + 2 * (n // 3)) % 4


def regroup(table_ref, parts_s, index_ref, store, done=None, y=0):
    for r in range(PROJ):
        even = table_ref[r, pl.ds(0, 32, stride=2), :]
        odd = table_ref[r, pl.ds(1, 32, stride=2), :]
        for n, part in enumerate(split3(jnp.concatenate([even, odd], axis=1))):
            parts_s[r * 32 : (r + 1) * 32, n * PIX : (n + 1) * PIX] = part
    high_id = iota((32, PIX), 0)
    low_id = iota((PIX, PIX), 0)

    def step(n, _):
        g = plane(y, n)
        at = pl.multiple_of(16 * g, 8)
        flat = index_ref[pl.ds(at, 8), :]
        high = lax.shift_right_logical(flat, 7)
        low = jnp.bitwise_and(flat, 127)
        held = [jnp.zeros((8, LANES), f32)] * PROJ
        for i in range(ROWS):
            here = high == i
            for r in range(PROJ):
                row = jnp.broadcast_to(table_ref[r, i : i + 1, :], (8, LANES))
                held[r] = jnp.where(here, lane_pick(row, low), held[r])
        for r in range(PROJ):
            store(r, at, held[r])
        for q in range(4):
            line = 16 * g + 8 + 2 * q
            index = jnp.concatenate([index_ref[pl.ds(line, 1), :], index_ref[pl.ds(line + 1, 1), :]], axis=1)
            column = jnp.where(low_id == jnp.bitwise_and(index, 255), 1.0, 0.0).astype(bf16)
            here = high_id == lax.shift_right_logical(index, 8)
            got = jnp.dot(
                parts_s[...], jnp.concatenate([column] * 3, axis=0), preferred_element_type=f32
            )
            for r in range(PROJ):
                value = jnp.sum(jnp.where(here, got[r * 32 : (r + 1) * 32], 0.0), axis=0, keepdims=True)
                store(r, line, value[:, :LANES])
                store(r, line + 1, value[:, LANES:])
        if done is not None:
            done(g)
        return 0

    lax.fori_loop(0, 4, step, 0)


def slot_of(row):
    return jnp.bitwise_and(row, 7) * (SLOTS // 8) + lax.shift_right_logical(row, 3)


def route(owner_ref, local_ref, want_ref, pos_ref, group_ref, own_s, loc_s, carry_s, sum_s):
    for d in range(SLOTS // LANES):
        row = iota((TILES, LANES), 1) + d * LANES
        slot = slot_of(row)
        high = lax.shift_right_logical(slot, 7)
        low = jnp.bitwise_and(slot, 127)
        for src, dst in ((owner_ref, own_s), (local_ref, loc_s)):
            held = jnp.zeros((TILES, LANES), i32)
            for c in range(SLOTS // LANES):
                held = jnp.where(high == c, lane_pick(src[:, c * LANES : (c + 1) * LANES], low), held)
            dst[:, d * LANES : (d + 1) * LANES] = held
    half = 256
    before = jnp.where(iota((half, half), 0) < iota((half, half), 1), 1.0, 0.0).astype(bf16)
    ones = jnp.ones((half, half), bf16)
    both = jnp.concatenate([before, ones], axis=1)
    carry_s[...] = jnp.zeros_like(carry_s)
    sum_s[...] = jnp.zeros_like(sum_s)
    owner_id = iota((DEVS, half), 0)
    pair_id = iota((ROWS, half), 0)
    lane_id = iota((LANES, half), 0)

    def step(t, _):
        for h in range(2):
            owner = own_s[pl.ds(t, 1), h * half : (h + 1) * half]
            local = loc_s[pl.ds(t, 1), h * half : (h + 1) * half]
            hit = owner_id == owner
            hit_f = jnp.where(hit, 1.0, 0.0)
            counts = jnp.dot(hit_f.astype(bf16), both, preferred_element_type=f32)
            seen = carry_s[...]
            rank = jnp.sum(hit_f * (counts[:, :half] + seen), axis=0, keepdims=True).astype(i32)
            carry_s[...] = seen + counts[:, half:]
            place = owner * ROWS + rank
            pos_ref[pl.ds(4 * t + 2 * h, 1), :] = place[:, :LANES]
            pos_ref[pl.ds(4 * t + 2 * h + 1, 1), :] = place[:, LANES:]
            pair = pair_id == lax.shift_right_logical(place, 7)
            lane = jnp.where(lane_id == jnp.bitwise_and(place, 127), 1.0, 0.0).astype(bf16)
            slot = t * SLOTS + h * half + iota((1, half), 1)
            parts = []
            for number in (local, slot):
                for part in (lax.shift_right_logical(number, 7), jnp.bitwise_and(number, 127)):
                    parts.append(jnp.where(pair, part.astype(f32), 0.0).astype(bf16))
            sum_s[...] += lax.dot_general(
                jnp.concatenate(parts, axis=0), lane, (((1,), (1,)), ((), ())), preferred_element_type=f32
            )
        return 0

    lax.fori_loop(0, TILES, step, 0, unroll=4)
    total = sum_s[...].astype(i32)
    want_ref[:, 0, :] = total[0:64] * 128 + total[64:128]
    group_ref[...] = total[128:192] * 128 + total[192:256]


class Exchange:
    def __init__(self, x_ref, near, far, send_sem, recv_sem, pair_sem):
        self.refs = (x_ref, near, far)
        self.sems = (send_sem, recv_sem, pair_sem)
        me = lax.axis_index("dev")
        self.chip = me // 2
        self.core = me % 2
        self.y = self.chip // 16
        self.other = self.chip * 2 + (1 - self.core)

    def copy(self, to):
        x_ref, near, _ = self.refs
        return pltpu.make_async_remote_copy(
            src_ref=x_ref.at[to],
            dst_ref=near.at[self.chip],
            send_sem=self.sems[0].at[0],
            recv_sem=self.sems[1].at[self.y],
            device_id=(to * 2 + self.core,),
            device_id_type=MESH,
        )

    def many(self, row, count, g):
        x_ref, near, _ = self.refs
        return pltpu.make_async_remote_copy(
            src_ref=x_ref.at[pl.ds(row, count)],
            dst_ref=near.at[pl.ds(row, count)],
            send_sem=self.sems[0].at[0],
            recv_sem=self.sems[1].at[g],
            device_id=(self.other,),
            device_id_type=MESH,
        )

    def send_group(self, g):
        def one(n, _):
            to = 16 * g + (self.chip + n) % 16

            @pl.when(to != self.chip)
            def _():
                self.copy(to).start()

            return 0

        lax.fori_loop(0, 16, one, 0, unroll=4)

    def keep_own(self):
        self.refs[1][self.chip] = self.refs[0][self.chip]

    def send(self):
        for n in range(4):
            self.send_group(plane(self.y, n))
        self.keep_own()

    def wait_group(self, n):
        g = plane(self.y, n)
        self.many(16 * g, 16 if n < 3 else 15, g).wait_recv()

    def swap(self, n):
        _, near, far = self.refs
        rows = pl.ds(16 * plane(self.y, n), 16)
        return pltpu.make_async_remote_copy(
            src_ref=near.at[rows],
            dst_ref=far.at[rows],
            send_sem=self.sems[2].at[n],
            recv_sem=self.sems[2].at[4 + n],
            device_id=(self.other,),
            device_id_type=MESH,
        )

    def receive(self, work):
        for n in range(4):
            self.wait_group(n)
            self.swap(n).start()
            if n > 0:
                self.swap(n - 1).wait()
                work(plane(self.y, n - 1))

        self.many(0, CHIPS - 1, 0).wait_send()
        self.swap(3).wait()
        work(plane(self.y, 3))

    def rows(self, g, r):
        _, near, far = self.refs
        at = pl.ds(16 * g, 16)
        mine = lax.shift_right_logical(iota((16, LANES), 1), 6) == self.core
        return jnp.where(mine, near[at, r, :], pltpu.roll(far[at, r, :], 64, 1))


def greet():
    me = lax.axis_index("dev")
    chip = me // 2
    core = me % 2
    barrier = pltpu.get_barrier_semaphore()

    def one(i, _):
        peer = ((chip + i) % CHIPS) * 2 + core
        pl.semaphore_signal(barrier, inc=1, device_id=(peer,), device_id_type=MESH)
        return 0

    lax.fori_loop(1, CHIPS, one, 0)
    pl.semaphore_signal(barrier, inc=1, device_id=(chip * 2 + (1 - core),), device_id_type=MESH)


def met():
    pl.semaphore_wait(pltpu.get_barrier_semaphore(), CHIPS)


def exchange_scratch(rows, dtype):
    box = pltpu.VMEM((CHIPS, rows, LANES), dtype)
    sem = pltpu.SemaphoreType.DMA
    return [box, box, box, sem((1,)), sem((4,)), sem((8,))]


def spread(gauss_ref, held, tiles):
    for i in range(tiles):
        held[i * 16 : i * 16 + 16, :] = gauss_ref[0:16, i * LANES : (i + 1) * LANES]
    return [held[pl.ds(r, tiles, stride=16), :] for r in range(11)]


def splat_kernel(
    count_ref, order_ref, angle_ref, owner_hbm, local_hbm, cot_hbm, gauss_hbm, image_ref, sum_ref, view_ref,
    own_s, loc_s, carry_s, sum_s, gauss_ref, held, table, where_s, pos_s, group_s, asked_s, coef, sums,
    alpha_s, w_s, v_s, gh_s, gl_s, wh_s, wl_s, acc, low_s, parts_s, owner_ref, local_ref, cot_ref, load_sem, *boxes,
):
    loads = [
        pltpu.make_async_copy(src, dst, load_sem.at[n])
        for n, (src, dst) in enumerate(
            ((owner_hbm, owner_ref), (local_hbm, local_ref), (gauss_hbm, gauss_ref), (cot_hbm, cot_ref))
        )
    ]
    for load in loads:
        load.start()
    greet()
    ask, reply, back = (Exchange(*boxes[6 * n : 6 * n + 6]) for n in range(3))
    wanted, picked, grad_box = boxes[0], boxes[6], boxes[12]
    near, far = boxes[13], boxes[14]

    loads[0].wait()
    loads[1].wait()
    route(owner_ref, local_ref, wanted, pos_s, group_s, own_s, loc_s, carry_s, sum_s)
    met()
    ask.send()

    first, second, third = view_of(angle_ref)
    weights = colour_weights(harmonics(*third))
    for n, entry in enumerate(first + second):
        view_ref[n : n + 1, :] = entry
    for c, (low, high) in enumerate(COLOUR_ROWS):
        view_ref[8 + 24 * c : 8 + 24 * c + high - low, :] = weights[c]
    loads[2].wait()
    loads[3].wait()
    params = spread(gauss_ref, held, ROWS)
    for r, value in enumerate(project(params, first, second)):
        table[r] = value
    for i in range(ROWS):
        lanes = slice(i * LANES, (i + 1) * LANES)
        for c, (low, high) in enumerate(COLOUR_ROWS):
            table[6 + c, i : i + 1, :] = 0.5 + jnp.sum(
                gauss_ref[low:high, lanes] * weights[c], axis=0, keepdims=True
            )

    def note(g):
        asked_s[pl.ds(pl.multiple_of(16 * g, 16), 16), :] = ask.rows(g, 0)

    ask.receive(note)

    def answer(r, at, value):
        picked[pl.ds(at, value.shape[0]), r, :] = value

    regroup(table, parts_s, asked_s, answer, reply.send_group, reply.y)
    reply.keep_own()

    low_id = iota((PIX, PIX), 0)
    high_id = iota((32, PIX), 0)

    def find(i, _):
        index = jnp.concatenate([asked_s[pl.ds(2 * i, 1), :], asked_s[pl.ds(2 * i + 1, 1), :]], axis=1)
        at = pl.multiple_of(i * PIX, PIX)
        low_s[pl.ds(at, PIX), :] = jnp.where(low_id == jnp.bitwise_and(index, 255), 1.0, 0.0).astype(bf16)
        return 0

    lax.fori_loop(0, ROWS // 2, find, 0)
    acc[...] = jnp.zeros_like(acc)
    shape = (ROWS, LANES)
    tile = lax.shift_right_logical(iota(shape, 0), 2)
    slot = slot_of(jnp.bitwise_and(iota(shape, 0), 3) * LANES + iota(shape, 1))
    count = jnp.zeros(shape, i32)
    shown = jnp.zeros(shape, i32)
    for t in range(TILES):
        here = tile == t
        count = jnp.where(here, count_ref[t], count)
        shown = jnp.where(here, order_ref[t], shown)
    live = slot < count
    mid_x = (jnp.bitwise_and(shown, TX - 1) * 16 + 8).astype(f32)
    mid_y = (lax.shift_right_logical(shown, 5) * 16 + 8).astype(f32)

    def collect(g):
        for r in range(PROJ):
            table[r, pl.ds(pl.multiple_of(16 * g, 16), 16), :] = reply.rows(g, r)

    reply.receive(collect)

    def keep(r, at, value):
        where_s[r, pl.ds(at, value.shape[0]), :] = value

    regroup(table, parts_s, pos_s, keep)
    mx = where_s[0] - mid_x
    my = where_s[1] - mid_y
    ca, cb, cc = where_s[2], where_s[3], where_s[4]
    where_s[0] = mx
    where_s[1] = my
    numbers = (
        LOG2E * (-0.5 * (ca * mx * mx + cc * my * my) - cb * mx * my + where_s[5]),
        LOG2E * (ca * mx + cb * my),
        LOG2E * (cc * my + cb * mx),
        (-0.5 * LOG2E) * ca,
        -LOG2E * cb,
        (-0.5 * LOG2E) * cc,
        where_s[6],
        where_s[7],
        where_s[8],
    )
    coef[...] = jnp.zeros_like(coef)
    for q, number in enumerate(numbers):
        coef[pl.ds(q, ROWS, stride=16), :] = jnp.where(live, number, -1e9 if q == 0 else 0.0)

    flat = (16, PIX)
    line = iota(flat, 0)
    ox = jnp.bitwise_and(iota(flat, 1), 15).astype(f32) - 7.5
    oy = lax.shift_right_logical(iota(flat, 1), 4).astype(f32) - 7.5
    terms = (jnp.ones(flat, f32), ox, oy, ox * ox, ox * oy, oy * oy)
    basis = jnp.zeros(flat, f32)
    for q, term in enumerate(terms):
        basis = jnp.where(line == q, term, basis)
    basis = basis.astype(bf16)
    none = jnp.zeros(flat, bf16)
    powers_rhs = jnp.concatenate([basis, basis, basis, none, none, none], axis=0)
    sub = iota((8, PIX), 0)
    contract_first = (((0,), (0,)), ((), ()))
    contract_last = (((1,), (1,)), ((), ()))

    def one_pair(p, _):
        at, hi, mid, t_hi, t_mid, lhs, cot_rhs = [], [], [], [], [], [], []
        for u in range(2):
            t = 2 * p + u
            parts = []
            for c in range(4):
                at_c = pl.multiple_of((4 * t + c) * 16, 16)
                parts.append(coef[pl.ds(at_c, 16), :])
            c_hi, c_mid, c_lo = split3(jnp.concatenate(parts, axis=1))
            at.append(pl.multiple_of(t * PIX, PIX))
            cot = jnp.zeros(flat, f32)
            for c in range(3):
                cot = jnp.where(line == 6 + c, cot_ref[c : c + 1, pl.ds(at[u], PIX)], cot)
            d_hi, d_mid, d_lo = split3(cot)
            hi.append(c_hi)
            mid.append(c_mid)
            t_hi.append(d_hi)
            t_mid.append(d_mid)
            lhs.append(jnp.concatenate([c_hi, c_mid, c_lo, c_hi, c_mid, c_hi], axis=0))
            cot_rhs.append(jnp.concatenate([d_hi, d_hi, d_hi, d_mid, d_mid, d_lo], axis=0))

        for u in range(2):
            for b in range(4):
                part = lhs[u][:, b * 128 : (b + 1) * 128]
                rows = slice(b * 128, (b + 1) * 128)
                alpha_s[u, rows] = jnp.exp2(
                    lax.dot_general(part, powers_rhs, contract_first, preferred_element_type=f32)
                )
                w_s[u, rows] = lax.dot_general(part, cot_rhs[u], contract_first, preferred_element_type=f32)

        left = [jnp.ones((8, PIX), f32)] * 2
        total = [jnp.zeros((8, PIX), f32)] * 2
        for j in range(SLOTS // 8):
            rows = slice(8 * j, 8 * j + 8)
            for u in range(2):
                v = left[u] * alpha_s[u, rows]
                v_s[u, rows] = v
                left[u] = left[u] - v
                total[u] = total[u] + v * w_s[u, rows]
        enter, behind = [], []
        for u in range(2):
            front = jnp.ones((8, PIX), f32)
            run = left[u][0:1]
            for s in range(1, 8):
                front = jnp.where(sub == s, run, front)
                run = run * left[u][s : s + 1]
            enter.append(front)
            back = jnp.zeros((8, PIX), f32)
            run = total[u][7:8]
            for s in range(6, -1, -1):
                back = jnp.where(sub == s, run, back)
                run = total[u][s : s + 1] + left[u][s : s + 1] * run
            behind.append(back)
        for i in range(SLOTS // 16 - 1, -1, -1):
            both = slice(16 * i, 16 * i + 16)
            for u in range(2):
                weights = [None] * 2
                grads = [None] * 2
                for j in (1, 0):
                    rows = slice(16 * i + 8 * j, 16 * i + 8 * j + 8)
                    gap = w_s[u, rows] - behind[u]
                    weights[j] = enter[u] * v_s[u, rows]
                    grads[j] = weights[j] * gap
                    behind[u] = behind[u] + alpha_s[u, rows] * gap
                wh_s[u, both], wl_s[u, both] = split2(jnp.concatenate(weights, axis=0))
                gh_s[u, both], gl_s[u, both] = split2(jnp.concatenate(grads, axis=0))

        def pixel_sum(a, b):
            return lax.dot_general(a, b, contract_last, preferred_element_type=f32)

        for u in range(2):
            two = pixel_sum(jnp.concatenate([t_hi[u], t_mid[u]], axis=0), wh_s[u])
            got = (
                pixel_sum(basis, gh_s[u])
                + pixel_sum(basis, gl_s[u])
                + two[:16]
                + two[16:]
                + pixel_sum(t_hi[u], wl_s[u])
            )
            for c in range(4):
                at_c = pl.multiple_of((8 * p + 4 * u + c) * 16, 16)
                sums[pl.ds(at_c, 16), :] = got[:, c * LANES : (c + 1) * LANES]
            two = jnp.dot(jnp.concatenate([hi[u], mid[u]], axis=0), wh_s[u], preferred_element_type=f32)
            image = two[:16] + two[16:] + jnp.dot(hi[u], wl_s[u], preferred_element_type=f32)
            image_ref[:, pl.ds(at[u], PIX)] = image[6:9]
        return 0

    lax.fori_loop(0, TILES // 2, one_pair, 0)

    s = [sums[pl.ds(q, ROWS, stride=16), :] for q in range(PROJ)]
    mx, my, ca, cb, cc = (where_s[r] for r in range(5))
    sx = s[1] - mx * s[0]
    sy = s[2] - my * s[0]
    grads = (
        ca * sx + cb * sy,
        cc * sy + cb * sx,
        -0.5 * (s[3] - mx * (s[1] + sx)),
        -(s[4] - mx * s[2] - my * sx),
        -0.5 * (s[5] - my * (s[2] + sy)),
        s[0],
        s[6],
        s[7],
        s[8],
    )
    for r in range(PROJ):
        table[r] = jnp.where(live, grads[r], 0.0)


    def hand(r, at, value):
        grad_box[pl.ds(at, value.shape[0]), r, :] = value

    regroup(table, parts_s, group_s, hand, back.send_group, back.y)
    back.keep_own()

    mine = lax.shift_right_logical(iota((PROJ, LANES), 1), 6) == back.core

    def add(i, _):
        index = jnp.concatenate([asked_s[pl.ds(2 * i, 1), :], asked_s[pl.ds(2 * i + 1, 1), :]], axis=1)
        here = high_id == lax.shift_right_logical(index, 8)
        halves = []
        for j in range(2):
            halves.append(jnp.where(mine, near[2 * i + j], pltpu.roll(far[2 * i + j], 64, 1)))
        value = jnp.concatenate(halves, axis=1)
        hi = value.astype(bf16).astype(f32)
        lo = value - hi
        rows = []
        for r in range(PROJ):
            for part in (hi, lo):
                rows.append(jnp.where(here, part[r : r + 1], 0.0).astype(bf16))
        at = pl.multiple_of(i * PIX, PIX)
        acc[...] += lax.dot_general(
            jnp.concatenate(rows, axis=0),
            low_s[pl.ds(at, PIX), :],
            (((1,), (1,)), ((), ())),
            preferred_element_type=f32,
        )
        return 0

    def add_plane(g):
        lax.fori_loop(0, 8, lambda n, _: add(8 * g + n, 0), 0, unroll=4)

    back.receive(add_plane)
    for r in range(PROJ):
        both = acc[64 * r : 64 * r + 32, :] + acc[64 * r + 32 : 64 * r + 64, :]
        sum_ref[r, pl.ds(0, 32, stride=2), :] = both[:, :LANES]
        sum_ref[r, pl.ds(1, 32, stride=2), :] = both[:, LANES:]


def pull_kernel(view_ref, gauss_ref, sum_ref, shot_ref, out_ref, image_ref, held):
    image_ref[...] = shot_ref[...]
    tiles = sum_ref.shape[1]
    first = tuple(view_ref[n : n + 1, :] for n in range(3))
    second = tuple(view_ref[n : n + 1, :] for n in range(3, 6))
    w0, w1, w2 = (view_ref[8 + 24 * c : 8 + 24 * c + high - low, :] for c, (low, high) in enumerate(COLOUR_ROWS))
    params = spread(gauss_ref, held, tiles)
    _, pullback = jax.vjp(lambda *p: project(p, first, second), *params)
    grads = pullback(tuple(sum_ref[r] for r in range(6)))
    held[...] = jnp.zeros_like(held)
    for r in range(11):
        held[pl.ds(r, tiles, stride=16), :] = grads[r]
    for i in range(tiles):
        lanes = slice(i * LANES, (i + 1) * LANES)
        tint = [sum_ref[6 + c, i : i + 1, :] for c in range(3)]
        out_ref[0:8, lanes] = held[i * 16 : i * 16 + 8, :]
        out_ref[8:16, lanes] = held[i * 16 + 8 : i * 16 + 16, :] + w0[0:8] * tint[0]
        out_ref[16:24, lanes] = w0[8:16] * tint[0]
        out_ref[24:32, lanes] = w0[16:24] * tint[0] + w1[0:8] * tint[1]
        out_ref[32:40, lanes] = w1[8:16] * tint[1]
        out_ref[40:48, lanes] = w1[16:24] * tint[1] + w2[0:8] * tint[2]
        out_ref[48:56, lanes] = w2[8:16] * tint[2]
        out_ref[56:59, lanes] = w2[16:19] * tint[2]


VMEM = pl.BlockSpec(memory_space=pltpu.VMEM)
SMEM = pl.BlockSpec(memory_space=pltpu.SMEM)
ANY = pl.BlockSpec(memory_space=pl.ANY)


def sds(shape, dtype=f32):
    return jax.ShapeDtypeStruct(shape, dtype)


def splat(counts, order, angles, owners, locals_, cot, gaussians):
    square = pltpu.VMEM((ROWS, LANES), i32)
    pair = pltpu.VMEM((2, SLOTS, PIX), f32)
    pair_half = pltpu.VMEM((2, SLOTS, PIX), bf16)
    values = pltpu.VMEM((PROJ, ROWS, LANES), f32)
    lines = pltpu.VMEM((ROWS * 16, LANES), f32)
    return pl.pallas_call(
        splat_kernel,
        out_shape=(sds(cot.shape), sds((PROJ, ROWS, LANES)), sds((VIEW_ROWS, LANES))),
        in_specs=[SMEM, SMEM, SMEM, ANY, ANY, ANY, ANY],
        out_specs=(VMEM, VMEM, VMEM),
        scratch_shapes=[
            pltpu.VMEM((TILES, SLOTS), i32),
            pltpu.VMEM((TILES, SLOTS), i32),
            pltpu.VMEM((DEVS, 256), f32),
            pltpu.VMEM((256, LANES), f32),
            pltpu.VMEM(gaussians.shape, f32),
            lines,
            values,
            values,
            square,
            square,
            square,
            lines,
            lines,
            pair,
            pair,
            pair,
            pair_half,
            pair_half,
            pair_half,
            pair_half,
            pltpu.VMEM((64 * PROJ, PIX), f32),
            pltpu.VMEM((TILES * SLOTS, PIX), bf16),
            pltpu.VMEM((32 * PROJ, 3 * PIX), bf16),
            pltpu.VMEM(owners.shape, i32),
            pltpu.VMEM(locals_.shape, i32),
            pltpu.VMEM(cot.shape, f32),
            pltpu.SemaphoreType.DMA((4,)),
        ]
        + exchange_scratch(1, i32)
        + exchange_scratch(PROJ, f32)
        + exchange_scratch(PROJ, f32),
        compiler_params=pltpu.CompilerParams(
            collective_id=0, has_side_effects=True, vmem_limit_bytes=60 * 1024 * 1024
        ),
        name="splat",
    )(counts, order, angles, owners, locals_, cot, gaussians)


def pull(view, gaussians, sums, image, steps=2):
    tiles = ROWS // steps
    shot = pl.BlockSpec((3, image.shape[1] // steps), lambda i: (0, i))
    slab = pl.BlockSpec((gaussians.shape[0], tiles * LANES), lambda i: (0, i))
    return pl.pallas_call(
        pull_kernel,
        grid=(steps,),
        out_shape=(sds(gaussians.shape), sds(image.shape)),
        in_specs=[
            pl.BlockSpec((VIEW_ROWS, LANES), lambda i: (0, 0)),
            slab,
            pl.BlockSpec((PROJ, tiles, LANES), lambda i: (0, i, 0)),
            shot,
        ],
        out_specs=(slab, shot),
        scratch_shapes=[pltpu.VMEM((tiles * 16, LANES), f32)],
        name="pull",
    )(view, gaussians, sums, image)


def shards(gaussians, view_angles, tile_order, tile_owners, tile_locals, list_counts, image_cotangent):
    rendered, sums, view = splat(
        list_counts, tile_order, view_angles, tile_owners, tile_locals, image_cotangent, gaussians
    )
    gradients, rendered = pull(view, gaussians, sums, rendered)
    return rendered, gradients


def solution(mesh):
    return jax.shard_map(
        shards,
        mesh=mesh,
        in_specs=(
            P(None, "dev"),
            P(),
            P("dev"),
            P("dev", None),
            P("dev", None),
            P("dev"),
            P(None, "dev"),
        ),
        out_specs=(P(None, "dev"), P(None, "dev")),
        check_vma=False,
    )
```

```python
from functools import partial

import jax
import jax.numpy as jnp
from jax import lax
from jax.experimental import pallas as pl
from jax.experimental.pallas import tpu as pltpu
from jax.sharding import PartitionSpec as P

DEVS = 128
CHIPS = 64
TILES = 16
SLOTS = 512
ROWS = 64
LANES = 128
PROJ = 9
PIX = 256
TX = 32
FOCAL_X = 128.0
FOCAL_Y = 256.0
CENTRE_X = 256.0
CENTRE_Y = 512.0
LOG2E = 1.4426950408889634
MESH = pl.DeviceIdType.MESH
f32 = jnp.float32
bf16 = jnp.bfloat16
i32 = jnp.int32


def iota(shape, dim):
    return lax.broadcasted_iota(i32, shape, dim)


def split2(x):
    hi = x.astype(bf16)
    return hi, (x - hi.astype(f32)).astype(bf16)


def split3(x):
    hi = x.astype(bf16)
    rest = x - hi.astype(f32)
    mid = rest.astype(bf16)
    return hi, mid, (rest - mid.astype(f32)).astype(bf16)


def lane_pick(table, index):
    return jnp.take_along_axis(table, index, axis=1)


def view_of(angle_ref):
    def turn(i):
        angle = jnp.full((8, LANES), angle_ref[i], f32)
        return jnp.cos(angle)[0:1], jnp.sin(angle)[0:1]

    (ca, sa), (cb, sb), (cc, sc) = turn(0), turn(1), turn(2)
    first = (cc * cb, cc * sb * sa - sc * ca, cc * sb * ca + sc * sa)
    second = (sc * cb, sc * sb * sa + cc * ca, sc * sb * ca - cc * sa)
    third = (-sb, cb * sa, cb * ca)
    return first, second, third


def harmonics(x, y, z):
    xx, yy, zz = x * x, y * y, z * z
    return [
        0.28209479177387814 + 0.0 * x,
        -0.4886025119029199 * y,
        0.4886025119029199 * z,
        -0.4886025119029199 * x,
        1.0925484305920792 * x * y,
        -1.0925484305920792 * y * z,
        0.31539156525252005 * (2.0 * zz - xx - yy),
        -1.0925484305920792 * x * z,
        0.5462742152960396 * (xx - yy),
        -0.5900435899266435 * y * (3.0 * xx - yy),
        2.890611442640554 * x * y * z,
        -0.4570457994644658 * y * (4.0 * zz - xx - yy),
        0.3731763325901154 * z * (2.0 * zz - 3.0 * xx - 3.0 * yy),
        -0.4570457994644658 * x * (4.0 * zz - xx - yy),
        1.445305721320277 * z * (xx - yy),
        -0.5900435899266435 * x * (xx - 3.0 * yy),
    ]


COLOUR_ROWS = ((8, 32), (24, 48), (40, 59))
VIEW_ROWS = 80


def colour_weights(basis):
    out = []
    for c, (low, high) in enumerate(COLOUR_ROWS):
        row = iota((high - low, LANES), 0) + low - (11 + 16 * c)
        held = jnp.zeros((high - low, LANES), f32)
        for k in range(16):
            held = jnp.where(row == k, basis[k], held)
        out.append(held)
    return out


def project(params, first, second):
    px, py, pz, s0, s1, s2, qw, qx, qy, qz, logit = params
    mean_x = CENTRE_X + FOCAL_X * (first[0] * px + first[1] * py + first[2] * pz)
    mean_y = CENTRE_Y + FOCAL_Y * (second[0] * px + second[1] * py + second[2] * pz)
    scales = (jnp.exp(s0), jnp.exp(s1), jnp.exp(s2))
    two_n = 2.0 / jnp.maximum(qw * qw + qx * qx + qy * qy + qz * qz, 1.0)
    turned = (
        (1.0 - two_n * (qy * qy + qz * qz), two_n * (qx * qy - qw * qz), two_n * (qx * qz + qw * qy)),
        (two_n * (qx * qy + qw * qz), 1.0 - two_n * (qx * qx + qz * qz), two_n * (qy * qz - qw * qx)),
        (two_n * (qx * qz - qw * qy), two_n * (qy * qz + qw * qx), 1.0 - two_n * (qx * qx + qy * qy)),
    )
    va = []
    vb = []
    for j in range(3):
        va.append(FOCAL_X * (first[0] * turned[0][j] + first[1] * turned[1][j] + first[2] * turned[2][j]) * scales[j])
        vb.append(FOCAL_Y * (second[0] * turned[0][j] + second[1] * turned[1][j] + second[2] * turned[2][j]) * scales[j])
    cov_a = va[0] * va[0] + va[1] * va[1] + va[2] * va[2] + 0.3
    cov_b = va[0] * vb[0] + va[1] * vb[1] + va[2] * vb[2]
    cov_c = vb[0] * vb[0] + vb[1] * vb[1] + vb[2] * vb[2] + 0.3
    det = cov_a * cov_c - cov_b * cov_b
    inv = 1.0 / jnp.where(det == 0.0, 1.0, det)
    log_opacity = -jnp.log(1.0 + jnp.exp(-logit))
    return mean_x, mean_y, cov_c * inv, -cov_b * inv, cov_a * inv, log_opacity


def plane(y, n):
    return (y + 2 + 3 * n + 3 * (n // 2) + 2 * (n // 3)) % 4


def regroup(table_ref, parts_s, index_ref, store, done=None, y=0):
    for r in range(PROJ):
        even = table_ref[r, pl.ds(0, 32, stride=2), :]
        odd = table_ref[r, pl.ds(1, 32, stride=2), :]
        for n, part in enumerate(split3(jnp.concatenate([even, odd], axis=1))):
            parts_s[r * 32 : (r + 1) * 32, n * PIX : (n + 1) * PIX] = part
    high_id = iota((32, PIX), 0)
    low_id = iota((PIX, PIX), 0)

    def step(n, _):
        g = plane(y, n)
        at = pl.multiple_of(16 * g, 8)
        flat = index_ref[pl.ds(at, 8), :]
        high = lax.shift_right_logical(flat, 7)
        low = jnp.bitwise_and(flat, 127)
        held = [jnp.zeros((8, LANES), f32)] * PROJ
        for i in range(ROWS):
            here = high == i
            for r in range(PROJ):
                row = jnp.broadcast_to(table_ref[r, i : i + 1, :], (8, LANES))
                held[r] = jnp.where(here, lane_pick(row, low), held[r])
        for r in range(PROJ):
            store(r, at, held[r])
        for q in range(4):
            line = 16 * g + 8 + 2 * q
            index = jnp.concatenate([index_ref[pl.ds(line, 1), :], index_ref[pl.ds(line + 1, 1), :]], axis=1)
            column = jnp.where(low_id == jnp.bitwise_and(index, 255), 1.0, 0.0).astype(bf16)
            here = high_id == lax.shift_right_logical(index, 8)
            got = jnp.dot(
                parts_s[...], jnp.concatenate([column] * 3, axis=0), preferred_element_type=f32
            )
            for r in range(PROJ):
                value = jnp.sum(jnp.where(here, got[r * 32 : (r + 1) * 32], 0.0), axis=0, keepdims=True)
                store(r, line, value[:, :LANES])
                store(r, line + 1, value[:, LANES:])
        if done is not None:
            done(g)
        return 0

    lax.fori_loop(0, 4, step, 0)


def slot_of(row):
    return jnp.bitwise_and(row, 7) * (SLOTS // 8) + lax.shift_right_logical(row, 3)


def route(owner_ref, local_ref, want_ref, pos_ref, group_ref, own_s, loc_s, carry_s, sum_s):
    for d in range(SLOTS // LANES):
        row = iota((TILES, LANES), 1) + d * LANES
        slot = slot_of(row)
        high = lax.shift_right_logical(slot, 7)
        low = jnp.bitwise_and(slot, 127)
        for src, dst in ((owner_ref, own_s), (local_ref, loc_s)):
            held = jnp.zeros((TILES, LANES), i32)
            for c in range(SLOTS // LANES):
                held = jnp.where(high == c, lane_pick(src[:, c * LANES : (c + 1) * LANES], low), held)
            dst[:, d * LANES : (d + 1) * LANES] = held
    half = 256
    before = jnp.where(iota((half, half), 0) < iota((half, half), 1), 1.0, 0.0).astype(bf16)
    ones = jnp.ones((half, half), bf16)
    both = jnp.concatenate([before, ones], axis=1)
    carry_s[...] = jnp.zeros_like(carry_s)
    sum_s[...] = jnp.zeros_like(sum_s)
    owner_id = iota((DEVS, half), 0)
    pair_id = iota((ROWS, half), 0)
    lane_id = iota((LANES, half), 0)

    def step(t, _):
        for h in range(2):
            owner = own_s[pl.ds(t, 1), h * half : (h + 1) * half]
            local = loc_s[pl.ds(t, 1), h * half : (h + 1) * half]
            hit = owner_id == owner
            hit_f = jnp.where(hit, 1.0, 0.0)
            counts = jnp.dot(hit_f.astype(bf16), both, preferred_element_type=f32)
            seen = carry_s[...]
            rank = jnp.sum(hit_f * (counts[:, :half] + seen), axis=0, keepdims=True).astype(i32)
            carry_s[...] = seen + counts[:, half:]
            place = owner * ROWS + rank
            pos_ref[pl.ds(4 * t + 2 * h, 1), :] = place[:, :LANES]
            pos_ref[pl.ds(4 * t + 2 * h + 1, 1), :] = place[:, LANES:]
            pair = pair_id == lax.shift_right_logical(place, 7)
            lane = jnp.where(lane_id == jnp.bitwise_and(place, 127), 1.0, 0.0).astype(bf16)
            slot = t * SLOTS + h * half + iota((1, half), 1)
            parts = []
            for number in (local, slot):
                for part in (lax.shift_right_logical(number, 7), jnp.bitwise_and(number, 127)):
                    parts.append(jnp.where(pair, part.astype(f32), 0.0).astype(bf16))
            sum_s[...] += lax.dot_general(
                jnp.concatenate(parts, axis=0), lane, (((1,), (1,)), ((), ())), preferred_element_type=f32
            )
        return 0

    lax.fori_loop(0, TILES, step, 0, unroll=4)
    total = sum_s[...].astype(i32)
    want_ref[:, 0, :] = total[0:64] * 128 + total[64:128]
    group_ref[...] = total[128:192] * 128 + total[192:256]


class Exchange:
    def __init__(self, x_ref, near, far, send_sem, recv_sem, pair_sem):
        self.refs = (x_ref, near, far)
        self.sems = (send_sem, recv_sem, pair_sem)
        me = lax.axis_index("dev")
        self.chip = me // 2
        self.core = me % 2
        self.y = self.chip // 16
        self.other = self.chip * 2 + (1 - self.core)

    def copy(self, to):
        x_ref, near, _ = self.refs
        return pltpu.make_async_remote_copy(
            src_ref=x_ref.at[to],
            dst_ref=near.at[self.chip],
            send_sem=self.sems[0].at[0],
            recv_sem=self.sems[1].at[self.y],
            device_id=(to * 2 + self.core,),
            device_id_type=MESH,
        )

    def many(self, row, count, g):
        x_ref, near, _ = self.refs
        return pltpu.make_async_remote_copy(
            src_ref=x_ref.at[pl.ds(row, count)],
            dst_ref=near.at[pl.ds(row, count)],
            send_sem=self.sems[0].at[0],
            recv_sem=self.sems[1].at[g],
            device_id=(self.other,),
            device_id_type=MESH,
        )

    def send_group(self, g):
        def one(n, _):
            to = 16 * g + (self.chip + n) % 16

            @pl.when(to != self.chip)
            def _():
                self.copy(to).start()

            return 0

        lax.fori_loop(0, 16, one, 0, unroll=4)

    def keep_own(self):
        self.refs[1][self.chip] = self.refs[0][self.chip]

    def send(self):
        for n in range(4):
            self.send_group(plane(self.y, n))
        self.keep_own()

    def wait_group(self, n):
        g = plane(self.y, n)
        self.many(16 * g, 16 if n < 3 else 15, g).wait_recv()

    def swap(self, n):
        _, near, far = self.refs
        rows = pl.ds(16 * plane(self.y, n), 16)
        return pltpu.make_async_remote_copy(
            src_ref=near.at[rows],
            dst_ref=far.at[rows],
            send_sem=self.sems[2].at[n],
            recv_sem=self.sems[2].at[4 + n],
            device_id=(self.other,),
            device_id_type=MESH,
        )

    def receive(self, work):
        for n in range(4):
            self.wait_group(n)
            self.swap(n).start()
            if n > 0:
                self.swap(n - 1).wait()
                work(plane(self.y, n - 1))

        self.many(0, CHIPS - 1, 0).wait_send()
        self.swap(3).wait()
        work(plane(self.y, 3))

    def rows(self, g, r):
        _, near, far = self.refs
        at = pl.ds(16 * g, 16)
        mine = lax.shift_right_logical(iota((16, LANES), 1), 6) == self.core
        return jnp.where(mine, near[at, r, :], pltpu.roll(far[at, r, :], 64, 1))


def greet():
    me = lax.axis_index("dev")
    chip = me // 2
    core = me % 2
    barrier = pltpu.get_barrier_semaphore()

    def one(i, _):
        peer = ((chip + i) % CHIPS) * 2 + core
        pl.semaphore_signal(barrier, inc=1, device_id=(peer,), device_id_type=MESH)
        return 0

    lax.fori_loop(1, CHIPS, one, 0)
    pl.semaphore_signal(barrier, inc=1, device_id=(chip * 2 + (1 - core),), device_id_type=MESH)


def met():
    pl.semaphore_wait(pltpu.get_barrier_semaphore(), CHIPS)


def exchange_scratch(rows, dtype):
    box = pltpu.VMEM((CHIPS, rows, LANES), dtype)
    sem = pltpu.SemaphoreType.DMA
    return [box, box, box, sem((1,)), sem((4,)), sem((8,))]


def spread(gauss_ref, held, tiles):
    for i in range(tiles):
        held[i * 16 : i * 16 + 16, :] = gauss_ref[0:16, i * LANES : (i + 1) * LANES]
    return [held[pl.ds(r, tiles, stride=16), :] for r in range(11)]


def splat_kernel(
    count_ref, order_ref, angle_ref, owner_hbm, local_hbm, cot_hbm, gauss_hbm, image_ref, sum_ref, view_ref,
    own_s, loc_s, carry_s, sum_s, gauss_ref, held, table, where_s, pos_s, group_s, asked_s, coef, sums,
    alpha_s, w_s, v_s, gh_s, gl_s, wh_s, wl_s, acc, low_s, parts_s, owner_ref, local_ref, cot_ref, load_sem, *boxes,
):
    loads = [
        pltpu.make_async_copy(src, dst, load_sem.at[n])
        for n, (src, dst) in enumerate(
            ((owner_hbm, owner_ref), (local_hbm, local_ref), (gauss_hbm, gauss_ref), (cot_hbm, cot_ref))
        )
    ]
    for load in loads:
        load.start()
    greet()
    ask, reply, back = (Exchange(*boxes[6 * n : 6 * n + 6]) for n in range(3))
    wanted, picked, grad_box = boxes[0], boxes[6], boxes[12]
    near, far = boxes[13], boxes[14]

    loads[0].wait()
    loads[1].wait()
    route(owner_ref, local_ref, wanted, pos_s, group_s, own_s, loc_s, carry_s, sum_s)
    met()
    ask.send()

    first, second, third = view_of(angle_ref)
    weights = colour_weights(harmonics(*third))
    for n, entry in enumerate(first + second):
        view_ref[n : n + 1, :] = entry
    for c, (low, high) in enumerate(COLOUR_ROWS):
        view_ref[8 + 24 * c : 8 + 24 * c + high - low, :] = weights[c]
    loads[2].wait()
    loads[3].wait()
    params = spread(gauss_ref, held, ROWS)
    for r, value in enumerate(project(params, first, second)):
        table[r] = value
    for i in range(ROWS):
        lanes = slice(i * LANES, (i + 1) * LANES)
        for c, (low, high) in enumerate(COLOUR_ROWS):
            table[6 + c, i : i + 1, :] = 0.5 + jnp.sum(
                gauss_ref[low:high, lanes] * weights[c], axis=0, keepdims=True
            )

    def note(g):
        asked_s[pl.ds(pl.multiple_of(16 * g, 16), 16), :] = ask.rows(g, 0)

    ask.receive(note)

    def answer(r, at, value):
        picked[pl.ds(at, value.shape[0]), r, :] = value

    regroup(table, parts_s, asked_s, answer, reply.send_group, reply.y)
    reply.keep_own()

    low_id = iota((PIX, PIX), 0)
    high_id = iota((32, PIX), 0)

    def find(i, _):
        index = jnp.concatenate([asked_s[pl.ds(2 * i, 1), :], asked_s[pl.ds(2 * i + 1, 1), :]], axis=1)
        at = pl.multiple_of(i * PIX, PIX)
        low_s[pl.ds(at, PIX), :] = jnp.where(low_id == jnp.bitwise_and(index, 255), 1.0, 0.0).astype(bf16)
        return 0

    lax.fori_loop(0, ROWS // 2, find, 0)
    acc[...] = jnp.zeros_like(acc)
    shape = (ROWS, LANES)
    tile = lax.shift_right_logical(iota(shape, 0), 2)
    slot = slot_of(jnp.bitwise_and(iota(shape, 0), 3) * LANES + iota(shape, 1))
    count = jnp.zeros(shape, i32)
    shown = jnp.zeros(shape, i32)
    for t in range(TILES):
        here = tile == t
        count = jnp.where(here, count_ref[t], count)
        shown = jnp.where(here, order_ref[t], shown)
    live = slot < count
    mid_x = (jnp.bitwise_and(shown, TX - 1) * 16 + 8).astype(f32)
    mid_y = (lax.shift_right_logical(shown, 5) * 16 + 8).astype(f32)

    def collect(g):
        for r in range(PROJ):
            table[r, pl.ds(pl.multiple_of(16 * g, 16), 16), :] = reply.rows(g, r)

    reply.receive(collect)

    def keep(r, at, value):
        where_s[r, pl.ds(at, value.shape[0]), :] = value

    regroup(table, parts_s, pos_s, keep)
    mx = where_s[0] - mid_x
    my = where_s[1] - mid_y
    ca, cb, cc = where_s[2], where_s[3], where_s[4]
    where_s[0] = mx
    where_s[1] = my
    numbers = (
        LOG2E * (-0.5 * (ca * mx * mx + cc * my * my) - cb * mx * my + where_s[5]),
        LOG2E * (ca * mx + cb * my),
        LOG2E * (cc * my + cb * mx),
        (-0.5 * LOG2E) * ca,
        -LOG2E * cb,
        (-0.5 * LOG2E) * cc,
        where_s[6],
        where_s[7],
        where_s[8],
    )
    coef[...] = jnp.zeros_like(coef)
    for q, number in enumerate(numbers):
        coef[pl.ds(q, ROWS, stride=16), :] = jnp.where(live, number, -1e9 if q == 0 else 0.0)

    flat = (16, PIX)
    line = iota(flat, 0)
    ox = jnp.bitwise_and(iota(flat, 1), 15).astype(f32) - 7.5
    oy = lax.shift_right_logical(iota(flat, 1), 4).astype(f32) - 7.5
    terms = (jnp.ones(flat, f32), ox, oy, ox * ox, ox * oy, oy * oy)
    basis = jnp.zeros(flat, f32)
    for q, term in enumerate(terms):
        basis = jnp.where(line == q, term, basis)
    basis = basis.astype(bf16)
    none = jnp.zeros(flat, bf16)
    powers_rhs = jnp.concatenate([basis, basis, basis, none, none, none], axis=0)
    sub = iota((8, PIX), 0)
    contract_first = (((0,), (0,)), ((), ()))
    contract_last = (((1,), (1,)), ((), ()))

    def one_pair(p, _):
        at, hi, mid, t_hi, t_mid, lhs, cot_rhs = [], [], [], [], [], [], []
        for u in range(2):
            t = 2 * p + u
            parts = []
            for c in range(4):
                at_c = pl.multiple_of((4 * t + c) * 16, 16)
                parts.append(coef[pl.ds(at_c, 16), :])
            c_hi, c_mid, c_lo = split3(jnp.concatenate(parts, axis=1))
            at.append(pl.multiple_of(t * PIX, PIX))
            cot = jnp.zeros(flat, f32)
            for c in range(3):
                cot = jnp.where(line == 6 + c, cot_ref[c : c + 1, pl.ds(at[u], PIX)], cot)
            d_hi, d_mid, d_lo = split3(cot)
            hi.append(c_hi)
            mid.append(c_mid)
            t_hi.append(d_hi)
            t_mid.append(d_mid)
            lhs.append(jnp.concatenate([c_hi, c_mid, c_lo, c_hi, c_mid, c_hi], axis=0))
            cot_rhs.append(jnp.concatenate([d_hi, d_hi, d_hi, d_mid, d_mid, d_lo], axis=0))

        for u in range(2):
            for b in range(4):
                part = lhs[u][:, b * 128 : (b + 1) * 128]
                rows = slice(b * 128, (b + 1) * 128)
                alpha_s[u, rows] = jnp.exp2(
                    lax.dot_general(part, powers_rhs, contract_first, preferred_element_type=f32)
                )
                w_s[u, rows] = lax.dot_general(part, cot_rhs[u], contract_first, preferred_element_type=f32)

        left = [jnp.ones((8, PIX), f32)] * 2
        total = [jnp.zeros((8, PIX), f32)] * 2
        for j in range(SLOTS // 8):
            rows = slice(8 * j, 8 * j + 8)
            for u in range(2):
                v = left[u] * alpha_s[u, rows]
                v_s[u, rows] = v
                left[u] = left[u] - v
                total[u] = total[u] + v * w_s[u, rows]
        enter, behind = [], []
        for u in range(2):
            front = jnp.ones((8, PIX), f32)
            run = left[u][0:1]
            for s in range(1, 8):
                front = jnp.where(sub == s, run, front)
                run = run * left[u][s : s + 1]
            enter.append(front)
            back = jnp.zeros((8, PIX), f32)
            run = total[u][7:8]
            for s in range(6, -1, -1):
                back = jnp.where(sub == s, run, back)
                run = total[u][s : s + 1] + left[u][s : s + 1] * run
            behind.append(back)
        for i in range(SLOTS // 16 - 1, -1, -1):
            both = slice(16 * i, 16 * i + 16)
            for u in range(2):
                weights = [None] * 2
                grads = [None] * 2
                for j in (1, 0):
                    rows = slice(16 * i + 8 * j, 16 * i + 8 * j + 8)
                    gap = w_s[u, rows] - behind[u]
                    weights[j] = enter[u] * v_s[u, rows]
                    grads[j] = weights[j] * gap
                    behind[u] = behind[u] + alpha_s[u, rows] * gap
                wh_s[u, both], wl_s[u, both] = split2(jnp.concatenate(weights, axis=0))
                gh_s[u, both], gl_s[u, both] = split2(jnp.concatenate(grads, axis=0))

        def pixel_sum(a, b):
            return lax.dot_general(a, b, contract_last, preferred_element_type=f32)

        for u in range(2):
            two = pixel_sum(jnp.concatenate([t_hi[u], t_mid[u]], axis=0), wh_s[u])
            got = (
                pixel_sum(basis, gh_s[u])
                + pixel_sum(basis, gl_s[u])
                + two[:16]
                + two[16:]
                + pixel_sum(t_hi[u], wl_s[u])
            )
            for c in range(4):
                at_c = pl.multiple_of((8 * p + 4 * u + c) * 16, 16)
                sums[pl.ds(at_c, 16), :] = got[:, c * LANES : (c + 1) * LANES]
            two = jnp.dot(jnp.concatenate([hi[u], mid[u]], axis=0), wh_s[u], preferred_element_type=f32)
            image = two[:16] + two[16:] + jnp.dot(hi[u], wl_s[u], preferred_element_type=f32)
            image_ref[:, pl.ds(at[u], PIX)] = image[6:9]
        return 0

    lax.fori_loop(0, TILES // 2, one_pair, 0)

    s = [sums[pl.ds(q, ROWS, stride=16), :] for q in range(PROJ)]
    mx, my, ca, cb, cc = (where_s[r] for r in range(5))
    sx = s[1] - mx * s[0]
    sy = s[2] - my * s[0]
    grads = (
        ca * sx + cb * sy,
        cc * sy + cb * sx,
        -0.5 * (s[3] - mx * (s[1] + sx)),
        -(s[4] - mx * s[2] - my * sx),
        -0.5 * (s[5] - my * (s[2] + sy)),
        s[0],
        s[6],
        s[7],
        s[8],
    )
    for r in range(PROJ):
        table[r] = jnp.where(live, grads[r], 0.0)


    def hand(r, at, value):
        grad_box[pl.ds(at, value.shape[0]), r, :] = value

    regroup(table, parts_s, group_s, hand, back.send_group, back.y)
    back.keep_own()

    mine = lax.shift_right_logical(iota((PROJ, LANES), 1), 6) == back.core

    def add(i, _):
        index = jnp.concatenate([asked_s[pl.ds(2 * i, 1), :], asked_s[pl.ds(2 * i + 1, 1), :]], axis=1)
        here = high_id == lax.shift_right_logical(index, 8)
        halves = []
        for j in range(2):
            halves.append(jnp.where(mine, near[2 * i + j], pltpu.roll(far[2 * i + j], 64, 1)))
        value = jnp.concatenate(halves, axis=1)
        hi = value.astype(bf16).astype(f32)
        lo = value - hi
        rows = []
        for r in range(PROJ):
            for part in (hi, lo):
                rows.append(jnp.where(here, part[r : r + 1], 0.0).astype(bf16))
        at = pl.multiple_of(i * PIX, PIX)
        acc[...] += lax.dot_general(
            jnp.concatenate(rows, axis=0),
            low_s[pl.ds(at, PIX), :],
            (((1,), (1,)), ((), ())),
            preferred_element_type=f32,
        )
        return 0

    def add_plane(g):
        lax.fori_loop(0, 8, lambda n, _: add(8 * g + n, 0), 0, unroll=4)

    back.receive(add_plane)
    for r in range(PROJ):
        both = acc[64 * r : 64 * r + 32, :] + acc[64 * r + 32 : 64 * r + 64, :]
        sum_ref[r, pl.ds(0, 32, stride=2), :] = both[:, :LANES]
        sum_ref[r, pl.ds(1, 32, stride=2), :] = both[:, LANES:]


def pull_kernel(view_ref, gauss_ref, sum_ref, shot_ref, out_ref, image_ref, held):
    image_ref[...] = shot_ref[...]
    tiles = sum_ref.shape[1]
    first = tuple(view_ref[n : n + 1, :] for n in range(3))
    second = tuple(view_ref[n : n + 1, :] for n in range(3, 6))
    w0, w1, w2 = (view_ref[8 + 24 * c : 8 + 24 * c + high - low, :] for c, (low, high) in enumerate(COLOUR_ROWS))
    params = spread(gauss_ref, held, tiles)
    _, pullback = jax.vjp(lambda *p: project(p, first, second), *params)
    grads = pullback(tuple(sum_ref[r] for r in range(6)))
    held[...] = jnp.zeros_like(held)
    for r in range(11):
        held[pl.ds(r, tiles, stride=16), :] = grads[r]
    for i in range(tiles):
        lanes = slice(i * LANES, (i + 1) * LANES)
        tint = [sum_ref[6 + c, i : i + 1, :] for c in range(3)]
        out_ref[0:8, lanes] = held[i * 16 : i * 16 + 8, :]
        out_ref[8:16, lanes] = held[i * 16 + 8 : i * 16 + 16, :] + w0[0:8] * tint[0]
        out_ref[16:24, lanes] = w0[8:16] * tint[0]
        out_ref[24:32, lanes] = w0[16:24] * tint[0] + w1[0:8] * tint[1]
        out_ref[32:40, lanes] = w1[8:16] * tint[1]
        out_ref[40:48, lanes] = w1[16:24] * tint[1] + w2[0:8] * tint[2]
        out_ref[48:56, lanes] = w2[8:16] * tint[2]
        out_ref[56:59, lanes] = w2[16:19] * tint[2]


VMEM = pl.BlockSpec(memory_space=pltpu.VMEM)
SMEM = pl.BlockSpec(memory_space=pltpu.SMEM)
ANY = pl.BlockSpec(memory_space=pl.ANY)


def sds(shape, dtype=f32):
    return jax.ShapeDtypeStruct(shape, dtype)


def splat(counts, order, angles, owners, locals_, cot, gaussians):
    square = pltpu.VMEM((ROWS, LANES), i32)
    pair = pltpu.VMEM((2, SLOTS, PIX), f32)
    pair_half = pltpu.VMEM((2, SLOTS, PIX), bf16)
    values = pltpu.VMEM((PROJ, ROWS, LANES), f32)
    lines = pltpu.VMEM((ROWS * 16, LANES), f32)
    return pl.pallas_call(
        splat_kernel,
        out_shape=(sds(cot.shape), sds((PROJ, ROWS, LANES)), sds((VIEW_ROWS, LANES))),
        in_specs=[SMEM, SMEM, SMEM, ANY, ANY, ANY, ANY],
        out_specs=(VMEM, VMEM, VMEM),
        scratch_shapes=[
            pltpu.VMEM((TILES, SLOTS), i32),
            pltpu.VMEM((TILES, SLOTS), i32),
            pltpu.VMEM((DEVS, 256), f32),
            pltpu.VMEM((256, LANES), f32),
            pltpu.VMEM(gaussians.shape, f32),
            lines,
            values,
            values,
            square,
            square,
            square,
            lines,
            lines,
            pair,
            pair,
            pair,
            pair_half,
            pair_half,
            pair_half,
            pair_half,
            pltpu.VMEM((64 * PROJ, PIX), f32),
            pltpu.VMEM((TILES * SLOTS, PIX), bf16),
            pltpu.VMEM((32 * PROJ, 3 * PIX), bf16),
            pltpu.VMEM(owners.shape, i32),
            pltpu.VMEM(locals_.shape, i32),
            pltpu.VMEM(cot.shape, f32),
            pltpu.SemaphoreType.DMA((4,)),
        ]
        + exchange_scratch(1, i32)
        + exchange_scratch(PROJ, f32)
        + exchange_scratch(PROJ, f32),
        compiler_params=pltpu.CompilerParams(
            collective_id=0, has_side_effects=True, vmem_limit_bytes=60 * 1024 * 1024
        ),
        name="splat",
    )(counts, order, angles, owners, locals_, cot, gaussians)


def pull(view, gaussians, sums, image, steps=2):
    tiles = ROWS // steps
    shot = pl.BlockSpec((3, image.shape[1] // steps), lambda i: (0, i))
    slab = pl.BlockSpec((gaussians.shape[0], tiles * LANES), lambda i: (0, i))
    return pl.pallas_call(
        pull_kernel,
        grid=(steps,),
        out_shape=(sds(gaussians.shape), sds(image.shape)),
        in_specs=[
            pl.BlockSpec((VIEW_ROWS, LANES), lambda i: (0, 0)),
            slab,
            pl.BlockSpec((PROJ, tiles, LANES), lambda i: (0, i, 0)),
            shot,
        ],
        out_specs=(slab, shot),
        scratch_shapes=[pltpu.VMEM((tiles * 16, LANES), f32)],
        name="pull",
    )(view, gaussians, sums, image)


def shards(gaussians, view_angles, tile_order, tile_owners, tile_locals, list_counts, image_cotangent):
    rendered, sums, view = splat(
        list_counts, tile_order, view_angles, tile_owners, tile_locals, image_cotangent, gaussians
    )
    gradients, rendered = pull(view, gaussians, sums, rendered)
    return rendered, gradients


def solution(mesh):
    return jax.shard_map(
        shards,
        mesh=mesh,
        in_specs=(
            P(None, "dev"),
            P(),
            P("dev"),
            P("dev", None),
            P("dev", None),
            P("dev"),
            P(None, "dev"),
        ),
        out_specs=(P(None, "dev"), P(None, "dev")),
        check_vma=False,
    )
```

```python
from functools import partial

import jax
import jax.numpy as jnp
from jax import lax
from jax.experimental import pallas as pl
from jax.experimental.pallas import tpu as pltpu
from jax.sharding import PartitionSpec as P

DEVS = 128
CHIPS = 64
TILES = 16
SLOTS = 512
ROWS = 64
LANES = 128
PROJ = 9
PIX = 256
TX = 32
FOCAL_X = 128.0
FOCAL_Y = 256.0
CENTRE_X = 256.0
CENTRE_Y = 512.0
LOG2E = 1.4426950408889634
MESH = pl.DeviceIdType.MESH
f32 = jnp.float32
bf16 = jnp.bfloat16
i32 = jnp.int32


def iota(shape, dim):
    return lax.broadcasted_iota(i32, shape, dim)


def split2(x):
    hi = x.astype(bf16)
    return hi, (x - hi.astype(f32)).astype(bf16)


def split3(x):
    hi = x.astype(bf16)
    rest = x - hi.astype(f32)
    mid = rest.astype(bf16)
    return hi, mid, (rest - mid.astype(f32)).astype(bf16)


def lane_pick(table, index):
    return jnp.take_along_axis(table, index, axis=1)


def view_of(angle_ref):
    def turn(i):
        angle = jnp.full((8, LANES), angle_ref[i], f32)
        return jnp.cos(angle)[0:1], jnp.sin(angle)[0:1]

    (ca, sa), (cb, sb), (cc, sc) = turn(0), turn(1), turn(2)
    first = (cc * cb, cc * sb * sa - sc * ca, cc * sb * ca + sc * sa)
    second = (sc * cb, sc * sb * sa + cc * ca, sc * sb * ca - cc * sa)
    third = (-sb, cb * sa, cb * ca)
    return first, second, third


def harmonics(x, y, z):
    xx, yy, zz = x * x, y * y, z * z
    return [
        0.28209479177387814 + 0.0 * x,
        -0.4886025119029199 * y,
        0.4886025119029199 * z,
        -0.4886025119029199 * x,
        1.0925484305920792 * x * y,
        -1.0925484305920792 * y * z,
        0.31539156525252005 * (2.0 * zz - xx - yy),
        -1.0925484305920792 * x * z,
        0.5462742152960396 * (xx - yy),
        -0.5900435899266435 * y * (3.0 * xx - yy),
        2.890611442640554 * x * y * z,
        -0.4570457994644658 * y * (4.0 * zz - xx - yy),
        0.3731763325901154 * z * (2.0 * zz - 3.0 * xx - 3.0 * yy),
        -0.4570457994644658 * x * (4.0 * zz - xx - yy),
        1.445305721320277 * z * (xx - yy),
        -0.5900435899266435 * x * (xx - 3.0 * yy),
    ]


COLOUR_ROWS = ((8, 32), (24, 48), (40, 59))
VIEW_ROWS = 80


def colour_weights(basis):
    out = []
    for c, (low, high) in enumerate(COLOUR_ROWS):
        row = iota((high - low, LANES), 0) + low - (11 + 16 * c)
        held = jnp.zeros((high - low, LANES), f32)
        for k in range(16):
            held = jnp.where(row == k, basis[k], held)
        out.append(held)
    return out


def project(params, first, second):
    px, py, pz, s0, s1, s2, qw, qx, qy, qz, logit = params
    mean_x = CENTRE_X + FOCAL_X * (first[0] * px + first[1] * py + first[2] * pz)
    mean_y = CENTRE_Y + FOCAL_Y * (second[0] * px + second[1] * py + second[2] * pz)
    scales = (jnp.exp(s0), jnp.exp(s1), jnp.exp(s2))
    two_n = 2.0 / jnp.maximum(qw * qw + qx * qx + qy * qy + qz * qz, 1.0)
    turned = (
        (1.0 - two_n * (qy * qy + qz * qz), two_n * (qx * qy - qw * qz), two_n * (qx * qz + qw * qy)),
        (two_n * (qx * qy + qw * qz), 1.0 - two_n * (qx * qx + qz * qz), two_n * (qy * qz - qw * qx)),
        (two_n * (qx * qz - qw * qy), two_n * (qy * qz + qw * qx), 1.0 - two_n * (qx * qx + qy * qy)),
    )
    va = []
    vb = []
    for j in range(3):
        va.append(FOCAL_X * (first[0] * turned[0][j] + first[1] * turned[1][j] + first[2] * turned[2][j]) * scales[j])
        vb.append(FOCAL_Y * (second[0] * turned[0][j] + second[1] * turned[1][j] + second[2] * turned[2][j]) * scales[j])
    cov_a = va[0] * va[0] + va[1] * va[1] + va[2] * va[2] + 0.3
    cov_b = va[0] * vb[0] + va[1] * vb[1] + va[2] * vb[2]
    cov_c = vb[0] * vb[0] + vb[1] * vb[1] + vb[2] * vb[2] + 0.3
    det = cov_a * cov_c - cov_b * cov_b
    inv = 1.0 / jnp.where(det == 0.0, 1.0, det)
    log_opacity = -jnp.log(1.0 + jnp.exp(-logit))
    return mean_x, mean_y, cov_c * inv, -cov_b * inv, cov_a * inv, log_opacity


def plane(y, n):
    return (y + 2 + 3 * n + 3 * (n // 2) + 2 * (n // 3)) % 4


def regroup(table_ref, parts_s, index_ref, store, done=None, y=0):
    for r in range(PROJ):
        even = table_ref[r, pl.ds(0, 32, stride=2), :]
        odd = table_ref[r, pl.ds(1, 32, stride=2), :]
        for n, part in enumerate(split3(jnp.concatenate([even, odd], axis=1))):
            parts_s[r * 32 : (r + 1) * 32, n * PIX : (n + 1) * PIX] = part
    high_id = iota((32, PIX), 0)
    low_id = iota((PIX, PIX), 0)

    def step(n, _):
        g = plane(y, n)
        at = pl.multiple_of(16 * g, 8)
        flat = index_ref[pl.ds(at, 8), :]
        high = lax.shift_right_logical(flat, 7)
        low = jnp.bitwise_and(flat, 127)
        held = [jnp.zeros((8, LANES), f32)] * PROJ
        for i in range(ROWS):
            here = high == i
            for r in range(PROJ):
                row = jnp.broadcast_to(table_ref[r, i : i + 1, :], (8, LANES))
                held[r] = jnp.where(here, lane_pick(row, low), held[r])
        for r in range(PROJ):
            store(r, at, held[r])
        for q in range(4):
            line = 16 * g + 8 + 2 * q
            index = jnp.concatenate([index_ref[pl.ds(line, 1), :], index_ref[pl.ds(line + 1, 1), :]], axis=1)
            column = jnp.where(low_id == jnp.bitwise_and(index, 255), 1.0, 0.0).astype(bf16)
            here = high_id == lax.shift_right_logical(index, 8)
            got = jnp.dot(
                parts_s[...], jnp.concatenate([column] * 3, axis=0), preferred_element_type=f32
            )
            for r in range(PROJ):
                value = jnp.sum(jnp.where(here, got[r * 32 : (r + 1) * 32], 0.0), axis=0, keepdims=True)
                store(r, line, value[:, :LANES])
                store(r, line + 1, value[:, LANES:])
        if done is not None:
            done(g)
        return 0

    lax.fori_loop(0, 4, step, 0)


def slot_of(row):
    return jnp.bitwise_and(row, 7) * (SLOTS // 8) + lax.shift_right_logical(row, 3)


def route(owner_ref, local_ref, want_ref, pos_ref, group_ref, own_s, loc_s, carry_s, sum_s):
    for d in range(SLOTS // LANES):
        row = iota((TILES, LANES), 1) + d * LANES
        slot = slot_of(row)
        high = lax.shift_right_logical(slot, 7)
        low = jnp.bitwise_and(slot, 127)
        for src, dst in ((owner_ref, own_s), (local_ref, loc_s)):
            held = jnp.zeros((TILES, LANES), i32)
            for c in range(SLOTS // LANES):
                held = jnp.where(high == c, lane_pick(src[:, c * LANES : (c + 1) * LANES], low), held)
            dst[:, d * LANES : (d + 1) * LANES] = held
    half = 256
    before = jnp.where(iota((half, half), 0) < iota((half, half), 1), 1.0, 0.0).astype(bf16)
    ones = jnp.ones((half, half), bf16)
    both = jnp.concatenate([before, ones], axis=1)
    carry_s[...] = jnp.zeros_like(carry_s)
    sum_s[...] = jnp.zeros_like(sum_s)
    owner_id = iota((DEVS, half), 0)
    pair_id = iota((ROWS, half), 0)
    lane_id = iota((LANES, half), 0)

    def step(t, _):
        for h in range(2):
            owner = own_s[pl.ds(t, 1), h * half : (h + 1) * half]
            local = loc_s[pl.ds(t, 1), h * half : (h + 1) * half]
            hit = owner_id == owner
            hit_f = jnp.where(hit, 1.0, 0.0)
            counts = jnp.dot(hit_f.astype(bf16), both, preferred_element_type=f32)
            seen = carry_s[...]
            rank = jnp.sum(hit_f * (counts[:, :half] + seen), axis=0, keepdims=True).astype(i32)
            carry_s[...] = seen + counts[:, half:]
            place = owner * ROWS + rank
            pos_ref[pl.ds(4 * t + 2 * h, 1), :] = place[:, :LANES]
            pos_ref[pl.ds(4 * t + 2 * h + 1, 1), :] = place[:, LANES:]
            pair = pair_id == lax.shift_right_logical(place, 7)
            lane = jnp.where(lane_id == jnp.bitwise_and(place, 127), 1.0, 0.0).astype(bf16)
            slot = t * SLOTS + h * half + iota((1, half), 1)
            parts = []
            for number in (local, slot):
                for part in (lax.shift_right_logical(number, 7), jnp.bitwise_and(number, 127)):
                    parts.append(jnp.where(pair, part.astype(f32), 0.0).astype(bf16))
            sum_s[...] += lax.dot_general(
                jnp.concatenate(parts, axis=0), lane, (((1,), (1,)), ((), ())), preferred_element_type=f32
            )
        return 0

    lax.fori_loop(0, TILES, step, 0, unroll=4)
    total = sum_s[...].astype(i32)
    want_ref[:, 0, :] = total[0:64] * 128 + total[64:128]
    group_ref[...] = total[128:192] * 128 + total[192:256]


class Exchange:
    def __init__(self, x_ref, near, far, send_sem, recv_sem, pair_sem):
        self.refs = (x_ref, near, far)
        self.sems = (send_sem, recv_sem, pair_sem)
        me = lax.axis_index("dev")
        self.chip = me // 2
        self.core = me % 2
        self.y = self.chip // 16
        self.other = self.chip * 2 + (1 - self.core)

    def copy(self, to):
        x_ref, near, _ = self.refs
        return pltpu.make_async_remote_copy(
            src_ref=x_ref.at[to],
            dst_ref=near.at[self.chip],
            send_sem=self.sems[0].at[0],
            recv_sem=self.sems[1].at[self.y],
            device_id=(to * 2 + self.core,),
            device_id_type=MESH,
        )

    def many(self, row, count, g):
        x_ref, near, _ = self.refs
        return pltpu.make_async_remote_copy(
            src_ref=x_ref.at[pl.ds(row, count)],
            dst_ref=near.at[pl.ds(row, count)],
            send_sem=self.sems[0].at[0],
            recv_sem=self.sems[1].at[g],
            device_id=(self.other,),
            device_id_type=MESH,
        )

    def send_group(self, g):
        def one(n, _):
            to = 16 * g + (self.chip + n) % 16

            @pl.when(to != self.chip)
            def _():
                self.copy(to).start()

            return 0

        lax.fori_loop(0, 16, one, 0, unroll=4)

    def keep_own(self):
        self.refs[1][self.chip] = self.refs[0][self.chip]

    def send(self):
        for n in range(4):
            self.send_group(plane(self.y, n))
        self.keep_own()

    def wait_group(self, n):
        g = plane(self.y, n)
        self.many(16 * g, 16 if n < 3 else 15, g).wait_recv()

    def swap(self, n):
        _, near, far = self.refs
        rows = pl.ds(16 * plane(self.y, n), 16)
        return pltpu.make_async_remote_copy(
            src_ref=near.at[rows],
            dst_ref=far.at[rows],
            send_sem=self.sems[2].at[n],
            recv_sem=self.sems[2].at[4 + n],
            device_id=(self.other,),
            device_id_type=MESH,
        )

    def receive(self, work):
        for n in range(4):
            self.wait_group(n)
            self.swap(n).start()
            if n > 0:
                self.swap(n - 1).wait()
                work(plane(self.y, n - 1))

        self.many(0, CHIPS - 1, 0).wait_send()
        self.swap(3).wait()
        work(plane(self.y, 3))

    def rows(self, g, r):
        _, near, far = self.refs
        at = pl.ds(16 * g, 16)
        mine = lax.shift_right_logical(iota((16, LANES), 1), 6) == self.core
        return jnp.where(mine, near[at, r, :], pltpu.roll(far[at, r, :], 64, 1))


def greet():
    me = lax.axis_index("dev")
    chip = me // 2
    core = me % 2
    barrier = pltpu.get_barrier_semaphore()

    def one(i, _):
        peer = ((chip + i) % CHIPS) * 2 + core
        pl.semaphore_signal(barrier, inc=1, device_id=(peer,), device_id_type=MESH)
        return 0

    lax.fori_loop(1, CHIPS, one, 0, unroll=9)
    pl.semaphore_signal(barrier, inc=1, device_id=(chip * 2 + (1 - core),), device_id_type=MESH)


def met():
    pl.semaphore_wait(pltpu.get_barrier_semaphore(), CHIPS)


def exchange_scratch(rows, dtype):
    box = pltpu.VMEM((CHIPS, rows, LANES), dtype)
    sem = pltpu.SemaphoreType.DMA
    return [box, box, box, sem((1,)), sem((4,)), sem((8,))]


def spread(gauss_ref, held, tiles):
    for i in range(tiles):
        held[i * 16 : i * 16 + 16, :] = gauss_ref[0:16, i * LANES : (i + 1) * LANES]
    return [held[pl.ds(r, tiles, stride=16), :] for r in range(11)]


def splat_kernel(
    count_ref, order_ref, angle_ref, owner_hbm, local_hbm, cot_hbm, gauss_hbm, image_ref, sum_ref, view_ref,
    own_s, loc_s, carry_s, sum_s, gauss_ref, held, table, where_s, pos_s, group_s, asked_s, coef, sums,
    alpha_s, w_s, v_s, gh_s, gl_s, wh_s, wl_s, acc, low_s, parts_s, owner_ref, local_ref, cot_ref, load_sem, *boxes,
):
    loads = [
        pltpu.make_async_copy(src, dst, load_sem.at[n])
        for n, (src, dst) in enumerate(
            ((owner_hbm, owner_ref), (local_hbm, local_ref), (gauss_hbm, gauss_ref), (cot_hbm, cot_ref))
        )
    ]
    greet()
    for load in loads:
        load.start()
    ask, reply, back = (Exchange(*boxes[6 * n : 6 * n + 6]) for n in range(3))
    wanted, picked, grad_box = boxes[0], boxes[6], boxes[12]
    near, far = boxes[13], boxes[14]

    loads[0].wait()
    loads[1].wait()
    route(owner_ref, local_ref, wanted, pos_s, group_s, own_s, loc_s, carry_s, sum_s)
    met()
    ask.send()

    first, second, third = view_of(angle_ref)
    weights = colour_weights(harmonics(*third))
    for n, entry in enumerate(first + second):
        view_ref[n : n + 1, :] = entry
    for c, (low, high) in enumerate(COLOUR_ROWS):
        view_ref[8 + 24 * c : 8 + 24 * c + high - low, :] = weights[c]
    loads[2].wait()
    loads[3].wait()
    params = spread(gauss_ref, held, ROWS)
    for r, value in enumerate(project(params, first, second)):
        table[r] = value
    for i in range(ROWS):
        lanes = slice(i * LANES, (i + 1) * LANES)
        for c, (low, high) in enumerate(COLOUR_ROWS):
            table[6 + c, i : i + 1, :] = 0.5 + jnp.sum(
                gauss_ref[low:high, lanes] * weights[c], axis=0, keepdims=True
            )

    def note(g):
        asked_s[pl.ds(pl.multiple_of(16 * g, 16), 16), :] = ask.rows(g, 0)

    ask.receive(note)

    def answer(r, at, value):
        picked[pl.ds(at, value.shape[0]), r, :] = value

    regroup(table, parts_s, asked_s, answer, reply.send_group, reply.y)
    reply.keep_own()

    low_id = iota((PIX, PIX), 0)
    high_id = iota((32, PIX), 0)

    def find(i, _):
        index = jnp.concatenate([asked_s[pl.ds(2 * i, 1), :], asked_s[pl.ds(2 * i + 1, 1), :]], axis=1)
        at = pl.multiple_of(i * PIX, PIX)
        low_s[pl.ds(at, PIX), :] = jnp.where(low_id == jnp.bitwise_and(index, 255), 1.0, 0.0).astype(bf16)
        return 0

    lax.fori_loop(0, ROWS // 2, find, 0, unroll=4)
    acc[...] = jnp.zeros_like(acc)
    shape = (ROWS, LANES)
    tile = lax.shift_right_logical(iota(shape, 0), 2)
    slot = slot_of(jnp.bitwise_and(iota(shape, 0), 3) * LANES + iota(shape, 1))
    count = jnp.zeros(shape, i32)
    shown = jnp.zeros(shape, i32)
    for t in range(TILES):
        here = tile == t
        count = jnp.where(here, count_ref[t], count)
        shown = jnp.where(here, order_ref[t], shown)
    live = slot < count
    mid_x = (jnp.bitwise_and(shown, TX - 1) * 16 + 8).astype(f32)
    mid_y = (lax.shift_right_logical(shown, 5) * 16 + 8).astype(f32)

    def collect(g):
        for r in range(PROJ):
            table[r, pl.ds(pl.multiple_of(16 * g, 16), 16), :] = reply.rows(g, r)

    reply.receive(collect)

    def keep(r, at, value):
        where_s[r, pl.ds(at, value.shape[0]), :] = value

    regroup(table, parts_s, pos_s, keep)
    mx = where_s[0] - mid_x
    my = where_s[1] - mid_y
    ca, cb, cc = where_s[2], where_s[3], where_s[4]
    where_s[0] = mx
    where_s[1] = my
    numbers = (
        LOG2E * (-0.5 * (ca * mx * mx + cc * my * my) - cb * mx * my + where_s[5]),
        LOG2E * (ca * mx + cb * my),
        LOG2E * (cc * my + cb * mx),
        (-0.5 * LOG2E) * ca,
        -LOG2E * cb,
        (-0.5 * LOG2E) * cc,
        where_s[6],
        where_s[7],
        where_s[8],
    )
    coef[...] = jnp.zeros_like(coef)
    for q, number in enumerate(numbers):
        coef[pl.ds(q, ROWS, stride=16), :] = jnp.where(live, number, -1e9 if q == 0 else 0.0)

    flat = (16, PIX)
    line = iota(flat, 0)
    ox = jnp.bitwise_and(iota(flat, 1), 15).astype(f32) - 7.5
    oy = lax.shift_right_logical(iota(flat, 1), 4).astype(f32) - 7.5
    terms = (jnp.ones(flat, f32), ox, oy, ox * ox, ox * oy, oy * oy)
    basis = jnp.zeros(flat, f32)
    for q, term in enumerate(terms):
        basis = jnp.where(line == q, term, basis)
    basis = basis.astype(bf16)
    none = jnp.zeros(flat, bf16)
    powers_rhs = jnp.concatenate([basis, basis, basis, none, none, none], axis=0)
    sub = iota((8, PIX), 0)
    contract_first = (((0,), (0,)), ((), ()))
    contract_last = (((1,), (1,)), ((), ()))

    def one_pair(p, _):
        at, hi, mid, t_hi, t_mid, lhs, cot_rhs = [], [], [], [], [], [], []
        for u in range(2):
            t = 2 * p + u
            parts = []
            for c in range(4):
                at_c = pl.multiple_of((4 * t + c) * 16, 16)
                parts.append(coef[pl.ds(at_c, 16), :])
            c_hi, c_mid, c_lo = split3(jnp.concatenate(parts, axis=1))
            at.append(pl.multiple_of(t * PIX, PIX))
            cot = jnp.zeros(flat, f32)
            for c in range(3):
                cot = jnp.where(line == 6 + c, cot_ref[c : c + 1, pl.ds(at[u], PIX)], cot)
            d_hi, d_mid, d_lo = split3(cot)
            hi.append(c_hi)
            mid.append(c_mid)
            t_hi.append(d_hi)
            t_mid.append(d_mid)
            lhs.append(jnp.concatenate([c_hi, c_mid, c_lo, c_hi, c_mid, c_hi], axis=0))
            cot_rhs.append(jnp.concatenate([d_hi, d_hi, d_hi, d_mid, d_mid, d_lo], axis=0))

        for u in range(2):
            for b in range(4):
                part = lhs[u][:, b * 128 : (b + 1) * 128]
                rows = slice(b * 128, (b + 1) * 128)
                alpha_s[u, rows] = jnp.exp2(
                    lax.dot_general(part, powers_rhs, contract_first, preferred_element_type=f32)
                )
                w_s[u, rows] = lax.dot_general(part, cot_rhs[u], contract_first, preferred_element_type=f32)

        left = [jnp.ones((8, PIX), f32)] * 2
        total = [jnp.zeros((8, PIX), f32)] * 2
        for j in range(SLOTS // 8):
            rows = slice(8 * j, 8 * j + 8)
            for u in range(2):
                v = left[u] * alpha_s[u, rows]
                v_s[u, rows] = v
                left[u] = left[u] - v
                total[u] = total[u] + v * w_s[u, rows]
        enter, behind = [], []
        for u in range(2):
            front = jnp.ones((8, PIX), f32)
            run = left[u][0:1]
            for s in range(1, 8):
                front = jnp.where(sub == s, run, front)
                run = run * left[u][s : s + 1]
            enter.append(front)
            back = jnp.zeros((8, PIX), f32)
            run = total[u][7:8]
            for s in range(6, -1, -1):
                back = jnp.where(sub == s, run, back)
                run = total[u][s : s + 1] + left[u][s : s + 1] * run
            behind.append(back)
        for i in range(SLOTS // 16 - 1, -1, -1):
            both = slice(16 * i, 16 * i + 16)
            for u in range(2):
                weights = [None] * 2
                grads = [None] * 2
                for j in (1, 0):
                    rows = slice(16 * i + 8 * j, 16 * i + 8 * j + 8)
                    gap = w_s[u, rows] - behind[u]
                    weights[j] = enter[u] * v_s[u, rows]
                    grads[j] = weights[j] * gap
                    behind[u] = behind[u] + alpha_s[u, rows] * gap
                wh_s[u, both], wl_s[u, both] = split2(jnp.concatenate(weights, axis=0))
                gh_s[u, both], gl_s[u, both] = split2(jnp.concatenate(grads, axis=0))

        def pixel_sum(a, b):
            return lax.dot_general(a, b, contract_last, preferred_element_type=f32)

        for u in range(2):
            two = pixel_sum(jnp.concatenate([t_hi[u], t_mid[u]], axis=0), wh_s[u])
            got = (
                pixel_sum(basis, gh_s[u])
                + pixel_sum(basis, gl_s[u])
                + two[:16]
                + two[16:]
                + pixel_sum(t_hi[u], wl_s[u])
            )
            for c in range(4):
                at_c = pl.multiple_of((8 * p + 4 * u + c) * 16, 16)
                sums[pl.ds(at_c, 16), :] = got[:, c * LANES : (c + 1) * LANES]
            two = jnp.dot(jnp.concatenate([hi[u], mid[u]], axis=0), wh_s[u], preferred_element_type=f32)
            image = two[:16] + two[16:] + jnp.dot(hi[u], wl_s[u], preferred_element_type=f32)
            image_ref[:, pl.ds(at[u], PIX)] = image[6:9]
        return 0

    lax.fori_loop(0, TILES // 2, one_pair, 0)

    s = [sums[pl.ds(q, ROWS, stride=16), :] for q in range(PROJ)]
    mx, my, ca, cb, cc = (where_s[r] for r in range(5))
    sx = s[1] - mx * s[0]
    sy = s[2] - my * s[0]
    grads = (
        ca * sx + cb * sy,
        cc * sy + cb * sx,
        -0.5 * (s[3] - mx * (s[1] + sx)),
        -(s[4] - mx * s[2] - my * sx),
        -0.5 * (s[5] - my * (s[2] + sy)),
        s[0],
        s[6],
        s[7],
        s[8],
    )
    for r in range(PROJ):
        table[r] = jnp.where(live, grads[r], 0.0)


    def hand(r, at, value):
        grad_box[pl.ds(at, value.shape[0]), r, :] = value

    regroup(table, parts_s, group_s, hand, back.send_group, back.y)
    back.keep_own()

    mine = lax.shift_right_logical(iota((PROJ, LANES), 1), 6) == back.core

    def add(i, _):
        index = jnp.concatenate([asked_s[pl.ds(2 * i, 1), :], asked_s[pl.ds(2 * i + 1, 1), :]], axis=1)
        here = high_id == lax.shift_right_logical(index, 8)
        halves = []
        for j in range(2):
            halves.append(jnp.where(mine, near[2 * i + j], pltpu.roll(far[2 * i + j], 64, 1)))
        value = jnp.concatenate(halves, axis=1)
        hi = value.astype(bf16).astype(f32)
        lo = value - hi
        rows = []
        for r in range(PROJ):
            for part in (hi, lo):
                rows.append(jnp.where(here, part[r : r + 1], 0.0).astype(bf16))
        at = pl.multiple_of(i * PIX, PIX)
        acc[...] += lax.dot_general(
            jnp.concatenate(rows, axis=0),
            low_s[pl.ds(at, PIX), :],
            (((1,), (1,)), ((), ())),
            preferred_element_type=f32,
        )
        return 0

    def add_plane(g):
        lax.fori_loop(0, 8, lambda n, _: add(8 * g + n, 0), 0, unroll=4)

    back.receive(add_plane)
    for r in range(PROJ):
        both = acc[64 * r : 64 * r + 32, :] + acc[64 * r + 32 : 64 * r + 64, :]
        sum_ref[r, pl.ds(0, 32, stride=2), :] = both[:, :LANES]
        sum_ref[r, pl.ds(1, 32, stride=2), :] = both[:, LANES:]


def pull_kernel(view_ref, gauss_ref, sum_ref, shot_ref, out_ref, image_ref, held):
    image_ref[...] = shot_ref[...]
    tiles = sum_ref.shape[1]
    first = tuple(view_ref[n : n + 1, :] for n in range(3))
    second = tuple(view_ref[n : n + 1, :] for n in range(3, 6))
    w0, w1, w2 = (view_ref[8 + 24 * c : 8 + 24 * c + high - low, :] for c, (low, high) in enumerate(COLOUR_ROWS))
    params = spread(gauss_ref, held, tiles)
    _, pullback = jax.vjp(lambda *p: project(p, first, second), *params)
    grads = pullback(tuple(sum_ref[r] for r in range(6)))
    held[...] = jnp.zeros_like(held)
    for r in range(11):
        held[pl.ds(r, tiles, stride=16), :] = grads[r]
    for i in range(tiles):
        lanes = slice(i * LANES, (i + 1) * LANES)
        tint = [sum_ref[6 + c, i : i + 1, :] for c in range(3)]
        out_ref[0:8, lanes] = held[i * 16 : i * 16 + 8, :]
        out_ref[8:16, lanes] = held[i * 16 + 8 : i * 16 + 16, :] + w0[0:8] * tint[0]
        out_ref[16:24, lanes] = w0[8:16] * tint[0]
        out_ref[24:32, lanes] = w0[16:24] * tint[0] + w1[0:8] * tint[1]
        out_ref[32:40, lanes] = w1[8:16] * tint[1]
        out_ref[40:48, lanes] = w1[16:24] * tint[1] + w2[0:8] * tint[2]
        out_ref[48:56, lanes] = w2[8:16] * tint[2]
        out_ref[56:59, lanes] = w2[16:19] * tint[2]


VMEM = pl.BlockSpec(memory_space=pltpu.VMEM)
SMEM = pl.BlockSpec(memory_space=pltpu.SMEM)
ANY = pl.BlockSpec(memory_space=pl.ANY)


def sds(shape, dtype=f32):
    return jax.ShapeDtypeStruct(shape, dtype)


def splat(counts, order, angles, owners, locals_, cot, gaussians):
    square = pltpu.VMEM((ROWS, LANES), i32)
    pair = pltpu.VMEM((2, SLOTS, PIX), f32)
    pair_half = pltpu.VMEM((2, SLOTS, PIX), bf16)
    values = pltpu.VMEM((PROJ, ROWS, LANES), f32)
    lines = pltpu.VMEM((ROWS * 16, LANES), f32)
    return pl.pallas_call(
        splat_kernel,
        out_shape=(sds(cot.shape), sds((PROJ, ROWS, LANES)), sds((VIEW_ROWS, LANES))),
        in_specs=[SMEM, SMEM, SMEM, ANY, ANY, ANY, ANY],
        out_specs=(VMEM, VMEM, VMEM),
        scratch_shapes=[
            pltpu.VMEM((TILES, SLOTS), i32),
            pltpu.VMEM((TILES, SLOTS), i32),
            pltpu.VMEM((DEVS, 256), f32),
            pltpu.VMEM((256, LANES), f32),
            pltpu.VMEM(gaussians.shape, f32),
            lines,
            values,
            values,
            square,
            square,
            square,
            lines,
            lines,
            pair,
            pair,
            pair,
            pair_half,
            pair_half,
            pair_half,
            pair_half,
            pltpu.VMEM((64 * PROJ, PIX), f32),
            pltpu.VMEM((TILES * SLOTS, PIX), bf16),
            pltpu.VMEM((32 * PROJ, 3 * PIX), bf16),
            pltpu.VMEM(owners.shape, i32),
            pltpu.VMEM(locals_.shape, i32),
            pltpu.VMEM(cot.shape, f32),
            pltpu.SemaphoreType.DMA((4,)),
        ]
        + exchange_scratch(1, i32)
        + exchange_scratch(PROJ, f32)
        + exchange_scratch(PROJ, f32),
        compiler_params=pltpu.CompilerParams(
            collective_id=0, has_side_effects=True, vmem_limit_bytes=60 * 1024 * 1024
        ),
        name="splat",
    )(counts, order, angles, owners, locals_, cot, gaussians)


def pull(view, gaussians, sums, image, steps=2):
    tiles = ROWS // steps
    shot = pl.BlockSpec((3, image.shape[1] // steps), lambda i: (0, i))
    slab = pl.BlockSpec((gaussians.shape[0], tiles * LANES), lambda i: (0, i))
    return pl.pallas_call(
        pull_kernel,
        grid=(steps,),
        out_shape=(sds(gaussians.shape), sds(image.shape)),
        in_specs=[
            pl.BlockSpec((VIEW_ROWS, LANES), lambda i: (0, 0)),
            slab,
            pl.BlockSpec((PROJ, tiles, LANES), lambda i: (0, i, 0)),
            shot,
        ],
        out_specs=(slab, shot),
        scratch_shapes=[pltpu.VMEM((tiles * 16, LANES), f32)],
        name="pull",
    )(view, gaussians, sums, image)


def shards(gaussians, view_angles, tile_order, tile_owners, tile_locals, list_counts, image_cotangent):
    rendered, sums, view = splat(
        list_counts, tile_order, view_angles, tile_owners, tile_locals, image_cotangent, gaussians
    )
    gradients, rendered = pull(view, gaussians, sums, rendered)
    return rendered, gradients


def solution(mesh):
    return jax.shard_map(
        shards,
        mesh=mesh,
        in_specs=(
            P(None, "dev"),
            P(),
            P("dev"),
            P("dev", None),
            P("dev", None),
            P("dev"),
            P(None, "dev"),
        ),
        out_specs=(P(None, "dev"), P(None, "dev")),
        check_vma=False,
    )
```
